32 devices in a mesh: shard: 4 (over z), ctx: 4 (over y, x), tp: 2 (over core).
Axes of the slice: x: 2, y: 2, z: 4, core: 2. Of those that a mesh axis runs over, the one named last changes fastest.
Arguments:
- tokens: bfloat16 [32, 1024, 768], P('shard', ('ctx', 'tp')), may hold values from -6 to 6
- project_weight: bfloat16 [768, 3, 768], P(('shard', 'ctx'), None, 'tp'), may hold values from -0.21875 to 0.21875
- attend_weight: bfloat16 [768, 768], P('tp', ('shard', 'ctx')), may hold values from -1.25 to 1.25
- up_weight: bfloat16 [768, 3072], P(('shard', 'ctx'), 'tp'), may hold values from -0.21875 to 0.21875
- down_weight: bfloat16 [3072, 768], P('tp', ('shard', 'ctx')), may hold values from -0.109375 to 0.109375
- project_bias: bfloat16 [3, 768], P(None, ('shard', 'ctx')), may hold values from -3 to 3
- attend_bias: bfloat16 [768], P(('shard', 'ctx')), may hold values from -3 to 3
- up_bias: bfloat16 [3072], P(('shard', 'ctx')), may hold values from -3 to 3
- down_bias: bfloat16 [768], P(('shard', 'ctx')), may hold values from -3 to 3
- first_gain: bfloat16 [768], P(('shard', 'ctx')), may hold values from 0.25 to 1.75
- first_shift: bfloat16 [768], P(('shard', 'ctx')), may hold values from -2 to 2
- second_gain: bfloat16 [768], P(('shard', 'ctx')), may hold values from 0.25 to 1.75
- second_shift: bfloat16 [768], P(('shard', 'ctx')), may hold values from -2 to 2
- segment_ids: int32 [32, 1024], P('shard'), may hold values from 0 to 63, never falling along the last dimension, each value on 1 to 512 neighbouring positions
- padding: int32 [32, 1024], P('shard'), may hold values 0 or 1
- cotangent: bfloat16 [32, 1024, 768], P('shard', ('ctx', 'tp')), may hold values from -6 to 6
Outputs:
- output: bfloat16 [32, 1024, 768], P('shard', ('ctx', 'tp'))
- tokens_grad: bfloat16 [32, 1024, 768], P('shard', ('ctx', 'tp'))
- project_weight_grad: float32 [768, 3, 768], P(('shard', 'ctx'), None, 'tp')
- attend_weight_grad: float32 [768, 768], P('tp', ('shard', 'ctx'))
- up_weight_grad: float32 [768, 3072], P(('shard', 'ctx'), 'tp')
- down_weight_grad: float32 [3072, 768], P('tp', ('shard', 'ctx'))
- project_bias_grad: float32 [3, 768], P(None, ('shard', 'ctx'))
- attend_bias_grad: float32 [768], P(('shard', 'ctx'))
- up_bias_grad: float32 [3072], P(('shard', 'ctx'))
- down_bias_grad: float32 [768], P(('shard', 'ctx'))
- first_gain_grad: float32 [768], P(('shard', 'ctx'))
- first_shift_grad: float32 [768], P(('shard', 'ctx'))
- second_gain_grad: float32 [768], P(('shard', 'ctx'))
- second_shift_grad: float32 [768], P(('shard', 'ctx'))
The draws below stay inside these ranges and needn't reach their ends.
Inputs may be any that keep to these rules, and one draw needn't show every extreme that they name: `segment_ids`: segment numbers never fall along a sequence; a segment has 1 to 512 positions, and some segment of the draw has exactly 512.
All inputs are finite; a program needn't handle non-finite values. No bound on the sum of `padding` on one device may be relied on, other than what follows from the above.
Results may differ from the reference program's by a relative error of at most 0.02.
Values may be sent and summed in bfloat16 or wider, within the bound.
A program may use at most 320 MiB of HBM per device.

```python
import math
import jax
import jax.numpy as jnp
import numpy as np
from jax import lax

D = 768
HEADS = 12
HEAD_DIM = 64
FF = 3072
S = 1024
SEQS = 32


def set_ends(drawn, key, smallest, high):
    longest = drawn.shape.index(max(drawn.shape))
    spots = []
    for shift in (0, 1):
        where = [jax.random.randint(jax.random.fold_in(key, axis), (), 0, length) for axis, length in enumerate(drawn.shape)]
        where[longest] = (where[longest] + shift) % drawn.shape[longest]
        spots.append(tuple(where))
    return drawn.at[spots[0]].set(smallest).at[spots[1]].set(high)


def with_spikes(entries, key, source, target, shards_of, factor):
    owner, partner = [(jnp.arange(entries.shape[axis_at]) // (entries.shape[axis_at] // shards_of)).reshape([-1 if axis == axis_at else 1 for axis in range(entries.ndim)]) for axis_at in (source, target)]
    chosen = jax.random.permutation(key, shards_of)[partner]
    strong = (owner == chosen) | (owner == (partner + shards_of // 2) % shards_of)
    return jnp.where(strong, factor * entries, entries)


def block_levels(own_key, shape, cuts, low, top_value):
    factor_of, own = 1.0, jax.random.fold_in(own_key, 6)
    for dim, blocks in cuts:
        steps = jnp.exp(jax.random.uniform(jax.random.fold_in(own, dim), (blocks,), jnp.float32, low / len(cuts), top_value / len(cuts)))
        factor_of = factor_of * jnp.repeat(steps, shape[dim] // blocks).reshape([-1 if axis == dim else 1 for axis in range(len(shape))])
    return factor_of


def profile(number_of, total, reach, lean):
    portions = [(1 << 20) // math.isqrt(grade ** lean) + 1 for grade in range(2, number_of + 1)]
    spare, counts = total - reach - (number_of - 1), [1] * (number_of - 1)
    while spare > 0:
        candidates = [i for i in range(number_of - 1) if counts[i] < reach]
        whole, remaining = sum([portions[i] for i in candidates]), spare
        for i in candidates:
            extra = min(reach - counts[i], max(1, remaining * portions[i] // whole), spare)
            counts[i] = counts[i] + extra
            spare = spare - extra
    return np.array([reach] + counts)


def uneven(own_key, count, total, bound, slope):
    if count == 2:
        one = jax.random.randint(own_key, (), max(1, total - bound), min(bound, total - 1) + 1)
        return jnp.stack([one, total - one])
    lengths = jnp.asarray(profile(count, total, bound, slope), jnp.int32)
    couples = (count - 1) // 2
    giver, taker = lengths[1:1 + 2 * couples:2], lengths[2:2 + 2 * couples:2]
    slack = jnp.minimum(giver - 1, bound - taker)
    moved = jax.random.randint(jax.random.fold_in(own_key, 1), (couples,), 0, 1 << 20) % (slack + 1)
    lengths = lengths.at[1:1 + 2 * couples:2].set(giver - moved).at[2:2 + 2 * couples:2].set(taker + moved)
    return lengths[jax.random.permutation(jax.random.fold_in(own_key, 2), count)]


def normal_values(own_key, shape, scale, bound, split=(), kind=jnp.bfloat16):
    level = block_levels(own_key, shape, split, -0.22, 0.18) if split else 1.0
    entries = jax.random.normal(own_key, shape, jnp.float32) * scale * level
    return jnp.minimum(jnp.maximum(entries, -bound), bound).astype(kind)


def heavy_noise(own_key, extent, deviation, bound, shards, heavy, kind=jnp.bfloat16):
    array = deviation * jax.random.normal(own_key, extent, jnp.float32)
    if shards:
        array = array * block_levels(own_key, extent, shards, -0.22, 0.18)
    return jnp.clip(with_spikes(array, jax.random.fold_in(own_key, 3), *heavy), -bound, bound).astype(kind)


def setup_inputs(seed: int = 0) -> dict:
    key_of = jax.random.split(jax.random.key(seed), 17)
    return {
        "tokens": normal_values(key_of[0], (SEQS, S, D), 1.0, 6.0, ((0, 4), (1, 8))),
        "project_weight": normal_values(key_of[1], (D, 3, D), D ** -0.5, 0.21875, ((0, 16), (2, 2))),
        "attend_weight": normal_values(key_of[2], (D, D), (D // 32) ** -0.5, 1.25, ((0, 2), (1, 16))),
        "up_weight": normal_values(key_of[3], (D, FF), D ** -0.5, 0.21875, ((0, 16), (1, 2))),
        "down_weight": normal_values(key_of[4], (FF, D), FF ** -0.5, 0.109375, ((0, 2), (1, 16))),
        "project_bias": normal_values(key_of[5], (3, D), 0.5, 3.0, ((1, 16),)),
        "attend_bias": normal_values(key_of[6], (D,), 0.5, 3.0, ((0, 16),)),
        "up_bias": normal_values(key_of[7], (FF,), 0.5, 3.0, ((0, 16),)),
        "down_bias": normal_values(key_of[8], (D,), 0.5, 3.0, ((0, 16),)),
        "first_gain": jnp.clip(1.0 + 0.15 * jax.random.normal(key_of[9], (D,), jnp.float32), 0.25, 1.75).astype(jnp.bfloat16),
        "first_shift": normal_values(key_of[10], (D,), 0.3, 2.0, ((0, 16),)),
        "second_gain": jnp.clip(1.0 + 0.15 * jax.random.normal(key_of[11], (D,), jnp.float32), 0.25, 1.75).astype(jnp.bfloat16),
        "second_shift": normal_values(key_of[12], (D,), 0.3, 2.0, ((0, 16),)),
        "segment_ids": jax.vmap(lambda own: jnp.searchsorted(jnp.cumsum(uneven(own, S // 16, S, S // 2, 2)), jnp.arange(S), side="right"))(jax.random.split(key_of[13], SEQS)).reshape((SEQS, S)).astype(jnp.int32),
        "padding": set_ends((jax.random.randint(key_of[14], (SEQS, S), 0, 16) < 15).astype(jnp.int32), jax.random.fold_in(key_of[14], 1), 0, 1),
        "cotangent": heavy_noise(key_of[15], (SEQS, S, D), 1.0, 6.0, ((0, 4), (1, 8)), (0, 2, 4, 2.0)),
    }


norm_eps = 1e-12
mask_fill = -1000000000.0

@jax.custom_vjp
def low(v):
    return lax.optimization_barrier(v.astype(jnp.bfloat16)).astype(jnp.float32)

@jax.custom_vjp
def low_back(v):
    return v

def low_keep(v):
    return (low(v), None)

def low_pass(kept, grad):
    return (grad,)

def back_keep(v):
    return (v, None)

def back_low(kept, grad):
    return (low(grad),)
low.defvjp(low_keep, low_pass)
low_back.defvjp(back_keep, back_low)

def angles(first, count, width):
    position = (first + jnp.arange(count, dtype=jnp.int32)).astype(jnp.float32)
    column = jnp.arange(width, dtype=jnp.int32) % HEAD_DIM // 2
    rate = jnp.exp(column.astype(jnp.float32) * (-2.0 * math.log(10000.0) / HEAD_DIM))
    phase = position[:, None] * rate[None, :]
    return (jnp.cos(phase), jnp.sin(phase))

def rotate(values, cosine, sine):
    even = jnp.arange(values.shape[-1], dtype=jnp.int32) % 2 == 0
    partner = jnp.where(even, -jnp.roll(values, -1, axis=-1), jnp.roll(values, 1, axis=-1))
    return values * cosine + partner * sine

def layer_norm(rows, gain, shift):
    mean = lax.optimization_barrier(jnp.mean(rows, axis=-1, keepdims=True))
    centred = rows - mean
    factor = lax.rsqrt(lax.optimization_barrier(jnp.mean(centred * centred, axis=-1, keepdims=True)) + norm_eps)
    return centred * factor * gain + shift

def matmul(left, right):
    return jnp.dot(left, right, precision=lax.Precision.HIGHEST, preferred_element_type=jnp.float32)

def block(tokens, segments, padding, params):
    project_weight, attend_weight, up_weight, down_weight, project_bias, attend_bias, up_bias, down_bias, first_gain, first_shift, second_gain, second_shift = params
    group, length, width = tokens.shape
    rows = tokens.reshape(group * length, width)
    joint = low_back(matmul(rows, project_weight.reshape(width, 3 * width)) + project_bias.reshape(3 * width))
    joint = joint.reshape(group, length, 3 * width)
    cosine, sine = angles(0, length, width)
    query = low(rotate(joint[..., :width], cosine, sine)).reshape(group, length, HEADS, HEAD_DIM)
    keyed = low(rotate(joint[..., width:2 * width], cosine, sine)).reshape(group, length, HEADS, HEAD_DIM)
    valued = low(joint[..., 2 * width:]).reshape(group, length, HEADS, HEAD_DIM)
    scores = jnp.einsum('gqhd,gkhd->ghqk', query, keyed, precision=lax.Precision.HIGHEST) * (1.0 / math.sqrt(HEAD_DIM))
    scores = low_back(scores)
    allowed = (segments[:, :, None] == segments[:, None, :]) & (padding[:, None, :] >= padding[:, :, None])
    scores = jnp.where(allowed[:, None], scores, mask_fill)
    probs = low(jax.nn.softmax(scores, axis=-1))
    attended = jnp.einsum('ghqk,gkhd->gqhd', probs, valued, precision=lax.Precision.HIGHEST)
    attended = low(low_back(attended.reshape(group * length, width)))
    branch = low_back(matmul(attended, attend_weight) + attend_bias)
    first = layer_norm(rows + branch, first_gain, first_shift)
    first_low = low(first)
    pre = low_back(matmul(first_low, up_weight) + up_bias)
    hidden = low(jax.nn.gelu(pre, approximate=False))
    ffn = low_back(matmul(hidden, down_weight) + down_bias)
    second = layer_norm(first + ffn, second_gain, second_shift)
    return second.reshape(group, length, width)

def forward(tokens, params, segment_ids, padding):
    count, length, width = tokens.shape
    group = math.gcd(count, 4)
    batches = count // group
    checked = jax.checkpoint(block)

    def step(carry, items):
        return (carry, checked(items[0], items[1], items[2], params))
    _, outs = lax.scan(step, None, (tokens.reshape(batches, group, length, width), segment_ids.reshape(batches, group, length), padding.reshape(batches, group, length)))
    return outs.reshape(count, length, width)

def reference(tokens, project_weight, attend_weight, up_weight, down_weight, project_bias, attend_bias, up_bias, down_bias, first_gain, first_shift, second_gain, second_shift, segment_ids, padding, cotangent):
    params = tuple((item.astype(jnp.float32) for item in (project_weight, attend_weight, up_weight, down_weight, project_bias, attend_bias, up_bias, down_bias, first_gain, first_shift, second_gain, second_shift)))

    def whole(inputs, weights):
        return forward(inputs, weights, segment_ids, padding)
    output, pullback = jax.vjp(whole, tokens.astype(jnp.float32), params)
    tokens_grad, grads = pullback(cotangent.astype(jnp.float32))
    return (output.astype(jnp.bfloat16), tokens_grad.astype(jnp.bfloat16), grads[0], grads[1], grads[2], grads[3], grads[4], grads[5], grads[6], grads[7], grads[8], grads[9], grads[10], grads[11])
```

```python
import math

import jax
import jax.numpy as jnp
from jax import lax
from jax.experimental import pallas as pl
from jax.experimental.pallas import tpu as pltpu
from jax.sharding import PartitionSpec as P

D = 768
HEADS = 12
HEAD_DIM = 64
FF = 3072
S = 1024
LANES = 128
PAIRS = HEADS // 2
Q_ROWS = 128
K_ROWS = 256

norm_eps = 1e-12
mask_fill = -1000000000.0

NT = (((1,), (1,)), ((), ()))
TN = (((0,), (0,)), ((), ()))
NN = (((1,), (0,)), ((), ()))


def dot(left, right, dims):
    return lax.dot_general(left, right, dims, preferred_element_type=jnp.float32)


def swap_pairs(values):
    lane = lax.broadcasted_iota(jnp.int32, values.shape, 1)
    width = values.shape[1]
    return jnp.where(
        lane % 2 == 0, -pltpu.roll(values, width - 1, 1), pltpu.roll(values, 1, 1)
    )


def stack_heads(rows):
    lane = lax.broadcasted_iota(jnp.int32, rows.shape, 1)
    zero = jnp.zeros_like(rows)
    return jnp.concatenate(
        [jnp.where(lane < HEAD_DIM, rows, zero), jnp.where(lane < HEAD_DIM, zero, rows)], axis=0
    )


def pick_heads(both):
    return jnp.concatenate([both[:HEAD_DIM, :Q_ROWS], both[HEAD_DIM:, Q_ROWS:]], axis=0)


def spread_heads(row):
    return jnp.concatenate(
        [
            jnp.broadcast_to(row[:, :Q_ROWS], (HEAD_DIM, Q_ROWS)),
            jnp.broadcast_to(row[:, Q_ROWS:], (HEAD_DIM, Q_ROWS)),
        ],
        axis=0,
    )


def mask_bias(key_code, query_low, query_high):
    keys = jnp.broadcast_to(key_code, (K_ROWS, Q_ROWS))
    allowed = (keys >= query_low) & (keys <= query_high)
    bias = jnp.where(allowed, 0.0, mask_fill)
    return jnp.concatenate([bias, bias], axis=1)


def attend_kernel(
    first_ref, count_ref, x_ref, w_ref, b_ref, cos_ref, sin_ref, code_ref, low_ref, high_ref,
    q_ref, k_ref, v_ref, o_ref, lse_ref, top, total, acc, stacked,
):
    own = pl.program_id(0)
    row_tile = 256

    @pl.loop(0, S // row_tile)
    def _(tile):
        rows = pl.ds(pl.multiple_of(tile * row_tile, row_tile), row_tile)
        x = x_ref[rows, :]
        cosine = cos_ref[rows, :]
        sine = sin_ref[rows, :]
        for part, out in enumerate((q_ref, k_ref, v_ref)):
            joint = dot(x, w_ref[part], NN) + b_ref[pl.ds(part, 1), :]
            for pair in range(PAIRS):
                lanes = slice(pair * LANES, (pair + 1) * LANES)
                piece = joint[:, lanes]
                if part < 2:
                    piece = piece * cosine + swap_pairs(piece) * sine
                if part == 0:
                    piece = piece.astype(jnp.bfloat16) * jnp.asarray(HEAD_DIM**-0.5, jnp.bfloat16)
                out[rows, lanes] = piece.astype(jnp.bfloat16)

    @pl.loop(0, S // Q_ROWS)
    def _(block):
        start = pl.multiple_of(block * Q_ROWS, Q_ROWS)
        rows = pl.ds(start, Q_ROWS)
        for pair in range(PAIRS):
            stacked[pair] = stack_heads(q_ref[rows, pair * LANES : (pair + 1) * LANES])
        top[...] = jnp.full_like(top, 2.0 * mask_fill)
        total[...] = jnp.zeros_like(total)
        acc[...] = jnp.zeros_like(acc)
        low = low_ref[:, rows]
        high = high_ref[:, rows]

        @pl.loop(0, count_ref[own, block])
        def _(step):
            window = pl.ds(pl.multiple_of(first_ref[own, block] + step * K_ROWS, 16), K_ROWS)
            bias = mask_bias(code_ref[window, :], low, high)
            for pair in range(PAIRS):
                lanes = slice(pair * LANES, (pair + 1) * LANES)
                scores = dot(k_ref[window, lanes], stacked[pair], NT) + bias
                old = top[pair]
                new = jnp.maximum(old, jnp.max(scores, axis=0, keepdims=True))
                expo = jnp.exp(scores - new)
                fade = jnp.exp(old - new)
                top[pair] = new
                total[pair] = total[pair] * fade + jnp.sum(expo, axis=0, keepdims=True)
                mixed = dot(v_ref[window, lanes], expo.astype(jnp.bfloat16), TN)
                acc[pair] = acc[pair] * spread_heads(fade) + pick_heads(mixed)

        for pair in range(PAIRS):
            lanes = slice(pair * LANES, (pair + 1) * LANES)
            summed = total[pair]
            out = acc[pair] / spread_heads(summed)
            o_ref[rows, lanes] = jnp.transpose(out).astype(jnp.bfloat16)
            lse = top[pair] + jnp.log(summed)
            lse_ref[pl.ds(2 * pair, 1), rows] = lse[:, :Q_ROWS]
            lse_ref[pl.ds(2 * pair + 1, 1), rows] = lse[:, Q_ROWS:]


def attend_back_kernel(
    first_ref, count_ref, q_ref, k_ref, v_ref, o_ref, g_ref, lse_ref, cos_ref, sin_ref, code_ref,
    low_ref, high_ref, joint_ref, acc, keys, values, stacked, grads, delta, level,
):
    own = pl.program_id(0)
    keys[...] = jnp.zeros_like(keys)
    values[...] = jnp.zeros_like(values)

    @pl.loop(0, S // Q_ROWS)
    def _(block):
        start = pl.multiple_of(block * Q_ROWS, Q_ROWS)
        rows = pl.ds(start, Q_ROWS)
        for pair in range(PAIRS):
            lanes = slice(pair * LANES, (pair + 1) * LANES)
            stacked[pair] = stack_heads(q_ref[rows, lanes])
            grad = g_ref[rows, lanes]
            grads[pair] = stack_heads(grad)
            both = jnp.transpose(grad.astype(jnp.float32) * o_ref[rows, lanes].astype(jnp.float32))
            delta[pair] = jnp.concatenate(
                [
                    jnp.sum(both[:HEAD_DIM], axis=0, keepdims=True),
                    jnp.sum(both[HEAD_DIM:], axis=0, keepdims=True),
                ],
                axis=1,
            )
            level[pair] = jnp.concatenate(
                [lse_ref[pl.ds(2 * pair, 1), rows], lse_ref[pl.ds(2 * pair + 1, 1), rows]], axis=1
            )
        acc[...] = jnp.zeros_like(acc)
        low = low_ref[:, rows]
        high = high_ref[:, rows]

        @pl.loop(0, count_ref[own, block])
        def _(step):
            window = pl.ds(pl.multiple_of(first_ref[own, block] + step * K_ROWS, 16), K_ROWS)
            bias = mask_bias(code_ref[window, :], low, high)
            for pair in range(PAIRS):
                lanes = slice(pair * LANES, (pair + 1) * LANES)
                query = stacked[pair]
                grad = grads[pair]
                key = k_ref[window, lanes]
                scores = dot(key, query, NT) + bias
                probs = jnp.exp(scores - level[pair])
                prob_grad = dot(v_ref[window, lanes], grad, NT)
                score_grad = (probs * (prob_grad - delta[pair])).astype(jnp.bfloat16)
                values[window, lanes] += dot(probs.astype(jnp.bfloat16), grad, NN)
                keys[window, lanes] += dot(score_grad, query, NN)
                acc[pair] += pick_heads(dot(key, score_grad, TN))

        cosine = cos_ref[rows, :]
        sine = sin_ref[rows, :]
        for pair in range(PAIRS):
            lanes = slice(pair * LANES, (pair + 1) * LANES)
            query = jnp.transpose(acc[pair]) * (HEAD_DIM**-0.5)
            joint_ref[rows, lanes] = (query * cosine - swap_pairs(query) * sine).astype(jnp.bfloat16)

    @pl.loop(0, S // Q_ROWS)
    def _(block):
        rows = pl.ds(pl.multiple_of(block * Q_ROWS, Q_ROWS), Q_ROWS)
        cosine = cos_ref[rows, :]
        sine = sin_ref[rows, :]
        for pair in range(PAIRS):
            lanes = slice(pair * LANES, (pair + 1) * LANES)
            key = keys[rows, lanes]
            joint_ref[rows, D + pair * LANES : D + (pair + 1) * LANES] = (
                key * cosine - swap_pairs(key) * sine
            ).astype(jnp.bfloat16)
            joint_ref[rows, 2 * D + pair * LANES : 2 * D + (pair + 1) * LANES] = values[
                rows, lanes
            ].astype(jnp.bfloat16)


def whole(*shape):
    return pl.BlockSpec(shape, lambda i, *_: (0,) * len(shape))


def per(*shape):
    return pl.BlockSpec((None,) + shape, lambda i, *_: (i,) + (0,) * len(shape))


def attend(first, count, x, weight, bias, cosine, sine, code, low, high):
    own = x.shape[0]
    act = jax.ShapeDtypeStruct((own, S, D), jnp.bfloat16)
    return pl.pallas_call(
        attend_kernel,
        grid_spec=pltpu.PrefetchScalarGridSpec(
            num_scalar_prefetch=2,
            grid=(own,),
            in_specs=[
                per(S, D), whole(3, D, D), whole(3, D), whole(S, LANES), whole(S, LANES),
                per(S, 1), per(1, S), per(1, S),
            ],
            out_specs=[per(S, D), per(S, D), per(S, D), per(S, D), per(HEADS, S)],
            scratch_shapes=[
                pltpu.VMEM((PAIRS, 1, 2 * Q_ROWS), jnp.float32),
                pltpu.VMEM((PAIRS, 1, 2 * Q_ROWS), jnp.float32),
                pltpu.VMEM((PAIRS, LANES, Q_ROWS), jnp.float32),
                pltpu.VMEM((PAIRS, 2 * Q_ROWS, LANES), jnp.bfloat16),
            ],
        ),
        out_shape=[act, act, act, act, jax.ShapeDtypeStruct((own, HEADS, S), jnp.float32)],
        compiler_params=pltpu.CompilerParams(vmem_limit_bytes=60 << 20),
        name="attend",
        cost_estimate=pl.CostEstimate(flops=6 * 10**9, bytes_accessed=12 << 20, transcendentals=6 << 20),
    )(first, count, x, weight, bias, cosine, sine, code, low, high)


def attend_back(first, count, q, k, v, o, g, lse, cosine, sine, code, low, high):
    own = q.shape[0]
    return pl.pallas_call(
        attend_back_kernel,
        grid_spec=pltpu.PrefetchScalarGridSpec(
            num_scalar_prefetch=2,
            grid=(own,),
            in_specs=[
                per(S, D), per(S, D), per(S, D), per(S, D), per(S, D), per(HEADS, S),
                whole(S, LANES), whole(S, LANES), per(S, 1), per(1, S), per(1, S),
            ],
            out_specs=per(S, 3 * D),
            scratch_shapes=[
                pltpu.VMEM((PAIRS, LANES, Q_ROWS), jnp.float32),
                pltpu.VMEM((S, D), jnp.float32),
                pltpu.VMEM((S, D), jnp.float32),
                pltpu.VMEM((PAIRS, 2 * Q_ROWS, LANES), jnp.bfloat16),
                pltpu.VMEM((PAIRS, 2 * Q_ROWS, LANES), jnp.bfloat16),
                pltpu.VMEM((PAIRS, 1, 2 * Q_ROWS), jnp.float32),
                pltpu.VMEM((PAIRS, 1, 2 * Q_ROWS), jnp.float32),
            ],
        ),
        out_shape=jax.ShapeDtypeStruct((own, S, 3 * D), jnp.bfloat16),
        compiler_params=pltpu.CompilerParams(vmem_limit_bytes=60 << 20),
        name="attend_back",
        cost_estimate=pl.CostEstimate(flops=12 * 10**9, bytes_accessed=14 << 20, transcendentals=6 << 20),
    )(first, count, q, k, v, o, g, lse, cosine, sine, code, low, high)


def mask_tables(segments, padding):
    code = 2 * segments + padding
    low = code
    high = 2 * segments + 1
    blocks = segments.reshape(segments.shape[0], S // Q_ROWS, Q_ROWS)
    begin = jnp.sum(segments[:, None, :] < blocks[:, :, :1], axis=-1, dtype=jnp.int32)
    end = jnp.sum(segments[:, None, :] <= blocks[:, :, -1:], axis=-1, dtype=jnp.int32)
    begin = begin // 16 * 16
    count = (end - begin + K_ROWS - 1) // K_ROWS
    first = jnp.minimum(begin, S - count * K_ROWS)
    return first, count, code[:, :, None], low[:, None, :], high[:, None, :]


def angles():
    position = jnp.arange(S, dtype=jnp.int32).astype(jnp.float32)
    column = jnp.arange(LANES, dtype=jnp.int32) % HEAD_DIM // 2
    rate = jnp.exp(column.astype(jnp.float32) * (-2.0 * math.log(10000.0) / HEAD_DIM))
    phase = position[:, None] * rate[None, :]
    return jnp.cos(phase), jnp.sin(phase)


def normalize(rows, gain, shift):
    mean = jnp.mean(rows, axis=-1, keepdims=True)
    centred = rows - mean
    factor = lax.rsqrt(jnp.mean(centred * centred, axis=-1, keepdims=True) + norm_eps)
    unit = centred * factor
    return (unit * gain + shift, unit, factor)


def normalize_back(incoming, unit, factor, gain):
    gain_grad = jnp.sum(incoming * unit, axis=0)
    shift_grad = jnp.sum(incoming, axis=0)
    inner = incoming * gain
    rows_grad = factor * (
        inner
        - jnp.mean(inner, axis=-1, keepdims=True)
        - unit * jnp.mean(inner * unit, axis=-1, keepdims=True)
    )
    return (rows_grad, gain_grad, shift_grad)


def gelu_slope(values):
    cumulative = 0.5 * (1.0 + lax.erf(values * (1.0 / math.sqrt(2.0))))
    density = jnp.exp(-0.5 * values * values) * (1.0 / math.sqrt(2.0 * math.pi))
    return cumulative + values * density


ROWS = ("shard", "ctx")
EVERY = ("shard", "ctx", "tp")
SEQ = ("ctx", "tp")


def local(
    tokens, project_weight, attend_weight, up_weight, down_weight, project_bias, attend_bias,
    up_bias, down_bias, first_gain, first_shift, second_gain, second_shift, segment_ids, padding,
    cotangent,
):
    seq_count = tokens.shape[0]
    members = lax.axis_size("ctx") * lax.axis_size("tp")
    own = seq_count // members
    rank = lax.axis_index("ctx") * lax.axis_size("tp") + lax.axis_index("tp")
    rows = own * S
    pieces = lax.axis_size("shard") * lax.axis_size("ctx")
    depth = D // pieces

    def to_sequences(array):
        return lax.all_to_all(array, SEQ, 0, 1, tiled=True)

    def to_blocks(array):
        return lax.all_to_all(array, SEQ, 1, 0, tiled=True)

    x = to_sequences(tokens)
    segments = lax.dynamic_slice_in_dim(segment_ids, rank * own, own, 0)
    pads = lax.dynamic_slice_in_dim(padding, rank * own, own, 0)

    def gather(shard, axis):
        part = lax.all_gather(shard, ROWS, axis=axis, tiled=True)
        return lax.all_gather(part, "tp", axis=axis + 1, tiled=True)

    project = gather(jnp.transpose(project_weight, (1, 0, 2)), 1)
    attend_t = gather(jnp.transpose(attend_weight), 0)
    up = gather(up_weight, 0)
    down_t = gather(jnp.transpose(down_weight), 0)

    vectors = jnp.concatenate(
        [
            project_bias,
            attend_bias[None],
            down_bias[None],
            first_gain[None],
            first_shift[None],
            second_gain[None],
            second_shift[None],
            up_bias.reshape(FF // D, depth),
        ],
        axis=0,
    )
    vectors = lax.all_gather(vectors, ROWS, axis=0).astype(jnp.float32)
    wide = jnp.transpose(vectors[:, :9], (1, 0, 2)).reshape(9, D)
    up_shift = vectors[:, 9:].reshape(FF)

    tables = mask_tables(segments, pads)
    cosine, sine = angles()
    query, key, value, attended, level = attend(
        tables[0], tables[1], x, project, wide[:3], cosine, sine, *tables[2:]
    )
    flat = x.reshape(rows, D)
    attended_flat = attended.reshape(rows, D)
    branch = dot(attended_flat, attend_t, NT) + wide[3]
    first, first_unit, first_factor = normalize(flat.astype(jnp.float32) + branch, wide[5], wide[6])
    first_low = first.astype(jnp.bfloat16)
    pre = dot(first_low, up, NN) + up_shift
    hidden = jax.nn.gelu(pre, approximate=False).astype(jnp.bfloat16)
    ffn = dot(hidden, down_t, NT) + wide[4]
    second, second_unit, second_factor = normalize(first + ffn, wide[7], wide[8])
    output = to_blocks(second.astype(jnp.bfloat16).reshape(own, S, D))

    incoming = to_sequences(cotangent).reshape(rows, D).astype(jnp.float32)
    second_grad, second_gain_grad, second_shift_grad = normalize_back(
        incoming, second_unit, second_factor, wide[7]
    )
    ffn_grad = second_grad.astype(jnp.bfloat16)
    down_bias_grad = jnp.sum(ffn_grad.astype(jnp.float32), axis=0)
    down_t_grad = dot(ffn_grad, hidden, TN)
    pre_grad = (dot(ffn_grad, down_t, NN) * gelu_slope(pre)).astype(jnp.bfloat16)
    up_bias_grad = jnp.sum(pre_grad.astype(jnp.float32), axis=0)
    up_grad = dot(first_low, pre_grad, TN)
    first_total = second_grad + dot(pre_grad, up, NT)
    first_grad, first_gain_grad, first_shift_grad = normalize_back(
        first_total, first_unit, first_factor, wide[5]
    )
    branch_grad = first_grad.astype(jnp.bfloat16)
    attend_bias_grad = jnp.sum(branch_grad.astype(jnp.float32), axis=0)
    attend_t_grad = dot(branch_grad, attended_flat, TN)
    attended_grad = dot(branch_grad, attend_t, NN).astype(jnp.bfloat16)

    joint_grad = attend_back(
        tables[0], tables[1], query, key, value, attended, attended_grad.reshape(own, S, D), level,
        cosine, sine, *tables[2:],
    ).reshape(rows, 3 * D)
    project_bias_grad = jnp.sum(joint_grad.astype(jnp.float32), axis=0).reshape(3, D)
    project_grad = jnp.stack(
        [dot(flat, joint_grad[:, i * D : (i + 1) * D], TN) for i in range(3)]
    )
    token_part = sum(
        dot(joint_grad[:, i * D : (i + 1) * D], project[i], NT) for i in range(3)
    )
    tokens_grad = to_blocks((first_grad + token_part).astype(jnp.bfloat16).reshape(own, S, D))

    def scatter(grad, axis):
        part = lax.psum_scatter(
            grad.astype(jnp.bfloat16), "tp", scatter_dimension=axis + 1, tiled=True
        )
        return lax.psum_scatter(part, ROWS, scatter_dimension=axis, tiled=True).astype(jnp.float32)

    sums = jnp.concatenate(
        [
            project_bias_grad,
            attend_bias_grad[None],
            down_bias_grad[None],
            first_gain_grad[None],
            first_shift_grad[None],
            second_gain_grad[None],
            second_shift_grad[None],
        ],
        axis=0,
    )
    sums = jnp.concatenate(
        [
            jnp.transpose(sums.reshape(9, pieces, depth), (1, 0, 2)),
            up_bias_grad.reshape(pieces, FF // D, depth),
        ],
        axis=1,
    )
    sums = lax.psum(sums, EVERY)
    mine = lax.axis_index("shard") * lax.axis_size("ctx") + lax.axis_index("ctx")
    sums = lax.dynamic_index_in_dim(sums, mine, 0, keepdims=False)
    return (
        output,
        tokens_grad,
        jnp.transpose(scatter(project_grad, 1), (1, 0, 2)),
        jnp.transpose(scatter(attend_t_grad, 0)),
        scatter(up_grad, 0),
        jnp.transpose(scatter(down_t_grad, 0)),
        sums[:3],
        sums[3],
        sums[9:].reshape(-1),
        sums[4],
        sums[5],
        sums[6],
        sums[7],
        sums[8],
    )


def solution(mesh):
    in_specs = (
        P("shard", ("ctx", "tp"), None),
        P(("shard", "ctx"), None, "tp"),
        P("tp", ("shard", "ctx")),
        P(("shard", "ctx"), "tp"),
        P("tp", ("shard", "ctx")),
        P(None, ("shard", "ctx")),
        P(("shard", "ctx")),
        P(("shard", "ctx")),
        P(("shard", "ctx")),
        P(("shard", "ctx")),
        P(("shard", "ctx")),
        P(("shard", "ctx")),
        P(("shard", "ctx")),
        P("shard", None),
        P("shard", None),
        P("shard", ("ctx", "tp"), None),
    )
    out_specs = (
        P("shard", ("ctx", "tp"), None),
        P("shard", ("ctx", "tp"), None),
        P(("shard", "ctx"), None, "tp"),
        P("tp", ("shard", "ctx")),
        P(("shard", "ctx"), "tp"),
        P("tp", ("shard", "ctx")),
        P(None, ("shard", "ctx")),
        P(("shard", "ctx")),
        P(("shard", "ctx")),
        P(("shard", "ctx")),
        P(("shard", "ctx")),
        P(("shard", "ctx")),
        P(("shard", "ctx")),
        P(("shard", "ctx")),
    )
    return jax.shard_map(local, mesh=mesh, in_specs=in_specs, out_specs=out_specs, check_vma=False)
```

```python
import math

import jax
import jax.numpy as jnp
from jax import lax
from jax.experimental import pallas as pl
from jax.experimental.pallas import tpu as pltpu
from jax.sharding import PartitionSpec as P

D = 768
HEADS = 12
HEAD_DIM = 64
FF = 3072
S = 1024
LANES = 128
PAIRS = HEADS // 2
Q_ROWS = 128
K_ROWS = 256

norm_eps = 1e-12
mask_fill = -1000000000.0

NT = (((1,), (1,)), ((), ()))
TN = (((0,), (0,)), ((), ()))
NN = (((1,), (0,)), ((), ()))


def dot(left, right, dims):
    return lax.dot_general(left, right, dims, preferred_element_type=jnp.float32)


def swap_pairs(values):
    lane = lax.broadcasted_iota(jnp.int32, values.shape, 1)
    width = values.shape[1]
    return jnp.where(
        lane % 2 == 0, -pltpu.roll(values, width - 1, 1), pltpu.roll(values, 1, 1)
    )


def stack_heads(rows):
    lane = lax.broadcasted_iota(jnp.int32, rows.shape, 1)
    zero = jnp.zeros_like(rows)
    return jnp.concatenate(
        [jnp.where(lane < HEAD_DIM, rows, zero), jnp.where(lane < HEAD_DIM, zero, rows)], axis=0
    )


def pick_heads(both):
    return jnp.concatenate([both[:HEAD_DIM, :Q_ROWS], both[HEAD_DIM:, Q_ROWS:]], axis=0)


def spread_heads(row):
    return jnp.concatenate(
        [
            jnp.broadcast_to(row[:, :Q_ROWS], (HEAD_DIM, Q_ROWS)),
            jnp.broadcast_to(row[:, Q_ROWS:], (HEAD_DIM, Q_ROWS)),
        ],
        axis=0,
    )


def mask_bias(key_code, query_low, query_high):
    keys = jnp.broadcast_to(key_code, (K_ROWS, Q_ROWS))
    allowed = (keys >= query_low) & (keys <= query_high)
    bias = jnp.where(allowed, 0.0, mask_fill)
    return jnp.concatenate([bias, bias], axis=1)


def attend_kernel(
    first_ref, count_ref, x_ref, w_ref, b_ref, cos_ref, sin_ref, code_ref, low_ref, high_ref,
    q_ref, k_ref, v_ref, o_ref, lse_ref, top, total, acc, stacked,
):
    own = pl.program_id(0)
    row_tile = 256

    @pl.loop(0, S // row_tile)
    def _(tile):
        rows = pl.ds(pl.multiple_of(tile * row_tile, row_tile), row_tile)
        x = x_ref[rows, :]
        cosine = cos_ref[rows, :]
        sine = sin_ref[rows, :]
        for part, out in enumerate((q_ref, k_ref, v_ref)):
            joint = dot(x, w_ref[part], NN) + b_ref[pl.ds(part, 1), :]
            for pair in range(PAIRS):
                lanes = slice(pair * LANES, (pair + 1) * LANES)
                piece = joint[:, lanes]
                if part < 2:
                    piece = piece * cosine + swap_pairs(piece) * sine
                if part == 0:
                    piece = piece.astype(jnp.bfloat16) * jnp.asarray(HEAD_DIM**-0.5, jnp.bfloat16)
                out[rows, lanes] = piece.astype(jnp.bfloat16)

    @pl.loop(0, S // Q_ROWS)
    def _(block):
        start = pl.multiple_of(block * Q_ROWS, Q_ROWS)
        rows = pl.ds(start, Q_ROWS)
        for pair in range(PAIRS):
            stacked[pair] = stack_heads(q_ref[rows, pair * LANES : (pair + 1) * LANES])
        top[...] = jnp.full_like(top, 2.0 * mask_fill)
        total[...] = jnp.zeros_like(total)
        acc[...] = jnp.zeros_like(acc)
        low = low_ref[:, rows]
        high = high_ref[:, rows]

        @pl.loop(0, count_ref[own, block])
        def _(step):
            window = pl.ds(pl.multiple_of(first_ref[own, block] + step * K_ROWS, 16), K_ROWS)
            bias = mask_bias(code_ref[window, :], low, high)
            for pair in range(PAIRS):
                lanes = slice(pair * LANES, (pair + 1) * LANES)
                scores = dot(k_ref[window, lanes], stacked[pair], NT) + bias
                old = top[pair]
                new = jnp.maximum(old, jnp.max(scores, axis=0, keepdims=True))
                expo = jnp.exp(scores - new)
                fade = jnp.exp(old - new)
                top[pair] = new
                total[pair] = total[pair] * fade + jnp.sum(expo, axis=0, keepdims=True)
                mixed = dot(v_ref[window, lanes], expo.astype(jnp.bfloat16), TN)
                acc[pair] = acc[pair] * spread_heads(fade) + pick_heads(mixed)

        for pair in range(PAIRS):
            lanes = slice(pair * LANES, (pair + 1) * LANES)
            summed = total[pair]
            out = acc[pair] / spread_heads(summed)
            o_ref[rows, lanes] = jnp.transpose(out).astype(jnp.bfloat16)
            lse = top[pair] + jnp.log(summed)
            lse_ref[pl.ds(2 * pair, 1), rows] = lse[:, :Q_ROWS]
            lse_ref[pl.ds(2 * pair + 1, 1), rows] = lse[:, Q_ROWS:]


def attend_back_kernel(
    first_ref, count_ref, q_ref, k_ref, v_ref, o_ref, g_ref, lse_ref, cos_ref, sin_ref, code_ref,
    low_ref, high_ref, joint_ref, acc, keys, values, stacked, grads, delta, level,
):
    own = pl.program_id(0)
    keys[...] = jnp.zeros_like(keys)
    values[...] = jnp.zeros_like(values)

    @pl.loop(0, S // Q_ROWS)
    def _(block):
        start = pl.multiple_of(block * Q_ROWS, Q_ROWS)
        rows = pl.ds(start, Q_ROWS)
        for pair in range(PAIRS):
            lanes = slice(pair * LANES, (pair + 1) * LANES)
            stacked[pair] = stack_heads(q_ref[rows, lanes])
            grad = g_ref[rows, lanes]
            grads[pair] = stack_heads(grad)
            both = jnp.transpose(grad.astype(jnp.float32) * o_ref[rows, lanes].astype(jnp.float32))
            delta[pair] = jnp.concatenate(
                [
                    jnp.sum(both[:HEAD_DIM], axis=0, keepdims=True),
                    jnp.sum(both[HEAD_DIM:], axis=0, keepdims=True),
                ],
                axis=1,
            )
            level[pair] = jnp.concatenate(
                [lse_ref[pl.ds(2 * pair, 1), rows], lse_ref[pl.ds(2 * pair + 1, 1), rows]], axis=1
            )
        acc[...] = jnp.zeros_like(acc)
        low = low_ref[:, rows]
        high = high_ref[:, rows]

        @pl.loop(0, count_ref[own, block])
        def _(step):
            window = pl.ds(pl.multiple_of(first_ref[own, block] + step * K_ROWS, 16), K_ROWS)
            bias = mask_bias(code_ref[window, :], low, high)
            for pair in range(PAIRS):
                lanes = slice(pair * LANES, (pair + 1) * LANES)
                query = stacked[pair]
                grad = grads[pair]
                key = k_ref[window, lanes]
                scores = dot(key, query, NT) + bias
                probs = jnp.exp(scores - level[pair])
                prob_grad = dot(v_ref[window, lanes], grad, NT)
                score_grad = (probs * (prob_grad - delta[pair])).astype(jnp.bfloat16)
                values[window, lanes] += dot(probs.astype(jnp.bfloat16), grad, NN)
                keys[window, lanes] += dot(score_grad, query, NN)
                acc[pair] += pick_heads(dot(key, score_grad, TN))

        cosine = cos_ref[rows, :]
        sine = sin_ref[rows, :]
        for pair in range(PAIRS):
            lanes = slice(pair * LANES, (pair + 1) * LANES)
            query = jnp.transpose(acc[pair]) * (HEAD_DIM**-0.5)
            joint_ref[rows, lanes] = (query * cosine - swap_pairs(query) * sine).astype(jnp.bfloat16)

    @pl.loop(0, S // Q_ROWS)
    def _(block):
        rows = pl.ds(pl.multiple_of(block * Q_ROWS, Q_ROWS), Q_ROWS)
        cosine = cos_ref[rows, :]
        sine = sin_ref[rows, :]
        for pair in range(PAIRS):
            lanes = slice(pair * LANES, (pair + 1) * LANES)
            key = keys[rows, lanes]
            joint_ref[rows, D + pair * LANES : D + (pair + 1) * LANES] = (
                key * cosine - swap_pairs(key) * sine
            ).astype(jnp.bfloat16)
            joint_ref[rows, 2 * D + pair * LANES : 2 * D + (pair + 1) * LANES] = values[
                rows, lanes
            ].astype(jnp.bfloat16)


def whole(*shape):
    return pl.BlockSpec(shape, lambda i, *_: (0,) * len(shape))


def per(*shape):
    return pl.BlockSpec((None,) + shape, lambda i, *_: (i,) + (0,) * len(shape))


def attend(first, count, x, weight, bias, cosine, sine, code, low, high):
    own = x.shape[0]
    act = jax.ShapeDtypeStruct((own, S, D), jnp.bfloat16)
    return pl.pallas_call(
        attend_kernel,
        grid_spec=pltpu.PrefetchScalarGridSpec(
            num_scalar_prefetch=2,
            grid=(own,),
            in_specs=[
                per(S, D), whole(3, D, D), whole(3, D), whole(S, LANES), whole(S, LANES),
                per(S, 1), per(1, S), per(1, S),
            ],
            out_specs=[per(S, D), per(S, D), per(S, D), per(S, D), per(HEADS, S)],
            scratch_shapes=[
                pltpu.VMEM((PAIRS, 1, 2 * Q_ROWS), jnp.float32),
                pltpu.VMEM((PAIRS, 1, 2 * Q_ROWS), jnp.float32),
                pltpu.VMEM((PAIRS, LANES, Q_ROWS), jnp.float32),
                pltpu.VMEM((PAIRS, 2 * Q_ROWS, LANES), jnp.bfloat16),
            ],
        ),
        out_shape=[act, act, act, act, jax.ShapeDtypeStruct((own, HEADS, S), jnp.float32)],
        compiler_params=pltpu.CompilerParams(vmem_limit_bytes=60 << 20),
        name="attend",
        cost_estimate=pl.CostEstimate(flops=6 * 10**9, bytes_accessed=12 << 20, transcendentals=6 << 20),
    )(first, count, x, weight, bias, cosine, sine, code, low, high)


def attend_back(first, count, q, k, v, o, g, lse, cosine, sine, code, low, high):
    own = q.shape[0]
    return pl.pallas_call(
        attend_back_kernel,
        grid_spec=pltpu.PrefetchScalarGridSpec(
            num_scalar_prefetch=2,
            grid=(own,),
            in_specs=[
                per(S, D), per(S, D), per(S, D), per(S, D), per(S, D), per(HEADS, S),
                whole(S, LANES), whole(S, LANES), per(S, 1), per(1, S), per(1, S),
            ],
            out_specs=per(S, 3 * D),
            scratch_shapes=[
                pltpu.VMEM((PAIRS, LANES, Q_ROWS), jnp.float32),
                pltpu.VMEM((S, D), jnp.float32),
                pltpu.VMEM((S, D), jnp.float32),
                pltpu.VMEM((PAIRS, 2 * Q_ROWS, LANES), jnp.bfloat16),
                pltpu.VMEM((PAIRS, 2 * Q_ROWS, LANES), jnp.bfloat16),
                pltpu.VMEM((PAIRS, 1, 2 * Q_ROWS), jnp.float32),
                pltpu.VMEM((PAIRS, 1, 2 * Q_ROWS), jnp.float32),
            ],
        ),
        out_shape=jax.ShapeDtypeStruct((own, S, 3 * D), jnp.bfloat16),
        compiler_params=pltpu.CompilerParams(vmem_limit_bytes=60 << 20),
        name="attend_back",
        cost_estimate=pl.CostEstimate(flops=12 * 10**9, bytes_accessed=14 << 20, transcendentals=6 << 20),
    )(first, count, q, k, v, o, g, lse, cosine, sine, code, low, high)


def mask_tables(segments, padding):
    code = 2 * segments + padding
    low = code
    high = 2 * segments + 1
    blocks = segments.reshape(segments.shape[0], S // Q_ROWS, Q_ROWS)
    begin = jnp.sum(segments[:, None, :] < blocks[:, :, :1], axis=-1, dtype=jnp.int32)
    end = jnp.sum(segments[:, None, :] <= blocks[:, :, -1:], axis=-1, dtype=jnp.int32)
    begin = begin // 16 * 16
    count = (end - begin + K_ROWS - 1) // K_ROWS
    first = jnp.minimum(begin, S - count * K_ROWS)
    return first, count, code[:, :, None], low[:, None, :], high[:, None, :]


def angles():
    position = jnp.arange(S, dtype=jnp.int32).astype(jnp.float32)
    column = jnp.arange(LANES, dtype=jnp.int32) % HEAD_DIM // 2
    rate = jnp.exp(column.astype(jnp.float32) * (-2.0 * math.log(10000.0) / HEAD_DIM))
    phase = position[:, None] * rate[None, :]
    return jnp.cos(phase), jnp.sin(phase)


MESH = pl.DeviceIdType.MESH
ROWS = ("shard", "ctx")
EVERY = ("shard", "ctx", "tp")
SEQ = ("ctx", "tp")

ROUTES = {"up": "zyx", "attend": "zyx", "down": "zxy", "project": "xyz", "vectors": "xyz"}
ITEMS = ("project", "up", "down", "attend", "vectors")


def places(depth):
    steps = [0]
    for k in range(1, depth):
        steps += [k, -k]
    return [(k, dy, dx) for k in steps for dy in (0, 1) for dx in (0, 1)]


def hops(place):
    return abs(place[0]) + place[1] + place[2]


def links(route, place, depth):
    apart = {"z": place[0] != 0, "y": place[1], "x": place[2]}
    level = max([i for i, axis in enumerate(route) if apart[axis]], default=-1)
    sign = (place[0] > 0) - (place[0] < 0)
    onward = []
    if level >= 0 and route[level] == "z" and abs(place[0]) + 1 < depth:
        onward.append(("z", -sign))
    for axis in route[level + 1 :]:
        onward += [("z", 1), ("z", -1)] if axis == "z" else [(axis, 1)]
    back = None if level < 0 else (route[level], sign if route[level] == "z" else 1)
    return back, onward


def seen_from(place, link):
    k, dy, dx = place
    axis, way = link
    return {"z": (k - way, dy, dx), "y": (k, 1 - dy, dx), "x": (k, dy, 1 - dx)}[axis]


class Here:
    def __init__(self):
        self.depth = lax.axis_size("shard")
        self.z = lax.axis_index("shard")
        self.c = lax.axis_index("ctx")
        self.t = lax.axis_index("tp")
        self.y = self.c // 2
        self.x = self.c % 2

    def device(self, link):
        axis, way = link
        if axis == "z":
            return (self.z + way, self.c, self.t)
        if axis == "y":
            return (self.z, 2 * (1 - self.y) + self.x, self.t)
        if axis == "x":
            return (self.z, 2 * self.y + (1 - self.x), self.t)
        return (self.z, self.c, 1 - self.t)

    def piece(self, place):
        k, dy, dx = place
        y = 1 - self.y if dy else self.y
        x = 1 - self.x if dx else self.x
        return (self.z + k) * 4 + 2 * y + x

    def inside(self, way):
        if way == 0:
            return None
        return self.z + way < self.depth if way > 0 else self.z + way >= 0

    def meet(self):
        barrier = pltpu.get_barrier_semaphore()
        for link in (("x", 1), ("y", 1), ("tp", 1)):
            pl.semaphore_signal(barrier, inc=1, device_id=self.device(link), device_id_type=MESH)
        for way in (1, -1):

            @pl.when(self.inside(way))
            def _():
                pl.semaphore_signal(
                    barrier, inc=1, device_id=self.device(("z", way)), device_id_type=MESH
                )

        peers = 3 + (self.z > 0).astype(jnp.int32) + (self.z < self.depth - 1).astype(jnp.int32)
        pl.semaphore_wait(barrier, peers)


def guarded(condition, action):
    if condition is None:
        action()
    else:
        pl.when(condition)(action)


def columns(half, width):
    return pl.ds(pl.multiple_of(half * width, LANES), width)


def block_of(name, ref, piece, half, width):
    if name == "project":
        return ref.at[:, piece, :, columns(half, width)]
    if name == "vectors":
        return ref.at[piece]
    return ref.at[piece, :, columns(half, width)]


def gather_kernel(widths, chip_count, *refs):
    count = len(ITEMS)
    shards = dict(zip(ITEMS, refs[:count]))
    wholes = dict(zip(ITEMS, refs[count : 2 * count]))
    send_sem, recv_sem, side_send, side_recv, own_sem = refs[2 * count :]
    here = Here()
    spots = places(chip_count)
    order = sorted(spots, key=hops)
    slot = {}
    for i, name in enumerate(ITEMS):
        for place in spots:
            for link in links(ROUTES[name], place, chip_count)[1]:
                slot[name, place, link] = len(slot)

    def block(name, place, half):
        return block_of(name, wholes[name], here.piece(place), half, widths[name])

    def send(name, place, link):
        source = shards[name] if place == (0, 0, 0) else block(name, place, here.t)
        return pltpu.make_async_remote_copy(
            src_ref=source,
            dst_ref=block(name, place, here.t),
            send_sem=send_sem.at[slot[name, place, link]],
            recv_sem=recv_sem.at[ITEMS.index(name), spots.index(seen_from(place, link))],
            device_id=here.device(link),
            device_id_type=MESH,
        )

    def side(name, place, half):
        source = shards[name] if place == (0, 0, 0) else block(name, place, half)
        return pltpu.make_async_remote_copy(
            src_ref=source,
            dst_ref=block(name, place, half),
            send_sem=side_send.at[ITEMS.index(name), spots.index(place)],
            recv_sem=side_recv.at[ITEMS.index(name), spots.index(place)],
            device_id=here.device(("tp", 1)),
            device_id_type=MESH,
        )

    def arrival(name, place):
        return pltpu.make_async_remote_copy(
            src_ref=block(name, place, here.t),
            dst_ref=block(name, place, here.t),
            send_sem=send_sem.at[0],
            recv_sem=recv_sem.at[ITEMS.index(name), spots.index(place)],
            device_id=here.device(("tp", 1)),
            device_id_type=MESH,
        )

    here.meet()
    for name in ITEMS:
        pltpu.make_async_copy(
            shards[name], block(name, (0, 0, 0), here.t), own_sem.at[ITEMS.index(name)]
        ).start()
    for place in order:

        def pass_on(place=place):
            for name in ITEMS:
                if place != (0, 0, 0):
                    arrival(name, place).wait_recv()
                for link in links(ROUTES[name], place, chip_count)[1]:
                    guarded(
                        here.inside(link[1]) if link[0] == "z" else None,
                        lambda link=link: send(name, place, link).start(),
                    )
                if name != "vectors":
                    side(name, place, here.t).start()

        guarded(here.inside(place[0]), pass_on)
    for place in order:

        def finish(place=place):
            for name in ITEMS:
                if name != "vectors":
                    side(name, place, 1 - here.t).wait_recv()
                    side(name, place, here.t).wait_send()
                for link in links(ROUTES[name], place, chip_count)[1]:
                    guarded(
                        here.inside(link[1]) if link[0] == "z" else None,
                        lambda link=link: send(name, place, link).wait_send(),
                    )

        guarded(here.inside(place[0]), finish)
    for name in ITEMS:
        pltpu.make_async_copy(
            shards[name], block(name, (0, 0, 0), here.t), own_sem.at[ITEMS.index(name)]
        ).wait()


def link_count(depth):
    return sum(len(links(ROUTES[name], place, depth)[1]) for name in ITEMS for place in places(depth))


def gather_weights(shards):
    chips, pieces = lax.axis_size("shard"), lax.axis_size("shard") * lax.axis_size("ctx")
    widths = {name: shards[name].shape[-1] for name in ITEMS}
    shapes = []
    for name in ITEMS:
        shape = shards[name].shape
        if name == "project":
            shape = (shape[0], pieces, shape[1], 2 * shape[2])
        elif name == "vectors":
            shape = (pieces,) + shape
        else:
            shape = (pieces, shape[0], 2 * shape[1])
        shapes.append(jax.ShapeDtypeStruct(shape, jnp.bfloat16))
    spots = len(places(chips))
    outs = pl.pallas_call(
        lambda *refs: gather_kernel(widths, chips, *refs),
        out_shape=shapes,
        in_specs=[pl.BlockSpec(memory_space=pl.ANY)] * len(ITEMS),
        out_specs=[pl.BlockSpec(memory_space=pl.ANY)] * len(ITEMS),
        scratch_shapes=[
            pltpu.SemaphoreType.DMA((link_count(chips),)),
            pltpu.SemaphoreType.DMA((len(ITEMS), spots)),
            pltpu.SemaphoreType.DMA((len(ITEMS), spots)),
            pltpu.SemaphoreType.DMA((len(ITEMS), spots)),
            pltpu.SemaphoreType.DMA((len(ITEMS),)),
        ],
        compiler_params=pltpu.CompilerParams(collective_id=0, has_side_effects=True),
        name="gather_weights",
    )(*[shards[name] for name in ITEMS])
    return dict(zip(ITEMS, outs))


def add_into(target, addend):
    lead = target.shape[:-2]
    for index in range(math.prod(lead)):
        at = (index,) if lead else ()
        height = 16 if target.shape[-2] % 16 == 0 else 8

        @pl.loop(0, target.shape[-2] // height)
        def _(step):
            rows = pl.ds(pl.multiple_of(step * height, height), height)
            where = at + (rows, slice(None))
            total = target[where].astype(jnp.float32) + addend[where].astype(jnp.float32)
            target[where] = total.astype(target.dtype)


def scatter_kernel(widths, chip_count, *refs):
    count = len(ITEMS)
    grads = dict(zip(ITEMS, refs[:count]))
    outs = dict(zip(ITEMS, refs[count : 2 * count]))
    mine = dict(zip(ITEMS, refs[2 * count : 3 * count]))
    theirs = dict(zip(ITEMS, refs[3 * count : 4 * count]))
    inbox = dict(zip(ITEMS, refs[4 * count : 5 * count]))
    load_sem, side_send, side_recv, send_sem, recv_sem = refs[5 * count :]
    here = Here()
    spots = places(chip_count)
    order = sorted(spots, key=hops, reverse=True)
    slot = {}
    box = {}
    for name in ITEMS:
        local = 0
        for place in spots:
            for link in links(ROUTES[name], place, chip_count)[1]:
                slot[name, place, link] = len(slot)
                box[name, place, link] = local
                local += 1

    def opposite(link):
        return (link[0], -link[1]) if link[0] == "z" else link

    def load(name, place):
        return pltpu.make_async_copy(
            block_of(name, grads[name], here.piece(place), here.t, widths[name]),
            mine[name].at[spots.index(place)],
            load_sem.at[ITEMS.index(name), spots.index(place)],
        )

    def side(name, place):
        return pltpu.make_async_remote_copy(
            src_ref=block_of(name, grads[name], here.piece(place), 1 - here.t, widths[name]),
            dst_ref=theirs[name].at[spots.index(place)],
            send_sem=side_send.at[ITEMS.index(name), spots.index(place)],
            recv_sem=side_recv.at[ITEMS.index(name), spots.index(place)],
            device_id=here.device(("tp", 1)),
            device_id_type=MESH,
        )

    def send(name, place, link):
        there = seen_from(place, link)
        return pltpu.make_async_remote_copy(
            src_ref=mine[name].at[spots.index(place)],
            dst_ref=inbox[name].at[box[name, there, opposite(link)]],
            send_sem=send_sem.at[ITEMS.index(name), spots.index(place)],
            recv_sem=recv_sem.at[slot[name, there, opposite(link)]],
            device_id=here.device(link),
            device_id_type=MESH,
        )

    def arrival(name, place, link):
        return pltpu.make_async_remote_copy(
            src_ref=inbox[name].at[box[name, place, link]],
            dst_ref=inbox[name].at[box[name, place, link]],
            send_sem=send_sem.at[0, 0],
            recv_sem=recv_sem.at[slot[name, place, link]],
            device_id=here.device(link),
            device_id_type=MESH,
        )

    here.meet()
    for place in order:

        def begin(place=place):
            for name in ITEMS:
                side(name, place).start()
                load(name, place).start()

        guarded(here.inside(place[0]), begin)
    for place in order:

        def settle(place=place):
            for name in ITEMS:
                back, onward = links(ROUTES[name], place, chip_count)
                total = mine[name].at[spots.index(place)]
                load(name, place).wait()
                side(name, place).wait_recv()
                add_into(total, theirs[name].at[spots.index(place)])
                for link in onward:

                    def take(link=link):
                        arrival(name, place, link).wait_recv()
                        add_into(total, inbox[name].at[box[name, place, link]])

                    guarded(here.inside(link[1]) if link[0] == "z" else None, take)
                if back is not None:
                    send(name, place, back).start()

        guarded(here.inside(place[0]), settle)
    for name in ITEMS:
        outs[name][...] = mine[name][spots.index((0, 0, 0))].astype(jnp.float32)
    for place in order:

        def finish(place=place):
            for name in ITEMS:
                back, _ = links(ROUTES[name], place, chip_count)
                side(name, place).wait_send()
                if back is not None:
                    send(name, place, back).wait_send()

        guarded(here.inside(place[0]), finish)


def scatter_grads(grads):
    chips = lax.axis_size("shard")
    spots = len(places(chips))
    widths, blocks, boxes = {}, [], []
    for name in ITEMS:
        shape = grads[name].shape
        if name == "project":
            block = (shape[0], shape[2], shape[3] // 2)
        elif name == "vectors":
            block = shape[1:]
        else:
            block = (shape[1], shape[2] // 2)
        widths[name] = block[-1]
        blocks.append(block)
        boxes.append(sum(len(links(ROUTES[name], place, chips)[1]) for place in places(chips)))
    kinds = [grads[name].dtype for name in ITEMS]
    outs = pl.pallas_call(
        lambda *refs: scatter_kernel(widths, chips, *refs),
        out_shape=[jax.ShapeDtypeStruct(block, jnp.float32) for block in blocks],
        in_specs=[pl.BlockSpec(memory_space=pl.ANY)] * len(ITEMS),
        out_specs=[pl.BlockSpec(memory_space=pltpu.VMEM)] * len(ITEMS),
        scratch_shapes=(
            [pltpu.VMEM((spots,) + block, kind) for block, kind in zip(blocks, kinds)]
            + [pltpu.VMEM((spots,) + block, kind) for block, kind in zip(blocks, kinds)]
            + [pltpu.VMEM((box,) + block, kind) for box, block, kind in zip(boxes, blocks, kinds)]
            + [
                pltpu.SemaphoreType.DMA((len(ITEMS), spots)),
                pltpu.SemaphoreType.DMA((len(ITEMS), spots)),
                pltpu.SemaphoreType.DMA((len(ITEMS), spots)),
                pltpu.SemaphoreType.DMA((len(ITEMS), spots)),
                pltpu.SemaphoreType.DMA((link_count(chips),)),
            ]
        ),
        compiler_params=pltpu.CompilerParams(
            collective_id=1, has_side_effects=True, vmem_limit_bytes=60 << 20
        ),
        name="scatter_grads",
    )(*[grads[name] for name in ITEMS])
    return dict(zip(ITEMS, outs))


def normalize(rows, gain, shift):
    mean = jnp.mean(rows, axis=-1, keepdims=True)
    centred = rows - mean
    factor = lax.rsqrt(jnp.mean(centred * centred, axis=-1, keepdims=True) + norm_eps)
    unit = centred * factor
    return (unit * gain + shift, unit, factor)


def normalize_back(incoming, unit, factor, gain):
    gain_grad = jnp.sum(incoming * unit, axis=0)
    shift_grad = jnp.sum(incoming, axis=0)
    inner = incoming * gain
    rows_grad = factor * (
        inner
        - jnp.mean(inner, axis=-1, keepdims=True)
        - unit * jnp.mean(inner * unit, axis=-1, keepdims=True)
    )
    return (rows_grad, gain_grad, shift_grad)


def gelu_slope(values):
    cumulative = 0.5 * (1.0 + lax.erf(values * (1.0 / math.sqrt(2.0))))
    density = jnp.exp(-0.5 * values * values) * (1.0 / math.sqrt(2.0 * math.pi))
    return cumulative + values * density


def fitting(shards):
    return lax.axis_size("ctx") == 4 and lax.axis_size("tp") == 2 and shards["up"].shape[0] % 16 == 0


def gather_plain(shards):
    wholes = {}
    for name in ITEMS:
        axis = 1 if name == "project" else 0
        part = lax.all_gather(shards[name], ROWS, axis=axis)
        if name != "vectors":
            part = lax.all_gather(part, "tp", axis=axis + 2, tiled=True)
        wholes[name] = part
    return wholes


def scatter_plain(grads):
    shards = {}
    for name in ITEMS:
        axis = 1 if name == "project" else 0
        part = grads[name]
        if name == "vectors":
            part = lax.psum(part, "tp")
        else:
            part = lax.psum_scatter(part, "tp", scatter_dimension=axis + 2, tiled=True)
        part = lax.psum_scatter(part, ROWS, scatter_dimension=axis, tiled=False)
        shards[name] = part.astype(jnp.float32)
    return shards


def local(
    tokens, project_weight, attend_weight, up_weight, down_weight, project_bias, attend_bias,
    up_bias, down_bias, first_gain, first_shift, second_gain, second_shift, segment_ids, padding,
    cotangent,
):
    seq_count = tokens.shape[0]
    members = lax.axis_size("ctx") * lax.axis_size("tp")
    own = seq_count // members
    rank = lax.axis_index("ctx") * lax.axis_size("tp") + lax.axis_index("tp")
    rows = own * S
    pieces = lax.axis_size("shard") * lax.axis_size("ctx")
    depth = D // pieces

    def to_sequences(array):
        parts = array.reshape((members, own) + array.shape[1:])
        parts = lax.all_to_all(parts, SEQ, 0, 0, tiled=True)
        return jnp.swapaxes(parts, 0, 1).reshape(own, S, D)

    def to_blocks(array):
        parts = jnp.swapaxes(array.reshape(own, members, S // members, D), 0, 1)
        return lax.all_to_all(parts, SEQ, 0, 0, tiled=True).reshape(tokens.shape)

    x = to_sequences(tokens)
    segments = lax.dynamic_slice_in_dim(segment_ids, rank * own, own, 0)
    pads = lax.dynamic_slice_in_dim(padding, rank * own, own, 0)

    vectors = jnp.concatenate(
        [
            project_bias,
            attend_bias[None],
            down_bias[None],
            first_gain[None],
            first_shift[None],
            second_gain[None],
            second_shift[None],
            up_bias.reshape(FF // D, depth),
        ],
        axis=0,
    )
    shards = {
        "project": jnp.transpose(project_weight, (1, 0, 2)),
        "up": up_weight,
        "down": jnp.transpose(down_weight),
        "attend": jnp.transpose(attend_weight),
        "vectors": jnp.pad(vectors, ((0, 3), (0, LANES - depth))),
    }
    custom = fitting(shards)
    wholes = gather_weights(shards) if custom else gather_plain(shards)
    project = wholes["project"].reshape(3, D, D)
    up = wholes["up"].reshape(D, FF)
    down_t = wholes["down"].reshape(D, FF)
    attend_t = wholes["attend"].reshape(D, D)
    vectors = wholes["vectors"][:, :13, :depth].astype(jnp.float32)
    wide = jnp.transpose(vectors[:, :9], (1, 0, 2)).reshape(9, D)
    up_shift = vectors[:, 9:].reshape(FF)

    tables = mask_tables(segments, pads)
    cosine, sine = angles()
    query, key, value, attended, level = attend(
        tables[0], tables[1], x, project, wide[:3], cosine, sine, *tables[2:]
    )
    flat = x.reshape(rows, D)
    attended_flat = attended.reshape(rows, D)
    branch = dot(attended_flat, attend_t, NT) + wide[3]
    first, first_unit, first_factor = normalize(flat.astype(jnp.float32) + branch, wide[5], wide[6])
    first_low = first.astype(jnp.bfloat16)
    pre = dot(first_low, up, NN) + up_shift
    hidden = jax.nn.gelu(pre, approximate=False).astype(jnp.bfloat16)
    ffn = dot(hidden, down_t, NT) + wide[4]
    second, second_unit, second_factor = normalize(first + ffn, wide[7], wide[8])
    output = to_blocks(second.astype(jnp.bfloat16).reshape(own, S, D))

    incoming = to_sequences(cotangent).reshape(rows, D).astype(jnp.float32)
    second_grad, second_gain_grad, second_shift_grad = normalize_back(
        incoming, second_unit, second_factor, wide[7]
    )
    ffn_grad = second_grad.astype(jnp.bfloat16)
    down_bias_grad = jnp.sum(ffn_grad.astype(jnp.float32), axis=0)
    down_t_grad = dot(ffn_grad, hidden, TN)
    pre_grad = (dot(ffn_grad, down_t, NN) * gelu_slope(pre)).astype(jnp.bfloat16)
    up_bias_grad = jnp.sum(pre_grad.astype(jnp.float32), axis=0)
    up_grad = dot(first_low, pre_grad, TN)
    first_total = second_grad + dot(pre_grad, up, NT)
    first_grad, first_gain_grad, first_shift_grad = normalize_back(
        first_total, first_unit, first_factor, wide[5]
    )
    branch_grad = first_grad.astype(jnp.bfloat16)
    attend_bias_grad = jnp.sum(branch_grad.astype(jnp.float32), axis=0)
    attend_t_grad = dot(branch_grad, attended_flat, TN)
    attended_grad = dot(branch_grad, attend_t, NN).astype(jnp.bfloat16)

    joint_grad = attend_back(
        tables[0], tables[1], query, key, value, attended, attended_grad.reshape(own, S, D), level,
        cosine, sine, *tables[2:],
    ).reshape(rows, 3 * D)
    project_bias_grad = jnp.sum(joint_grad.astype(jnp.float32), axis=0).reshape(3, D)
    project_grad = jnp.stack(
        [dot(flat, joint_grad[:, i * D : (i + 1) * D], TN) for i in range(3)]
    )
    token_part = sum(
        dot(joint_grad[:, i * D : (i + 1) * D], project[i], NT) for i in range(3)
    )
    tokens_grad = to_blocks((first_grad + token_part).astype(jnp.bfloat16).reshape(own, S, D))

    sums = jnp.concatenate(
        [
            project_bias_grad,
            attend_bias_grad[None],
            down_bias_grad[None],
            first_gain_grad[None],
            first_shift_grad[None],
            second_gain_grad[None],
            second_shift_grad[None],
        ],
        axis=0,
    )
    sums = jnp.concatenate(
        [
            jnp.transpose(sums.reshape(9, pieces, depth), (1, 0, 2)),
            up_bias_grad.reshape(pieces, FF // D, depth),
        ],
        axis=1,
    )
    grads = {
        "project": project_grad.astype(jnp.bfloat16).reshape(3, pieces, depth, D),
        "up": up_grad.astype(jnp.bfloat16).reshape(pieces, depth, FF),
        "down": down_t_grad.astype(jnp.bfloat16).reshape(pieces, depth, FF),
        "attend": attend_t_grad.astype(jnp.bfloat16).reshape(pieces, depth, D),
        "vectors": jnp.pad(sums, ((0, 0), (0, 3), (0, LANES - depth))),
    }
    shards = scatter_grads(grads) if custom else scatter_plain(grads)
    sums = shards["vectors"][:13, :depth]
    return (
        output,
        tokens_grad,
        jnp.transpose(shards["project"], (1, 0, 2)),
        jnp.transpose(shards["attend"]),
        shards["up"],
        jnp.transpose(shards["down"]),
        sums[:3],
        sums[3],
        sums[9:].reshape(-1),
        sums[4],
        sums[5],
        sums[6],
        sums[7],
        sums[8],
    )


def solution(mesh):
    in_specs = (
        P("shard", ("ctx", "tp"), None),
        P(("shard", "ctx"), None, "tp"),
        P("tp", ("shard", "ctx")),
        P(("shard", "ctx"), "tp"),
        P("tp", ("shard", "ctx")),
        P(None, ("shard", "ctx")),
        P(("shard", "ctx")),
        P(("shard", "ctx")),
        P(("shard", "ctx")),
        P(("shard", "ctx")),
        P(("shard", "ctx")),
        P(("shard", "ctx")),
        P(("shard", "ctx")),
        P("shard", None),
        P("shard", None),
        P("shard", ("ctx", "tp"), None),
    )
    out_specs = (
        P("shard", ("ctx", "tp"), None),
        P("shard", ("ctx", "tp"), None),
        P(("shard", "ctx"), None, "tp"),
        P("tp", ("shard", "ctx")),
        P(("shard", "ctx"), "tp"),
        P("tp", ("shard", "ctx")),
        P(None, ("shard", "ctx")),
        P(("shard", "ctx")),
        P(("shard", "ctx")),
        P(("shard", "ctx")),
        P(("shard", "ctx")),
        P(("shard", "ctx")),
        P(("shard", "ctx")),
        P(("shard", "ctx")),
    )
    return jax.shard_map(local, mesh=mesh, in_specs=in_specs, out_specs=out_specs, check_vma=False)
```

```python
import math

import jax
import jax.numpy as jnp
from jax import lax
from jax.experimental import pallas as pl
from jax.experimental.pallas import tpu as pltpu
from jax.sharding import PartitionSpec as P

D = 768
HEADS = 12
HEAD_DIM = 64
FF = 3072
S = 1024
LANES = 128
PAIRS = HEADS // 2
Q_ROWS = 128
K_ROWS = 256

norm_eps = 1e-12
mask_fill = -1000000000.0

NT = (((1,), (1,)), ((), ()))
TN = (((0,), (0,)), ((), ()))
NN = (((1,), (0,)), ((), ()))


def dot(left, right, dims):
    return lax.dot_general(left, right, dims, preferred_element_type=jnp.float32)


def swap_pairs(values):
    lane = lax.broadcasted_iota(jnp.int32, values.shape, 1)
    width = values.shape[1]
    return jnp.where(
        lane % 2 == 0, -pltpu.roll(values, width - 1, 1), pltpu.roll(values, 1, 1)
    )


def stack_heads(rows):
    lane = lax.broadcasted_iota(jnp.int32, rows.shape, 1)
    zero = jnp.zeros_like(rows)
    return jnp.concatenate(
        [jnp.where(lane < HEAD_DIM, rows, zero), jnp.where(lane < HEAD_DIM, zero, rows)], axis=0
    )


def pick_heads(both):
    return jnp.concatenate([both[:HEAD_DIM, :Q_ROWS], both[HEAD_DIM:, Q_ROWS:]], axis=0)


def spread_heads(row):
    return jnp.concatenate(
        [
            jnp.broadcast_to(row[:, :Q_ROWS], (HEAD_DIM, Q_ROWS)),
            jnp.broadcast_to(row[:, Q_ROWS:], (HEAD_DIM, Q_ROWS)),
        ],
        axis=0,
    )


def mask_bias(key_code, query_low, query_high):
    keys = jnp.broadcast_to(key_code, (K_ROWS, Q_ROWS))
    allowed = (keys >= query_low) & (keys <= query_high)
    bias = jnp.where(allowed, 0.0, mask_fill)
    return jnp.concatenate([bias, bias], axis=1)


def attend_kernel(
    first_ref, count_ref, x_ref, w_ref, b_ref, cos_ref, sin_ref, code_ref, low_ref, high_ref,
    q_ref, k_ref, v_ref, o_ref, lse_ref, top, total, acc, stacked,
):
    own = pl.program_id(0)
    row_tile = 256

    @pl.loop(0, S // row_tile)
    def _(tile):
        rows = pl.ds(pl.multiple_of(tile * row_tile, row_tile), row_tile)
        x = x_ref[rows, :]
        cosine = cos_ref[rows, :]
        sine = sin_ref[rows, :]
        for part, out in enumerate((q_ref, k_ref, v_ref)):
            joint = dot(x, w_ref[part], NN) + b_ref[pl.ds(part, 1), :]
            for pair in range(PAIRS):
                lanes = slice(pair * LANES, (pair + 1) * LANES)
                piece = joint[:, lanes]
                if part < 2:
                    piece = piece * cosine + swap_pairs(piece) * sine
                if part == 0:
                    piece = piece.astype(jnp.bfloat16) * jnp.asarray(HEAD_DIM**-0.5, jnp.bfloat16)
                out[rows, lanes] = piece.astype(jnp.bfloat16)

    @pl.loop(0, S // Q_ROWS)
    def _(block):
        start = pl.multiple_of(block * Q_ROWS, Q_ROWS)
        rows = pl.ds(start, Q_ROWS)
        for pair in range(PAIRS):
            stacked[pair] = stack_heads(q_ref[rows, pair * LANES : (pair + 1) * LANES])
        top[...] = jnp.full_like(top, 2.0 * mask_fill)
        total[...] = jnp.zeros_like(total)
        acc[...] = jnp.zeros_like(acc)
        low = low_ref[:, rows]
        high = high_ref[:, rows]

        @pl.loop(0, count_ref[own, block])
        def _(step):
            window = pl.ds(pl.multiple_of(first_ref[own, block] + step * K_ROWS, 16), K_ROWS)
            bias = mask_bias(code_ref[window, :], low, high)
            for pair in range(PAIRS):
                lanes = slice(pair * LANES, (pair + 1) * LANES)
                scores = dot(k_ref[window, lanes], stacked[pair], NT) + bias
                old = top[pair]
                new = jnp.maximum(old, jnp.max(scores, axis=0, keepdims=True))
                expo = jnp.exp(scores - new)
                fade = jnp.exp(old - new)
                top[pair] = new
                total[pair] = total[pair] * fade + jnp.sum(expo, axis=0, keepdims=True)
                mixed = dot(v_ref[window, lanes], expo.astype(jnp.bfloat16), TN)
                acc[pair] = acc[pair] * spread_heads(fade) + pick_heads(mixed)

        for pair in range(PAIRS):
            lanes = slice(pair * LANES, (pair + 1) * LANES)
            summed = total[pair]
            out = acc[pair] / spread_heads(summed)
            o_ref[rows, lanes] = jnp.transpose(out).astype(jnp.bfloat16)
            lse = top[pair] + jnp.log(summed)
            lse_ref[pl.ds(2 * pair, 1), rows] = lse[:, :Q_ROWS]
            lse_ref[pl.ds(2 * pair + 1, 1), rows] = lse[:, Q_ROWS:]


def attend_back_kernel(
    first_ref, count_ref, q_ref, k_ref, v_ref, o_ref, g_ref, lse_ref, cos_ref, sin_ref, code_ref,
    low_ref, high_ref, joint_ref, acc, keys, values, stacked, grads, delta, level,
):
    own = pl.program_id(0)
    keys[...] = jnp.zeros_like(keys)
    values[...] = jnp.zeros_like(values)

    @pl.loop(0, S // Q_ROWS)
    def _(block):
        start = pl.multiple_of(block * Q_ROWS, Q_ROWS)
        rows = pl.ds(start, Q_ROWS)
        for pair in range(PAIRS):
            lanes = slice(pair * LANES, (pair + 1) * LANES)
            stacked[pair] = stack_heads(q_ref[rows, lanes])
            grad = g_ref[rows, lanes]
            grads[pair] = stack_heads(grad)
            both = jnp.transpose(grad.astype(jnp.float32) * o_ref[rows, lanes].astype(jnp.float32))
            delta[pair] = jnp.concatenate(
                [
                    jnp.sum(both[:HEAD_DIM], axis=0, keepdims=True),
                    jnp.sum(both[HEAD_DIM:], axis=0, keepdims=True),
                ],
                axis=1,
            )
            level[pair] = jnp.concatenate(
                [lse_ref[pl.ds(2 * pair, 1), rows], lse_ref[pl.ds(2 * pair + 1, 1), rows]], axis=1
            )
        acc[...] = jnp.zeros_like(acc)
        low = low_ref[:, rows]
        high = high_ref[:, rows]

        @pl.loop(0, count_ref[own, block])
        def _(step):
            window = pl.ds(pl.multiple_of(first_ref[own, block] + step * K_ROWS, 16), K_ROWS)
            bias = mask_bias(code_ref[window, :], low, high)
            for pair in range(PAIRS):
                lanes = slice(pair * LANES, (pair + 1) * LANES)
                query = stacked[pair]
                grad = grads[pair]
                key = k_ref[window, lanes]
                scores = dot(key, query, NT) + bias
                probs = jnp.exp(scores - level[pair])
                prob_grad = dot(v_ref[window, lanes], grad, NT)
                score_grad = (probs * (prob_grad - delta[pair])).astype(jnp.bfloat16)
                values[window, lanes] += dot(probs.astype(jnp.bfloat16), grad, NN)
                keys[window, lanes] += dot(score_grad, query, NN)
                acc[pair] += pick_heads(dot(key, score_grad, TN))

        cosine = cos_ref[rows, :]
        sine = sin_ref[rows, :]
        for pair in range(PAIRS):
            lanes = slice(pair * LANES, (pair + 1) * LANES)
            query = jnp.transpose(acc[pair]) * (HEAD_DIM**-0.5)
            joint_ref[rows, lanes] = (query * cosine - swap_pairs(query) * sine).astype(jnp.bfloat16)

    @pl.loop(0, S // Q_ROWS)
    def _(block):
        rows = pl.ds(pl.multiple_of(block * Q_ROWS, Q_ROWS), Q_ROWS)
        cosine = cos_ref[rows, :]
        sine = sin_ref[rows, :]
        for pair in range(PAIRS):
            lanes = slice(pair * LANES, (pair + 1) * LANES)
            key = keys[rows, lanes]
            joint_ref[rows, D + pair * LANES : D + (pair + 1) * LANES] = (
                key * cosine - swap_pairs(key) * sine
            ).astype(jnp.bfloat16)
            joint_ref[rows, 2 * D + pair * LANES : 2 * D + (pair + 1) * LANES] = values[
                rows, lanes
            ].astype(jnp.bfloat16)


def whole(*shape):
    return pl.BlockSpec(shape, lambda i, *_: (0,) * len(shape))


def per(*shape):
    return pl.BlockSpec((None,) + shape, lambda i, *_: (i,) + (0,) * len(shape))


def attend(first, count, x, weight, bias, cosine, sine, code, low, high):
    own = x.shape[0]
    act = jax.ShapeDtypeStruct((own, S, D), jnp.bfloat16)
    return pl.pallas_call(
        attend_kernel,
        grid_spec=pltpu.PrefetchScalarGridSpec(
            num_scalar_prefetch=2,
            grid=(own,),
            in_specs=[
                per(S, D), whole(3, D, D), whole(3, D), whole(S, LANES), whole(S, LANES),
                per(S, 1), per(1, S), per(1, S),
            ],
            out_specs=[per(S, D), per(S, D), per(S, D), per(S, D), per(HEADS, S)],
            scratch_shapes=[
                pltpu.VMEM((PAIRS, 1, 2 * Q_ROWS), jnp.float32),
                pltpu.VMEM((PAIRS, 1, 2 * Q_ROWS), jnp.float32),
                pltpu.VMEM((PAIRS, LANES, Q_ROWS), jnp.float32),
                pltpu.VMEM((PAIRS, 2 * Q_ROWS, LANES), jnp.bfloat16),
            ],
        ),
        out_shape=[act, act, act, act, jax.ShapeDtypeStruct((own, HEADS, S), jnp.float32)],
        compiler_params=pltpu.CompilerParams(vmem_limit_bytes=60 << 20),
        name="attend",
        cost_estimate=pl.CostEstimate(flops=6 * 10**9, bytes_accessed=12 << 20, transcendentals=6 << 20),
    )(first, count, x, weight, bias, cosine, sine, code, low, high)


def attend_back(first, count, q, k, v, o, g, lse, cosine, sine, code, low, high):
    own = q.shape[0]
    return pl.pallas_call(
        attend_back_kernel,
        grid_spec=pltpu.PrefetchScalarGridSpec(
            num_scalar_prefetch=2,
            grid=(own,),
            in_specs=[
                per(S, D), per(S, D), per(S, D), per(S, D), per(S, D), per(HEADS, S),
                whole(S, LANES), whole(S, LANES), per(S, 1), per(1, S), per(1, S),
            ],
            out_specs=per(S, 3 * D),
            scratch_shapes=[
                pltpu.VMEM((PAIRS, LANES, Q_ROWS), jnp.float32),
                pltpu.VMEM((S, D), jnp.float32),
                pltpu.VMEM((S, D), jnp.float32),
                pltpu.VMEM((PAIRS, 2 * Q_ROWS, LANES), jnp.bfloat16),
                pltpu.VMEM((PAIRS, 2 * Q_ROWS, LANES), jnp.bfloat16),
                pltpu.VMEM((PAIRS, 1, 2 * Q_ROWS), jnp.float32),
                pltpu.VMEM((PAIRS, 1, 2 * Q_ROWS), jnp.float32),
            ],
        ),
        out_shape=jax.ShapeDtypeStruct((own, S, 3 * D), jnp.bfloat16),
        compiler_params=pltpu.CompilerParams(vmem_limit_bytes=60 << 20),
        name="attend_back",
        cost_estimate=pl.CostEstimate(flops=12 * 10**9, bytes_accessed=14 << 20, transcendentals=6 << 20),
    )(first, count, q, k, v, o, g, lse, cosine, sine, code, low, high)


def mask_tables(segments, padding):
    code = 2 * segments + padding
    low = code
    high = 2 * segments + 1
    blocks = segments.reshape(segments.shape[0], S // Q_ROWS, Q_ROWS)
    begin = jnp.sum(segments[:, None, :] < blocks[:, :, :1], axis=-1, dtype=jnp.int32)
    end = jnp.sum(segments[:, None, :] <= blocks[:, :, -1:], axis=-1, dtype=jnp.int32)
    begin = begin // 16 * 16
    count = (end - begin + K_ROWS - 1) // K_ROWS
    first = jnp.minimum(begin, S - count * K_ROWS)
    return first, count, code[:, :, None], low[:, None, :], high[:, None, :]


def angles():
    position = jnp.arange(S, dtype=jnp.int32).astype(jnp.float32)
    column = jnp.arange(LANES, dtype=jnp.int32) % HEAD_DIM // 2
    rate = jnp.exp(column.astype(jnp.float32) * (-2.0 * math.log(10000.0) / HEAD_DIM))
    phase = position[:, None] * rate[None, :]
    return jnp.cos(phase), jnp.sin(phase)


CHUNK = 512
STEP = 16
UNROLL = 4
ATTEND_BIAS, DOWN_BIAS, FIRST_GAIN, FIRST_SHIFT, SECOND_GAIN, SECOND_SHIFT = range(3, 9)
SUMS = 6


def row_mean(values):
    return jnp.sum(values, axis=-1, keepdims=True) * (1.0 / D)


def fold(values):
    return jnp.sum(values.reshape(values.shape[0] // 8, 8, values.shape[1]), axis=0)


def chunk_at(index):
    return pl.ds(pl.multiple_of(index * CHUNK, CHUNK), CHUNK)


def ffn_kernel(
    a_ref, attend_ref, wide_ref, shift_ref, x_hbm, c_hbm, up_hbm, down_hbm,
    joined_ref, branch_ref, sums_ref, up_sums_ref, out_hbm, up_grad_hbm, down_grad_hbm, attend_grad_hbm,
    x_ref, c_ref, up_ref, down_ref, out_ref, hidden_ref, slope_ref, low_ref, ffn_ref, turned_ref,
    left, right, near, far, first, unit, acc, factor, sums, up_sums, stage, in_sem, out_sem, stage_sem,
):
    loads = [
        pltpu.make_async_copy(source, target, in_sem.at[i])
        for i, (source, target) in enumerate(
            ((x_hbm, x_ref), (up_hbm, up_ref), (down_hbm, down_ref), (c_hbm, c_ref))
        )
    ]
    for load in loads:
        load.start()
    sums[...] = jnp.zeros_like(sums)
    up_sums[...] = jnp.zeros_like(up_sums)
    pairs = FF // CHUNK // 2

    def vector(index):
        return wide_ref[pl.ds(index, 1), :]

    def add_sum(index, values):
        sums[index - ATTEND_BIAS] += fold(values)

    def rows_loop(body):
        @pl.loop(0, S // STEP, unroll=UNROLL)
        def _(step):
            body(pl.ds(pl.multiple_of(step * STEP, STEP), STEP))

    acc[...] = dot(a_ref[...], attend_ref[...], NT)
    loads[0].wait()

    @rows_loop
    def _(rows):
        joined = x_ref[rows, :].astype(jnp.float32) + acc[rows, :] + vector(ATTEND_BIAS)
        centred = joined - row_mean(joined)
        scale = lax.rsqrt(row_mean(centred * centred) + norm_eps)
        normed = centred * scale
        unit[rows, :] = normed
        factor[rows, :] = scale
        result = normed * vector(FIRST_GAIN) + vector(FIRST_SHIFT)
        first[rows, :] = result
        low_ref[rows, :] = result.astype(jnp.bfloat16)

    loads[1].wait()
    loads[2].wait()

    def expand(target, index):
        target[...] = dot(low_ref[...], up_ref[:, chunk_at(index)], NN)

    def activate(source, target, index):
        pre = source[...] + shift_ref[:, chunk_at(index)]
        cumulative = 0.5 + 0.5 * lax.erf(pre * (1.0 / math.sqrt(2.0)))
        density = jnp.exp(-0.5 * pre * pre) * (1.0 / math.sqrt(2.0 * math.pi))
        hidden = (pre * cumulative).astype(jnp.bfloat16)
        target[...] = hidden
        hidden_ref[:, chunk_at(index)] = hidden
        slope_ref[:, chunk_at(index)] = (cumulative + pre * density).astype(jnp.bfloat16)

    def contract(source, index):
        acc[...] += dot(source[...], down_ref[:, chunk_at(index)], NT)

    def forward(pair, last):
        expand(right, 2 * pair + 1)
        activate(left, near, 2 * pair)
        if not last:
            expand(left, 2 * pair + 2)
        contract(near, 2 * pair)
        activate(right, far, 2 * pair + 1)
        contract(far, 2 * pair + 1)

    expand(left, 0)
    acc[...] = jnp.zeros_like(acc)

    @pl.loop(0, pairs - 1)
    def _(pair):
        forward(pair, False)

    forward(pairs - 1, True)
    loads[3].wait()

    @rows_loop
    def _(rows):
        joined = first[rows, :] + acc[rows, :] + vector(DOWN_BIAS)
        centred = joined - row_mean(joined)
        scale = lax.rsqrt(row_mean(centred * centred) + norm_eps)
        normed = centred * scale
        out_ref[rows, :] = (normed * vector(SECOND_GAIN) + vector(SECOND_SHIFT)).astype(jnp.bfloat16)
        grad = c_ref[rows, :].astype(jnp.float32)
        add_sum(SECOND_GAIN, grad * normed)
        add_sum(SECOND_SHIFT, grad)
        inner = grad * vector(SECOND_GAIN)
        back = scale * (inner - row_mean(inner) - normed * row_mean(inner * normed))
        first[rows, :] = back
        low = back.astype(jnp.bfloat16)
        ffn_ref[rows, :] = low
        add_sum(DOWN_BIAS, low.astype(jnp.float32))

    store = pltpu.make_async_copy(out_ref, out_hbm, out_sem)
    store.start()

    def stored(slot, target, index):
        return pltpu.make_async_copy(
            stage.at[slot], target.at[:, chunk_at(index)], stage_sem.at[slot]
        )

    def weight_grad(source, target):
        @pl.loop(0, pairs)
        def _(pair):
            for slot in range(2):
                index = 2 * pair + slot

                @pl.when(pair > 0)
                def _():
                    stored(slot, target, index).wait()

                stage[slot] = dot(turned_ref[...], source[:, chunk_at(index)], NN).astype(jnp.bfloat16)
                stored(slot, target, index).start()

        for slot in range(2):
            stored(slot, target, slot).wait()

    turned_ref[...] = jnp.transpose(ffn_ref[...])
    weight_grad(hidden_ref, down_grad_hbm)

    def widen(target, index):
        target[...] = dot(ffn_ref[...], down_ref[:, chunk_at(index)], NN)

    def reweigh(source, target, index):
        grad = (source[...] * slope_ref[:, chunk_at(index)].astype(jnp.float32)).astype(jnp.bfloat16)
        target[...] = grad
        hidden_ref[:, chunk_at(index)] = grad
        up_sums[:, chunk_at(index)] += fold(grad.astype(jnp.float32))

    def collect(source, index):
        acc[...] += dot(source[...], up_ref[:, chunk_at(index)], NT)

    def backward(pair, last):
        widen(right, 2 * pair + 1)
        reweigh(left, near, 2 * pair)
        if not last:
            widen(left, 2 * pair + 2)
        collect(near, 2 * pair)
        reweigh(right, far, 2 * pair + 1)
        collect(far, 2 * pair + 1)

    widen(left, 0)
    acc[...] = jnp.zeros_like(acc)

    @pl.loop(0, pairs - 1)
    def _(pair):
        backward(pair, False)

    backward(pairs - 1, True)

    @rows_loop
    def _(rows):
        grad = first[rows, :] + acc[rows, :]
        normed = unit[rows, :]
        add_sum(FIRST_GAIN, grad * normed)
        add_sum(FIRST_SHIFT, grad)
        inner = grad * vector(FIRST_GAIN)
        back = factor[rows, :] * (inner - row_mean(inner) - normed * row_mean(inner * normed))
        low = back.astype(jnp.bfloat16)
        branch_ref[rows, :] = low
        add_sum(ATTEND_BIAS, low.astype(jnp.float32))

    joined_ref[...] = dot(branch_ref[...], attend_ref[...], NN).astype(jnp.bfloat16)
    turned_ref[...] = jnp.transpose(low_ref[...])
    weight_grad(hidden_ref, up_grad_hbm)
    turned_ref[...] = jnp.transpose(branch_ref[...])
    half = D // 2
    for slot in range(2):
        part = stage.at[slot, :, :half]
        stage[slot, :, :half] = dot(
            turned_ref[...], a_ref[:, slot * half : (slot + 1) * half], NN
        ).astype(jnp.bfloat16)
        pltpu.make_async_copy(
            part, attend_grad_hbm.at[:, slot * half : (slot + 1) * half], stage_sem.at[slot]
        ).start()
    for index in range(SUMS):
        sums_ref[pl.ds(index, 1), :] = jnp.sum(sums[index], axis=0, keepdims=True)
    up_sums_ref[...] = jnp.sum(up_sums[...], axis=0, keepdims=True)
    for slot in range(2):
        pltpu.make_async_copy(
            stage.at[slot, :, :half],
            attend_grad_hbm.at[:, slot * half : (slot + 1) * half],
            stage_sem.at[slot],
        ).wait()
    store.wait()


def feed_forward(attended, x, cotangent, attend_t, up, down_t, wide, up_shift):
    vmem, hbm = pl.BlockSpec(memory_space=pltpu.VMEM), pl.BlockSpec(memory_space=pl.ANY)

    def low(*shape):
        return jax.ShapeDtypeStruct(shape, jnp.bfloat16)

    def full(*shape):
        return jax.ShapeDtypeStruct(shape, jnp.float32)

    def scratch(width, kind=jnp.bfloat16):
        return pltpu.VMEM((S, width), kind)

    return pl.pallas_call(
        ffn_kernel,
        in_specs=[vmem] * 4 + [hbm] * 4,
        out_specs=[vmem] * 4 + [hbm] * 4,
        out_shape=[
            low(S, D), low(S, D), full(SUMS, D), full(1, FF), low(S, D), low(D, FF), low(D, FF),
            low(D, D),
        ],
        scratch_shapes=[
            scratch(D), scratch(D), pltpu.VMEM((D, FF), jnp.bfloat16), pltpu.VMEM((D, FF), jnp.bfloat16),
            scratch(D), scratch(FF), scratch(FF), scratch(D), scratch(D), pltpu.VMEM((D, S), jnp.bfloat16),
            scratch(CHUNK, jnp.float32), scratch(CHUNK, jnp.float32), scratch(CHUNK), scratch(CHUNK),
            scratch(D, jnp.float32), scratch(D, jnp.float32), scratch(D, jnp.float32),
            scratch(1, jnp.float32),
            pltpu.VMEM((SUMS, 8, D), jnp.float32), pltpu.VMEM((8, FF), jnp.float32),
            pltpu.VMEM((2, D, CHUNK), jnp.bfloat16),
            pltpu.SemaphoreType.DMA((4,)), pltpu.SemaphoreType.DMA, pltpu.SemaphoreType.DMA((2,)),
        ],
        compiler_params=pltpu.CompilerParams(vmem_limit_bytes=63 << 20),
        name="feed_forward",
        cost_estimate=pl.CostEstimate(
            flops=6 * S * D * (D + 2 * FF), bytes_accessed=30 << 20, transcendentals=2 * S * FF
        ),
    )(attended, attend_t, wide, up_shift.reshape(1, FF), x, cotangent, up, down_t)


MESH = pl.DeviceIdType.MESH
ROWS = ("shard", "ctx")
EVERY = ("shard", "ctx", "tp")
SEQ = ("ctx", "tp")

ROUTES = {"up": "zyx", "attend": "zyx", "down": "zxy", "project": "xyz", "vectors": "xyz"}
ITEMS = ("project", "up", "down", "attend", "vectors")


def places(depth):
    steps = [0]
    for k in range(1, depth):
        steps += [k, -k]
    return [(k, dy, dx) for k in steps for dy in (0, 1) for dx in (0, 1)]


def hops(place):
    return abs(place[0]) + place[1] + place[2]


def links(route, place, depth):
    apart = {"z": place[0] != 0, "y": place[1], "x": place[2]}
    level = max([i for i, axis in enumerate(route) if apart[axis]], default=-1)
    sign = (place[0] > 0) - (place[0] < 0)
    onward = []
    if level >= 0 and route[level] == "z" and abs(place[0]) + 1 < depth:
        onward.append(("z", -sign))
    for axis in route[level + 1 :]:
        onward += [("z", 1), ("z", -1)] if axis == "z" else [(axis, 1)]
    back = None if level < 0 else (route[level], sign if route[level] == "z" else 1)
    return back, onward


def seen_from(place, link):
    k, dy, dx = place
    axis, way = link
    return {"z": (k - way, dy, dx), "y": (k, 1 - dy, dx), "x": (k, dy, 1 - dx)}[axis]


class Here:
    def __init__(self):
        self.depth = lax.axis_size("shard")
        self.z = lax.axis_index("shard")
        self.c = lax.axis_index("ctx")
        self.t = lax.axis_index("tp")
        self.y = self.c // 2
        self.x = self.c % 2

    def device(self, link):
        axis, way = link
        if axis == "z":
            return (self.z + way, self.c, self.t)
        if axis == "y":
            return (self.z, 2 * (1 - self.y) + self.x, self.t)
        if axis == "x":
            return (self.z, 2 * self.y + (1 - self.x), self.t)
        return (self.z, self.c, 1 - self.t)

    def piece(self, place):
        k, dy, dx = place
        y = 1 - self.y if dy else self.y
        x = 1 - self.x if dx else self.x
        return (self.z + k) * 4 + 2 * y + x

    def inside(self, way):
        if way == 0:
            return None
        return self.z + way < self.depth if way > 0 else self.z + way >= 0

    def meet(self):
        barrier = pltpu.get_barrier_semaphore()
        for link in (("x", 1), ("y", 1), ("tp", 1)):
            pl.semaphore_signal(barrier, inc=1, device_id=self.device(link), device_id_type=MESH)
        for way in (1, -1):

            @pl.when(self.inside(way))
            def _():
                pl.semaphore_signal(
                    barrier, inc=1, device_id=self.device(("z", way)), device_id_type=MESH
                )

        peers = 3 + (self.z > 0).astype(jnp.int32) + (self.z < self.depth - 1).astype(jnp.int32)
        pl.semaphore_wait(barrier, peers)


def guarded(condition, action):
    if condition is None:
        action()
    else:
        pl.when(condition)(action)


def columns(half, width):
    return pl.ds(pl.multiple_of(half * width, LANES), width)


def block_of(name, ref, piece, half, width):
    if name == "project":
        return ref.at[:, piece, :, columns(half, width)]
    if name == "vectors":
        return ref.at[piece]
    return ref.at[piece, :, columns(half, width)]


def gather_kernel(widths, chip_count, *refs):
    count = len(ITEMS)
    shards = dict(zip(ITEMS, refs[:count]))
    wholes = dict(zip(ITEMS, refs[count : 2 * count]))
    send_sem, recv_sem, side_send, side_recv, own_sem = refs[2 * count :]
    here = Here()
    spots = places(chip_count)
    order = sorted(spots, key=hops)
    slot = {}
    for i, name in enumerate(ITEMS):
        for place in spots:
            for link in links(ROUTES[name], place, chip_count)[1]:
                slot[name, place, link] = len(slot)

    def block(name, place, half):
        return block_of(name, wholes[name], here.piece(place), half, widths[name])

    def send(name, place, link):
        source = shards[name] if place == (0, 0, 0) else block(name, place, here.t)
        return pltpu.make_async_remote_copy(
            src_ref=source,
            dst_ref=block(name, place, here.t),
            send_sem=send_sem.at[slot[name, place, link]],
            recv_sem=recv_sem.at[ITEMS.index(name), spots.index(seen_from(place, link))],
            device_id=here.device(link),
            device_id_type=MESH,
        )

    def side(name, place, half):
        source = shards[name] if place == (0, 0, 0) else block(name, place, half)
        return pltpu.make_async_remote_copy(
            src_ref=source,
            dst_ref=block(name, place, half),
            send_sem=side_send.at[ITEMS.index(name), spots.index(place)],
            recv_sem=side_recv.at[ITEMS.index(name), spots.index(place)],
            device_id=here.device(("tp", 1)),
            device_id_type=MESH,
        )

    def arrival(name, place):
        return pltpu.make_async_remote_copy(
            src_ref=block(name, place, here.t),
            dst_ref=block(name, place, here.t),
            send_sem=send_sem.at[0],
            recv_sem=recv_sem.at[ITEMS.index(name), spots.index(place)],
            device_id=here.device(("tp", 1)),
            device_id_type=MESH,
        )

    here.meet()
    for name in ITEMS:
        pltpu.make_async_copy(
            shards[name], block(name, (0, 0, 0), here.t), own_sem.at[ITEMS.index(name)]
        ).start()
    for place in order:

        def pass_on(place=place):
            for name in ITEMS:
                if place != (0, 0, 0):
                    arrival(name, place).wait_recv()
                for link in links(ROUTES[name], place, chip_count)[1]:
                    guarded(
                        here.inside(link[1]) if link[0] == "z" else None,
                        lambda link=link: send(name, place, link).start(),
                    )
                if name != "vectors":
                    side(name, place, here.t).start()

        guarded(here.inside(place[0]), pass_on)
    for place in order:

        def finish(place=place):
            for name in ITEMS:
                if name != "vectors":
                    side(name, place, 1 - here.t).wait_recv()
                    side(name, place, here.t).wait_send()
                for link in links(ROUTES[name], place, chip_count)[1]:
                    guarded(
                        here.inside(link[1]) if link[0] == "z" else None,
                        lambda link=link: send(name, place, link).wait_send(),
                    )

        guarded(here.inside(place[0]), finish)
    for name in ITEMS:
        pltpu.make_async_copy(
            shards[name], block(name, (0, 0, 0), here.t), own_sem.at[ITEMS.index(name)]
        ).wait()


def link_count(depth):
    return sum(len(links(ROUTES[name], place, depth)[1]) for name in ITEMS for place in places(depth))


def gather_weights(shards):
    chips, pieces = lax.axis_size("shard"), lax.axis_size("shard") * lax.axis_size("ctx")
    widths = {name: shards[name].shape[-1] for name in ITEMS}
    shapes = []
    for name in ITEMS:
        shape = shards[name].shape
        if name == "project":
            shape = (shape[0], pieces, shape[1], 2 * shape[2])
        elif name == "vectors":
            shape = (pieces,) + shape
        else:
            shape = (pieces, shape[0], 2 * shape[1])
        shapes.append(jax.ShapeDtypeStruct(shape, jnp.bfloat16))
    spots = len(places(chips))
    outs = pl.pallas_call(
        lambda *refs: gather_kernel(widths, chips, *refs),
        out_shape=shapes,
        in_specs=[pl.BlockSpec(memory_space=pl.ANY)] * len(ITEMS),
        out_specs=[pl.BlockSpec(memory_space=pl.ANY)] * len(ITEMS),
        scratch_shapes=[
            pltpu.SemaphoreType.DMA((link_count(chips),)),
            pltpu.SemaphoreType.DMA((len(ITEMS), spots)),
            pltpu.SemaphoreType.DMA((len(ITEMS), spots)),
            pltpu.SemaphoreType.DMA((len(ITEMS), spots)),
            pltpu.SemaphoreType.DMA((len(ITEMS),)),
        ],
        compiler_params=pltpu.CompilerParams(collective_id=0, has_side_effects=True),
        name="gather_weights",
    )(*[shards[name] for name in ITEMS])
    return dict(zip(ITEMS, outs))


def add_into(target, addend):
    lead = target.shape[:-2]
    for index in range(math.prod(lead)):
        at = (index,) if lead else ()
        height = 16 if target.shape[-2] % 16 == 0 else 8

        @pl.loop(0, target.shape[-2] // height)
        def _(step):
            rows = pl.ds(pl.multiple_of(step * height, height), height)
            where = at + (rows, slice(None))
            total = target[where].astype(jnp.float32) + addend[where].astype(jnp.float32)
            target[where] = total.astype(target.dtype)


def scatter_kernel(widths, chip_count, *refs):
    count = len(ITEMS)
    grads = dict(zip(ITEMS, refs[:count]))
    outs = dict(zip(ITEMS, refs[count : 2 * count]))
    mine = dict(zip(ITEMS, refs[2 * count : 3 * count]))
    theirs = dict(zip(ITEMS, refs[3 * count : 4 * count]))
    inbox = dict(zip(ITEMS, refs[4 * count : 5 * count]))
    load_sem, side_send, side_recv, send_sem, recv_sem = refs[5 * count :]
    here = Here()
    spots = places(chip_count)
    order = sorted(spots, key=hops, reverse=True)
    slot = {}
    box = {}
    for name in ITEMS:
        local = 0
        for place in spots:
            for link in links(ROUTES[name], place, chip_count)[1]:
                slot[name, place, link] = len(slot)
                box[name, place, link] = local
                local += 1

    def opposite(link):
        return (link[0], -link[1]) if link[0] == "z" else link

    def load(name, place):
        return pltpu.make_async_copy(
            block_of(name, grads[name], here.piece(place), here.t, widths[name]),
            mine[name].at[spots.index(place)],
            load_sem.at[ITEMS.index(name), spots.index(place)],
        )

    def side(name, place):
        return pltpu.make_async_remote_copy(
            src_ref=block_of(name, grads[name], here.piece(place), 1 - here.t, widths[name]),
            dst_ref=theirs[name].at[spots.index(place)],
            send_sem=side_send.at[ITEMS.index(name), spots.index(place)],
            recv_sem=side_recv.at[ITEMS.index(name), spots.index(place)],
            device_id=here.device(("tp", 1)),
            device_id_type=MESH,
        )

    def send(name, place, link):
        there = seen_from(place, link)
        return pltpu.make_async_remote_copy(
            src_ref=mine[name].at[spots.index(place)],
            dst_ref=inbox[name].at[box[name, there, opposite(link)]],
            send_sem=send_sem.at[ITEMS.index(name), spots.index(place)],
            recv_sem=recv_sem.at[slot[name, there, opposite(link)]],
            device_id=here.device(link),
            device_id_type=MESH,
        )

    def arrival(name, place, link):
        return pltpu.make_async_remote_copy(
            src_ref=inbox[name].at[box[name, place, link]],
            dst_ref=inbox[name].at[box[name, place, link]],
            send_sem=send_sem.at[0, 0],
            recv_sem=recv_sem.at[slot[name, place, link]],
            device_id=here.device(link),
            device_id_type=MESH,
        )

    here.meet()
    for place in order:

        def begin(place=place):
            for name in ITEMS:
                side(name, place).start()
                load(name, place).start()

        guarded(here.inside(place[0]), begin)
    for place in order:

        def settle(place=place):
            for name in ITEMS:
                back, onward = links(ROUTES[name], place, chip_count)
                total = mine[name].at[spots.index(place)]
                load(name, place).wait()
                side(name, place).wait_recv()
                add_into(total, theirs[name].at[spots.index(place)])
                for link in onward:

                    def take(link=link):
                        arrival(name, place, link).wait_recv()
                        add_into(total, inbox[name].at[box[name, place, link]])

                    guarded(here.inside(link[1]) if link[0] == "z" else None, take)
                if back is not None:
                    send(name, place, back).start()

        guarded(here.inside(place[0]), settle)
    for name in ITEMS:
        outs[name][...] = mine[name][spots.index((0, 0, 0))].astype(jnp.float32)
    for place in order:

        def finish(place=place):
            for name in ITEMS:
                back, _ = links(ROUTES[name], place, chip_count)
                side(name, place).wait_send()
                if back is not None:
                    send(name, place, back).wait_send()

        guarded(here.inside(place[0]), finish)


def scatter_grads(grads):
    chips = lax.axis_size("shard")
    spots = len(places(chips))
    widths, blocks, boxes = {}, [], []
    for name in ITEMS:
        shape = grads[name].shape
        if name == "project":
            block = (shape[0], shape[2], shape[3] // 2)
        elif name == "vectors":
            block = shape[1:]
        else:
            block = (shape[1], shape[2] // 2)
        widths[name] = block[-1]
        blocks.append(block)
        boxes.append(sum(len(links(ROUTES[name], place, chips)[1]) for place in places(chips)))
    kinds = [grads[name].dtype for name in ITEMS]
    outs = pl.pallas_call(
        lambda *refs: scatter_kernel(widths, chips, *refs),
        out_shape=[jax.ShapeDtypeStruct(block, jnp.float32) for block in blocks],
        in_specs=[pl.BlockSpec(memory_space=pl.ANY)] * len(ITEMS),
        out_specs=[pl.BlockSpec(memory_space=pltpu.VMEM)] * len(ITEMS),
        scratch_shapes=(
            [pltpu.VMEM((spots,) + block, kind) for block, kind in zip(blocks, kinds)]
            + [pltpu.VMEM((spots,) + block, kind) for block, kind in zip(blocks, kinds)]
            + [pltpu.VMEM((box,) + block, kind) for box, block, kind in zip(boxes, blocks, kinds)]
            + [
                pltpu.SemaphoreType.DMA((len(ITEMS), spots)),
                pltpu.SemaphoreType.DMA((len(ITEMS), spots)),
                pltpu.SemaphoreType.DMA((len(ITEMS), spots)),
                pltpu.SemaphoreType.DMA((len(ITEMS), spots)),
                pltpu.SemaphoreType.DMA((link_count(chips),)),
            ]
        ),
        compiler_params=pltpu.CompilerParams(
            collective_id=1, has_side_effects=True, vmem_limit_bytes=60 << 20
        ),
        name="scatter_grads",
    )(*[grads[name] for name in ITEMS])
    return dict(zip(ITEMS, outs))


def fitting(shards):
    return lax.axis_size("ctx") == 4 and lax.axis_size("tp") == 2 and shards["up"].shape[0] % 16 == 0


def gather_plain(shards):
    wholes = {}
    for name in ITEMS:
        axis = 1 if name == "project" else 0
        part = lax.all_gather(shards[name], ROWS, axis=axis)
        if name != "vectors":
            part = lax.all_gather(part, "tp", axis=axis + 2, tiled=True)
        wholes[name] = part
    return wholes


def scatter_plain(grads):
    shards = {}
    for name in ITEMS:
        axis = 1 if name == "project" else 0
        part = grads[name]
        if name == "vectors":
            part = lax.psum(part, "tp")
        else:
            part = lax.psum_scatter(part, "tp", scatter_dimension=axis + 2, tiled=True)
        part = lax.psum_scatter(part, ROWS, scatter_dimension=axis, tiled=False)
        shards[name] = part.astype(jnp.float32)
    return shards


def local(
    tokens, project_weight, attend_weight, up_weight, down_weight, project_bias, attend_bias,
    up_bias, down_bias, first_gain, first_shift, second_gain, second_shift, segment_ids, padding,
    cotangent,
):
    seq_count = tokens.shape[0]
    members = lax.axis_size("ctx") * lax.axis_size("tp")
    own = seq_count // members
    rank = lax.axis_index("ctx") * lax.axis_size("tp") + lax.axis_index("tp")
    rows = own * S
    pieces = lax.axis_size("shard") * lax.axis_size("ctx")
    depth = D // pieces

    def to_sequences(array):
        parts = array.reshape((members, own) + array.shape[1:])
        parts = lax.all_to_all(parts, SEQ, 0, 0, tiled=True)
        return jnp.swapaxes(parts, 0, 1).reshape(own, S, D)

    def to_blocks(array):
        parts = jnp.swapaxes(array.reshape(own, members, S // members, D), 0, 1)
        return lax.all_to_all(parts, SEQ, 0, 0, tiled=True).reshape(tokens.shape)

    x = to_sequences(tokens)
    segments = lax.dynamic_slice_in_dim(segment_ids, rank * own, own, 0)
    pads = lax.dynamic_slice_in_dim(padding, rank * own, own, 0)

    vectors = jnp.concatenate(
        [
            project_bias,
            attend_bias[None],
            down_bias[None],
            first_gain[None],
            first_shift[None],
            second_gain[None],
            second_shift[None],
            up_bias.reshape(FF // D, depth),
        ],
        axis=0,
    )
    shards = {
        "project": jnp.transpose(project_weight, (1, 0, 2)),
        "up": up_weight,
        "down": jnp.transpose(down_weight),
        "attend": jnp.transpose(attend_weight),
        "vectors": jnp.pad(vectors, ((0, 3), (0, LANES - depth))),
    }
    custom = fitting(shards)
    wholes = gather_weights(shards) if custom else gather_plain(shards)
    project = wholes["project"].reshape(3, D, D)
    up = wholes["up"].reshape(D, FF)
    down_t = wholes["down"].reshape(D, FF)
    attend_t = wholes["attend"].reshape(D, D)
    vectors = wholes["vectors"][:, :13, :depth].astype(jnp.float32)
    wide = jnp.transpose(vectors[:, :9], (1, 0, 2)).reshape(9, D)
    up_shift = vectors[:, 9:].reshape(FF)

    tables = mask_tables(segments, pads)
    cosine, sine = angles()
    query, key, value, attended, level = attend(
        tables[0], tables[1], x, project, wide[:3], cosine, sine, *tables[2:]
    )
    incoming = to_sequences(cotangent)
    parts = [
        feed_forward(attended[i], x[i], incoming[i], attend_t, up, down_t, wide, up_shift)
        for i in range(own)
    ]
    attended_grad = jnp.stack([part[0] for part in parts])
    branch_grad = jnp.concatenate([part[1] for part in parts])
    sums = sum(part[2] for part in parts)
    up_bias_grad = sum(part[3] for part in parts)
    output = to_blocks(jnp.stack([part[4] for part in parts]))
    up_grad, down_grad, attend_grad = (
        parts[0][k] if own == 1 else sum(part[k].astype(jnp.float32) for part in parts).astype(jnp.bfloat16)
        for k in (5, 6, 7)
    )
    flat = x.reshape(rows, D)

    joint_grad = attend_back(
        tables[0], tables[1], query, key, value, attended, attended_grad, level,
        cosine, sine, *tables[2:],
    ).reshape(rows, 3 * D)
    project_bias_grad = jnp.sum(joint_grad.astype(jnp.float32), axis=0).reshape(3, D)
    project_grad = jnp.stack(
        [dot(flat, joint_grad[:, i * D : (i + 1) * D], TN) for i in range(3)]
    )
    token_part = sum(
        dot(joint_grad[:, i * D : (i + 1) * D], project[i], NT) for i in range(3)
    )
    tokens_grad = to_blocks((branch_grad.astype(jnp.float32) + token_part).astype(jnp.bfloat16).reshape(own, S, D))

    sums = jnp.concatenate([project_bias_grad, sums], axis=0)
    sums = jnp.concatenate(
        [
            jnp.transpose(sums.reshape(9, pieces, depth), (1, 0, 2)),
            up_bias_grad.reshape(pieces, FF // D, depth),
        ],
        axis=1,
    )
    grads = {
        "project": project_grad.astype(jnp.bfloat16).reshape(3, pieces, depth, D),
        "up": up_grad.reshape(pieces, depth, FF),
        "down": down_grad.reshape(pieces, depth, FF),
        "attend": attend_grad.reshape(pieces, depth, D),
        "vectors": jnp.pad(sums, ((0, 0), (0, 3), (0, LANES - depth))),
    }
    shards = scatter_grads(grads) if custom else scatter_plain(grads)
    sums = shards["vectors"][:13, :depth]
    return (
        output,
        tokens_grad,
        jnp.transpose(shards["project"], (1, 0, 2)),
        jnp.transpose(shards["attend"]),
        shards["up"],
        jnp.transpose(shards["down"]),
        sums[:3],
        sums[3],
        sums[9:].reshape(-1),
        sums[4],
        sums[5],
        sums[6],
        sums[7],
        sums[8],
    )


def solution(mesh):
    in_specs = (
        P("shard", ("ctx", "tp"), None),
        P(("shard", "ctx"), None, "tp"),
        P("tp", ("shard", "ctx")),
        P(("shard", "ctx"), "tp"),
        P("tp", ("shard", "ctx")),
        P(None, ("shard", "ctx")),
        P(("shard", "ctx")),
        P(("shard", "ctx")),
        P(("shard", "ctx")),
        P(("shard", "ctx")),
        P(("shard", "ctx")),
        P(("shard", "ctx")),
        P(("shard", "ctx")),
        P("shard", None),
        P("shard", None),
        P("shard", ("ctx", "tp"), None),
    )
    out_specs = (
        P("shard", ("ctx", "tp"), None),
        P("shard", ("ctx", "tp"), None),
        P(("shard", "ctx"), None, "tp"),
        P("tp", ("shard", "ctx")),
        P(("shard", "ctx"), "tp"),
        P("tp", ("shard", "ctx")),
        P(None, ("shard", "ctx")),
        P(("shard", "ctx")),
        P(("shard", "ctx")),
        P(("shard", "ctx")),
        P(("shard", "ctx")),
        P(("shard", "ctx")),
        P(("shard", "ctx")),
        P(("shard", "ctx")),
    )
    return jax.shard_map(local, mesh=mesh, in_specs=in_specs, out_specs=out_specs, check_vma=False)
```

```python
import functools
import math

import jax
import jax.numpy as jnp
from jax import lax
from jax.experimental import pallas as pl
from jax.experimental.pallas import tpu as pltpu
from jax.sharding import PartitionSpec as P

D = 768
HEADS = 12
HEAD_DIM = 64
FF = 3072
S = 1024
LANES = 128
PAIRS = HEADS // 2
Q_ROWS = 128
K_ROWS = 256

norm_eps = 1e-12
mask_fill = -1000000000.0

NT = (((1,), (1,)), ((), ()))
TN = (((0,), (0,)), ((), ()))
NN = (((1,), (0,)), ((), ()))


def dot(left, right, dims):
    return lax.dot_general(left, right, dims, preferred_element_type=jnp.float32)


def swap_pairs(values):
    lane = lax.broadcasted_iota(jnp.int32, values.shape, 1)
    width = values.shape[1]
    return jnp.where(
        lane % 2 == 0, -pltpu.roll(values, width - 1, 1), pltpu.roll(values, 1, 1)
    )


def stack_heads(rows):
    lane = lax.broadcasted_iota(jnp.int32, rows.shape, 1)
    zero = jnp.zeros_like(rows)
    return jnp.concatenate(
        [jnp.where(lane < HEAD_DIM, rows, zero), jnp.where(lane < HEAD_DIM, zero, rows)], axis=0
    )


def pick_heads(both):
    return jnp.concatenate([both[:HEAD_DIM, :Q_ROWS], both[HEAD_DIM:, Q_ROWS:]], axis=0)


def spread_heads(row):
    return jnp.concatenate(
        [
            jnp.broadcast_to(row[:, :Q_ROWS], (HEAD_DIM, Q_ROWS)),
            jnp.broadcast_to(row[:, Q_ROWS:], (HEAD_DIM, Q_ROWS)),
        ],
        axis=0,
    )


def mask_bias(key_code, query_low, query_high):
    keys = jnp.broadcast_to(key_code, (K_ROWS, Q_ROWS))
    allowed = (keys >= query_low) & (keys <= query_high)
    bias = jnp.where(allowed, 0.0, mask_fill)
    return jnp.concatenate([bias, bias], axis=1)


def attend_kernel(
    first_ref, count_ref, x_ref, w_ref, b_ref, cos_ref, sin_ref, code_ref, low_ref, high_ref,
    q_ref, k_ref, v_ref, o_ref, lse_ref, top, total, acc, stacked,
):
    own = pl.program_id(0)
    row_tile = 256

    @pl.loop(0, S // row_tile)
    def _(tile):
        rows = pl.ds(pl.multiple_of(tile * row_tile, row_tile), row_tile)
        x = x_ref[rows, :]
        cosine = cos_ref[rows, :]
        sine = sin_ref[rows, :]
        for part, out in enumerate((q_ref, k_ref, v_ref)):
            joint = dot(x, w_ref[part], NN) + b_ref[pl.ds(part, 1), :]
            for pair in range(PAIRS):
                lanes = slice(pair * LANES, (pair + 1) * LANES)
                piece = joint[:, lanes]
                if part < 2:
                    piece = piece * cosine + swap_pairs(piece) * sine
                if part == 0:
                    piece = piece.astype(jnp.bfloat16) * jnp.asarray(HEAD_DIM**-0.5, jnp.bfloat16)
                out[rows, lanes] = piece.astype(jnp.bfloat16)

    @pl.loop(0, S // Q_ROWS)
    def _(block):
        start = pl.multiple_of(block * Q_ROWS, Q_ROWS)
        rows = pl.ds(start, Q_ROWS)
        for pair in range(PAIRS):
            stacked[pair] = stack_heads(q_ref[rows, pair * LANES : (pair + 1) * LANES])
        top[...] = jnp.full_like(top, 2.0 * mask_fill)
        total[...] = jnp.zeros_like(total)
        acc[...] = jnp.zeros_like(acc)
        low = low_ref[:, rows]
        high = high_ref[:, rows]

        @pl.loop(0, count_ref[own, block])
        def _(step):
            window = pl.ds(pl.multiple_of(first_ref[own, block] + step * K_ROWS, 16), K_ROWS)
            bias = mask_bias(code_ref[window, :], low, high)
            for pair in range(PAIRS):
                lanes = slice(pair * LANES, (pair + 1) * LANES)
                scores = dot(k_ref[window, lanes], stacked[pair], NT) + bias
                old = top[pair]
                new = jnp.maximum(old, jnp.max(scores, axis=0, keepdims=True))
                expo = jnp.exp(scores - new)
                fade = jnp.exp(old - new)
                top[pair] = new
                total[pair] = total[pair] * fade + jnp.sum(expo, axis=0, keepdims=True)
                mixed = dot(v_ref[window, lanes], expo.astype(jnp.bfloat16), TN)
                acc[pair] = acc[pair] * spread_heads(fade) + pick_heads(mixed)

        for pair in range(PAIRS):
            lanes = slice(pair * LANES, (pair + 1) * LANES)
            summed = total[pair]
            out = acc[pair] / spread_heads(summed)
            o_ref[rows, lanes] = jnp.transpose(out).astype(jnp.bfloat16)
            lse = top[pair] + jnp.log(summed)
            lse_ref[pl.ds(2 * pair, 1), rows] = lse[:, :Q_ROWS]
            lse_ref[pl.ds(2 * pair + 1, 1), rows] = lse[:, Q_ROWS:]


def attend_back_kernel(
    first_ref, count_ref, q_ref, k_ref, v_ref, o_ref, g_ref, lse_ref, cos_ref, sin_ref, code_ref,
    low_ref, high_ref, x_hbm, branch_hbm, w_hbm, token_ref, weight_ref, sums_ref,
    joint_ref, acc, keys, values, stacked, grads, delta, level, x_ref, branch_ref, w_ref, turned, sums, sem,
):
    own = pl.program_id(0)
    loads = [
        pltpu.make_async_copy(source, target, sem.at[i])
        for i, (source, target) in enumerate(
            ((x_hbm.at[own], x_ref), (branch_hbm.at[own], branch_ref), (w_hbm, w_ref))
        )
    ]
    for load in loads:
        load.start()
    sums[...] = jnp.zeros_like(sums)

    def keep(rows, lanes, grad):
        low = grad.astype(jnp.bfloat16)
        joint_ref[rows, lanes] = low
        sums[:, lanes] += jnp.sum(low.astype(jnp.float32).reshape(Q_ROWS // 8, 8, LANES), axis=0)

    keys[...] = jnp.zeros_like(keys)
    values[...] = jnp.zeros_like(values)

    @pl.loop(0, S // Q_ROWS)
    def _(block):
        start = pl.multiple_of(block * Q_ROWS, Q_ROWS)
        rows = pl.ds(start, Q_ROWS)
        for pair in range(PAIRS):
            lanes = slice(pair * LANES, (pair + 1) * LANES)
            stacked[pair] = stack_heads(q_ref[rows, lanes])
            grad = g_ref[rows, lanes]
            grads[pair] = stack_heads(grad)
            both = jnp.transpose(grad.astype(jnp.float32) * o_ref[rows, lanes].astype(jnp.float32))
            delta[pair] = jnp.concatenate(
                [
                    jnp.sum(both[:HEAD_DIM], axis=0, keepdims=True),
                    jnp.sum(both[HEAD_DIM:], axis=0, keepdims=True),
                ],
                axis=1,
            )
            level[pair] = jnp.concatenate(
                [lse_ref[pl.ds(2 * pair, 1), rows], lse_ref[pl.ds(2 * pair + 1, 1), rows]], axis=1
            )
        acc[...] = jnp.zeros_like(acc)
        low = low_ref[:, rows]
        high = high_ref[:, rows]

        @pl.loop(0, count_ref[own, block])
        def _(step):
            window = pl.ds(pl.multiple_of(first_ref[own, block] + step * K_ROWS, 16), K_ROWS)
            bias = mask_bias(code_ref[window, :], low, high)
            for pair in range(PAIRS):
                lanes = slice(pair * LANES, (pair + 1) * LANES)
                query = stacked[pair]
                grad = grads[pair]
                key = k_ref[window, lanes]
                scores = dot(key, query, NT) + bias
                probs = jnp.exp(scores - level[pair])
                prob_grad = dot(v_ref[window, lanes], grad, NT)
                score_grad = (probs * (prob_grad - delta[pair])).astype(jnp.bfloat16)
                values[window, lanes] += dot(probs.astype(jnp.bfloat16), grad, NN)
                keys[window, lanes] += dot(score_grad, query, NN)
                acc[pair] += pick_heads(dot(key, score_grad, TN))

        cosine = cos_ref[rows, :]
        sine = sin_ref[rows, :]
        for pair in range(PAIRS):
            lanes = slice(pair * LANES, (pair + 1) * LANES)
            query = jnp.transpose(acc[pair]) * (HEAD_DIM**-0.5)
            keep(rows, lanes, query * cosine - swap_pairs(query) * sine)

    @pl.loop(0, S // Q_ROWS)
    def _(block):
        rows = pl.ds(pl.multiple_of(block * Q_ROWS, Q_ROWS), Q_ROWS)
        cosine = cos_ref[rows, :]
        sine = sin_ref[rows, :]
        for pair in range(PAIRS):
            lanes = slice(pair * LANES, (pair + 1) * LANES)
            key = keys[rows, lanes]
            keep(
                rows,
                slice(D + pair * LANES, D + (pair + 1) * LANES),
                key * cosine - swap_pairs(key) * sine,
            )
            keep(rows, slice(2 * D + pair * LANES, 2 * D + (pair + 1) * LANES), values[rows, lanes])

    for load in loads:
        load.wait()
    turned[...] = jnp.transpose(x_ref[...])
    for part in range(3):
        columns = slice(part * D, (part + 1) * D)
        weight_ref[part] = dot(turned[...], joint_ref[:, columns], NN).astype(jnp.bfloat16)
        sums_ref[pl.ds(part, 1), :] = jnp.sum(sums[:, columns], axis=0, keepdims=True)

    @pl.loop(0, 2)
    def _(half):
        rows = pl.ds(pl.multiple_of(half * (S // 2), S // 2), S // 2)
        total = branch_ref[rows, :].astype(jnp.float32)
        for part in range(3):
            total += dot(joint_ref[rows, part * D : (part + 1) * D], w_ref[part], NT)
        token_ref[rows, :] = total.astype(jnp.bfloat16)


def whole(*shape):
    return pl.BlockSpec(shape, lambda i, *_: (0,) * len(shape))


def per(*shape):
    return pl.BlockSpec((None,) + shape, lambda i, *_: (i,) + (0,) * len(shape))


def attend(first, count, x, weight, bias, cosine, sine, code, low, high):
    own = x.shape[0]
    act = jax.ShapeDtypeStruct((own, S, D), jnp.bfloat16)
    return pl.pallas_call(
        attend_kernel,
        grid_spec=pltpu.PrefetchScalarGridSpec(
            num_scalar_prefetch=2,
            grid=(own,),
            in_specs=[
                per(S, D), whole(3, D, D), whole(3, D), whole(S, LANES), whole(S, LANES),
                per(S, 1), per(1, S), per(1, S),
            ],
            out_specs=[per(S, D), per(S, D), per(S, D), per(S, D), per(HEADS, S)],
            scratch_shapes=[
                pltpu.VMEM((PAIRS, 1, 2 * Q_ROWS), jnp.float32),
                pltpu.VMEM((PAIRS, 1, 2 * Q_ROWS), jnp.float32),
                pltpu.VMEM((PAIRS, LANES, Q_ROWS), jnp.float32),
                pltpu.VMEM((PAIRS, 2 * Q_ROWS, LANES), jnp.bfloat16),
            ],
        ),
        out_shape=[act, act, act, act, jax.ShapeDtypeStruct((own, HEADS, S), jnp.float32)],
        compiler_params=pltpu.CompilerParams(vmem_limit_bytes=60 << 20),
        name="attend",
        cost_estimate=pl.CostEstimate(flops=6 * 10**9, bytes_accessed=12 << 20, transcendentals=6 << 20),
    )(first, count, x, weight, bias, cosine, sine, code, low, high)


def attend_back(
    first, count, q, k, v, o, g, lse, cosine, sine, code, low, high, x, branch_grad, weight
):
    own = q.shape[0]
    hbm = pl.BlockSpec(memory_space=pl.ANY)
    return pl.pallas_call(
        attend_back_kernel,
        grid_spec=pltpu.PrefetchScalarGridSpec(
            num_scalar_prefetch=2,
            grid=(own,),
            in_specs=[
                per(S, D), per(S, D), per(S, D), per(S, D), per(S, D), per(HEADS, S),
                whole(S, LANES), whole(S, LANES), per(S, 1), per(1, S), per(1, S), hbm, hbm, hbm,
            ],
            out_specs=[per(S, D), per(3, D, D), per(3, D)],
            scratch_shapes=[
                pltpu.VMEM((S, 3 * D), jnp.bfloat16),
                pltpu.VMEM((PAIRS, LANES, Q_ROWS), jnp.float32),
                pltpu.VMEM((S, D), jnp.float32),
                pltpu.VMEM((S, D), jnp.float32),
                pltpu.VMEM((PAIRS, 2 * Q_ROWS, LANES), jnp.bfloat16),
                pltpu.VMEM((PAIRS, 2 * Q_ROWS, LANES), jnp.bfloat16),
                pltpu.VMEM((PAIRS, 1, 2 * Q_ROWS), jnp.float32),
                pltpu.VMEM((PAIRS, 1, 2 * Q_ROWS), jnp.float32),
                pltpu.VMEM((S, D), jnp.bfloat16),
                pltpu.VMEM((S, D), jnp.bfloat16),
                pltpu.VMEM((3, D, D), jnp.bfloat16),
                pltpu.VMEM((D, S), jnp.bfloat16),
                pltpu.VMEM((8, 3 * D), jnp.float32),
                pltpu.SemaphoreType.DMA((3,)),
            ],
        ),
        out_shape=[
            jax.ShapeDtypeStruct((own, S, D), jnp.bfloat16),
            jax.ShapeDtypeStruct((own, 3, D, D), jnp.bfloat16),
            jax.ShapeDtypeStruct((own, 3, D), jnp.float32),
        ],
        compiler_params=pltpu.CompilerParams(vmem_limit_bytes=60 << 20),
        name="attend_back",
        cost_estimate=pl.CostEstimate(flops=19 * 10**9, bytes_accessed=24 << 20, transcendentals=6 << 20),
    )(first, count, q, k, v, o, g, lse, cosine, sine, code, low, high, x, branch_grad, weight)


def mask_tables(segments, padding):
    code = 2 * segments + padding
    low = code
    high = 2 * segments + 1
    blocks = segments.reshape(segments.shape[0], S // Q_ROWS, Q_ROWS)
    begin = jnp.sum(segments[:, None, :] < blocks[:, :, :1], axis=-1, dtype=jnp.int32)
    end = jnp.sum(segments[:, None, :] <= blocks[:, :, -1:], axis=-1, dtype=jnp.int32)
    begin = begin // 16 * 16
    count = (end - begin + K_ROWS - 1) // K_ROWS
    first = jnp.minimum(begin, S - count * K_ROWS)
    return first, count, code[:, :, None], low[:, None, :], high[:, None, :]


def angles():
    position = jnp.arange(S, dtype=jnp.int32).astype(jnp.float32)
    column = jnp.arange(LANES, dtype=jnp.int32) % HEAD_DIM // 2
    rate = jnp.exp(column.astype(jnp.float32) * (-2.0 * math.log(10000.0) / HEAD_DIM))
    phase = position[:, None] * rate[None, :]
    return jnp.cos(phase), jnp.sin(phase)


MESH = pl.DeviceIdType.MESH
ROWS = ("shard", "ctx")
EVERY = ("shard", "ctx", "tp")
SEQ = ("ctx", "tp")

ROUTES = {"up": "zyx", "attend": "yxz", "down": "zxy", "project": "xyz", "vectors": "xyz"}
ITEMS = ("project", "up", "down", "attend", "vectors")


def places(depth):
    steps = [0]
    for k in range(1, depth):
        steps += [k, -k]
    return [(k, dy, dx) for k in steps for dy in (0, 1) for dx in (0, 1)]


def hops(place):
    return abs(place[0]) + place[1] + place[2]


def links(route, place, depth):
    apart = {"z": place[0] != 0, "y": place[1], "x": place[2]}
    level = max([i for i, axis in enumerate(route) if apart[axis]], default=-1)
    sign = (place[0] > 0) - (place[0] < 0)
    onward = []
    if level >= 0 and route[level] == "z" and abs(place[0]) + 1 < depth:
        onward.append(("z", -sign))
    for axis in route[level + 1 :]:
        onward += [("z", 1), ("z", -1)] if axis == "z" else [(axis, 1)]
    back = None if level < 0 else (route[level], sign if route[level] == "z" else 1)
    return back, onward


def seen_from(place, link):
    k, dy, dx = place
    axis, way = link
    return {"z": (k - way, dy, dx), "y": (k, 1 - dy, dx), "x": (k, dy, 1 - dx)}[axis]


class Here:
    def __init__(self):
        self.depth = lax.axis_size("shard")
        self.z = lax.axis_index("shard")
        self.c = lax.axis_index("ctx")
        self.t = lax.axis_index("tp")
        self.y = self.c // 2
        self.x = self.c % 2
        self.sides = lax.axis_size("tp")
        self.members = lax.axis_size("ctx") * self.sides
        self.rank = self.c * self.sides + self.t

    def rank_of(self, offset):
        return (self.rank + offset) % self.members

    def member(self, offset):
        rank = self.rank_of(offset)
        return (self.z, rank // self.sides, rank % self.sides)

    def device(self, link):
        axis, way = link
        if axis == "z":
            return (self.z + way, self.c, self.t)
        if axis == "y":
            return (self.z, 2 * (1 - self.y) + self.x, self.t)
        if axis == "x":
            return (self.z, 2 * self.y + (1 - self.x), self.t)
        return (self.z, self.c, 1 - self.t)

    def piece(self, place):
        k, dy, dx = place
        y = 1 - self.y if dy else self.y
        x = 1 - self.x if dx else self.x
        return (self.z + k) * 4 + 2 * y + x

    def inside(self, way):
        if way == 0:
            return None
        return self.z + way < self.depth if way > 0 else self.z + way >= 0

    def meet(self):
        barrier = pltpu.get_barrier_semaphore()
        for offset in range(1, self.members):
            pl.semaphore_signal(
                barrier, inc=1, device_id=self.member(offset), device_id_type=MESH
            )
        for way in (1, -1):

            @pl.when(self.inside(way))
            def _():
                pl.semaphore_signal(
                    barrier, inc=1, device_id=self.device(("z", way)), device_id_type=MESH
                )

        above = (self.z < self.depth - 1).astype(jnp.int32)
        below = (self.z > 0).astype(jnp.int32)
        pl.semaphore_wait(barrier, self.members - 1 + above + below)


class Exchange:
    def __init__(self, here, source, target, send_sem, recv_sem, own_sem):
        self.here, self.source, self.target = here, source, target
        self.send_sem, self.recv_sem, self.own_sem = send_sem, recv_sem, own_sem

    def block(self, ref, index):
        return ref.at[index] if len(ref.shape) == 3 else ref.at[rows_of(index)]

    def copy(self, offset):
        here = self.here
        return pltpu.make_async_remote_copy(
            src_ref=self.block(self.source, here.rank_of(offset)),
            dst_ref=self.block(self.target, here.rank),
            send_sem=self.send_sem.at[offset],
            recv_sem=self.recv_sem.at[offset],
            device_id=here.member(offset),
            device_id_type=MESH,
        )

    def arrival(self, offset):
        here = self.here
        landed = self.block(self.target, here.rank_of(here.members - offset))
        return pltpu.make_async_remote_copy(
            src_ref=landed,
            dst_ref=landed,
            send_sem=self.send_sem.at[offset],
            recv_sem=self.recv_sem.at[offset],
            device_id=here.member(offset),
            device_id_type=MESH,
        )

    def own(self):
        rank = self.here.rank
        return pltpu.make_async_copy(
            self.block(self.source, rank), self.block(self.target, rank), self.own_sem
        )

    def start(self):
        for offset in range(1, self.here.members):
            self.copy(offset).start()
        self.own().start()

    def receive(self):
        for offset in range(1, self.here.members):
            self.arrival(offset).wait_recv()
        self.own().wait()

    def drain(self):
        for offset in range(1, self.here.members):
            self.copy(offset).wait_send()


def rows_of(index):
    return pl.ds(pl.multiple_of(index * Q_ROWS, Q_ROWS), Q_ROWS)


def exchange_scratch(members):
    return [
        pltpu.SemaphoreType.DMA((members,)),
        pltpu.SemaphoreType.DMA((members,)),
        pltpu.SemaphoreType.DMA,
    ]


def guarded(condition, action):
    if condition is None:
        action()
    else:
        pl.when(condition)(action)


def columns(half, width):
    return pl.ds(pl.multiple_of(half * width, LANES), width)


def block_of(name, ref, piece, half, width):
    if name == "project":
        return ref.at[:, piece, :, columns(half, width)]
    if name == "vectors":
        return ref.at[piece]
    return ref.at[piece, :, columns(half, width)]


def gather_kernel(widths, chip_count, *refs):
    count = len(ITEMS)
    shards = dict(zip(ITEMS, refs[:count]))
    wholes = dict(zip(ITEMS, refs[count + 1 : 2 * count + 1]))
    send_sem, recv_sem, side_send, side_recv, own_sem = refs[2 * count + 2 : 2 * count + 7]
    here = Here()
    tokens = Exchange(here, refs[count], refs[2 * count + 1], *refs[2 * count + 7 :])
    spots = places(chip_count)
    order = sorted(spots, key=hops)
    slot = {}
    for i, name in enumerate(ITEMS):
        for place in spots:
            for link in links(ROUTES[name], place, chip_count)[1]:
                slot[name, place, link] = len(slot)

    def block(name, place, half):
        return block_of(name, wholes[name], here.piece(place), half, widths[name])

    def send(name, place, link):
        source = shards[name] if place == (0, 0, 0) else block(name, place, here.t)
        return pltpu.make_async_remote_copy(
            src_ref=source,
            dst_ref=block(name, place, here.t),
            send_sem=send_sem.at[slot[name, place, link]],
            recv_sem=recv_sem.at[ITEMS.index(name), spots.index(seen_from(place, link))],
            device_id=here.device(link),
            device_id_type=MESH,
        )

    def side(name, place, half):
        source = shards[name] if place == (0, 0, 0) else block(name, place, half)
        return pltpu.make_async_remote_copy(
            src_ref=source,
            dst_ref=block(name, place, half),
            send_sem=side_send.at[ITEMS.index(name), spots.index(place)],
            recv_sem=side_recv.at[ITEMS.index(name), spots.index(place)],
            device_id=here.device(("tp", 1)),
            device_id_type=MESH,
        )

    def arrival(name, place):
        return pltpu.make_async_remote_copy(
            src_ref=block(name, place, here.t),
            dst_ref=block(name, place, here.t),
            send_sem=send_sem.at[0],
            recv_sem=recv_sem.at[ITEMS.index(name), spots.index(place)],
            device_id=here.device(("tp", 1)),
            device_id_type=MESH,
        )

    here.meet()
    tokens.start()
    for name in ITEMS:
        pltpu.make_async_copy(
            shards[name], block(name, (0, 0, 0), here.t), own_sem.at[ITEMS.index(name)]
        ).start()
    for place in order:

        def pass_on(place=place):
            for name in ITEMS:
                if place != (0, 0, 0):
                    arrival(name, place).wait_recv()
                for link in links(ROUTES[name], place, chip_count)[1]:
                    guarded(
                        here.inside(link[1]) if link[0] == "z" else None,
                        lambda link=link: send(name, place, link).start(),
                    )
                if name != "vectors":
                    side(name, place, here.t).start()

        guarded(here.inside(place[0]), pass_on)
    tokens.receive()
    tokens.drain()
    for place in order:

        def finish(place=place):
            for name in ITEMS:
                if name != "vectors":
                    side(name, place, 1 - here.t).wait_recv()
                    side(name, place, here.t).wait_send()
                for link in links(ROUTES[name], place, chip_count)[1]:
                    guarded(
                        here.inside(link[1]) if link[0] == "z" else None,
                        lambda link=link: send(name, place, link).wait_send(),
                    )

        guarded(here.inside(place[0]), finish)
    for name in ITEMS:
        pltpu.make_async_copy(
            shards[name], block(name, (0, 0, 0), here.t), own_sem.at[ITEMS.index(name)]
        ).wait()


def link_count(depth):
    return sum(len(links(ROUTES[name], place, depth)[1]) for name in ITEMS for place in places(depth))


def gather_weights(shards, tokens):
    chips, pieces = lax.axis_size("shard"), lax.axis_size("shard") * lax.axis_size("ctx")
    widths = {name: shards[name].shape[-1] for name in ITEMS}
    shapes = []
    for name in ITEMS:
        shape = shards[name].shape
        if name == "project":
            shape = (shape[0], pieces, shape[1], 2 * shape[2])
        elif name == "vectors":
            shape = (pieces,) + shape
        else:
            shape = (pieces, shape[0], 2 * shape[1])
        shapes.append(jax.ShapeDtypeStruct(shape, jnp.bfloat16))
    spots = len(places(chips))
    shapes.append(jax.ShapeDtypeStruct(tokens.shape, tokens.dtype))
    outs = pl.pallas_call(
        lambda *refs: gather_kernel(widths, chips, *refs),
        out_shape=shapes,
        in_specs=[pl.BlockSpec(memory_space=pl.ANY)] * (len(ITEMS) + 1),
        out_specs=[pl.BlockSpec(memory_space=pl.ANY)] * (len(ITEMS) + 1),
        scratch_shapes=[
            pltpu.SemaphoreType.DMA((link_count(chips),)),
            pltpu.SemaphoreType.DMA((len(ITEMS), spots)),
            pltpu.SemaphoreType.DMA((len(ITEMS), spots)),
            pltpu.SemaphoreType.DMA((len(ITEMS), spots)),
            pltpu.SemaphoreType.DMA((len(ITEMS),)),
        ]
        + exchange_scratch(tokens.shape[0]),
        compiler_params=pltpu.CompilerParams(collective_id=0, has_side_effects=True),
        name="gather_weights",
    )(*[shards[name] for name in ITEMS], tokens)
    return dict(zip(ITEMS, outs)), outs[-1]


def add_into(target, addend):
    lead = target.shape[:-2]
    for index in range(math.prod(lead)):
        at = (index,) if lead else ()
        height = 16 if target.shape[-2] % 16 == 0 else 8

        @pl.loop(0, target.shape[-2] // height)
        def _(step):
            rows = pl.ds(pl.multiple_of(step * height, height), height)
            where = at + (rows, slice(None))
            total = target[where].astype(jnp.float32) + addend[where].astype(jnp.float32)
            target[where] = total.astype(target.dtype)


def scatter_kernel(widths, chip_count, *refs):
    count = len(ITEMS)
    grads = dict(zip(ITEMS, refs[:count]))
    outs = dict(zip(ITEMS, refs[count + 1 : 2 * count + 1]))
    rest = refs[2 * count + 2 :]
    mine = dict(zip(ITEMS, rest[:count]))
    theirs = dict(zip(ITEMS, rest[count : 2 * count]))
    inbox = dict(zip(ITEMS, rest[2 * count : 3 * count]))
    load_sem, side_send, side_recv, send_sem, recv_sem = rest[3 * count : 3 * count + 5]
    here = Here()
    tokens = Exchange(here, refs[count], refs[2 * count + 1], *rest[3 * count + 5 :])
    spots = places(chip_count)
    order = sorted(spots, key=hops, reverse=True)
    slot = {}
    box = {}
    for name in ITEMS:
        local = 0
        for place in spots:
            for link in links(ROUTES[name], place, chip_count)[1]:
                slot[name, place, link] = len(slot)
                box[name, place, link] = local
                local += 1

    def opposite(link):
        return (link[0], -link[1]) if link[0] == "z" else link

    def load(name, place):
        return pltpu.make_async_copy(
            block_of(name, grads[name], here.piece(place), here.t, widths[name]),
            mine[name].at[spots.index(place)],
            load_sem.at[ITEMS.index(name), spots.index(place)],
        )

    def side(name, place):
        return pltpu.make_async_remote_copy(
            src_ref=block_of(name, grads[name], here.piece(place), 1 - here.t, widths[name]),
            dst_ref=theirs[name].at[spots.index(place)],
            send_sem=side_send.at[ITEMS.index(name), spots.index(place)],
            recv_sem=side_recv.at[ITEMS.index(name), spots.index(place)],
            device_id=here.device(("tp", 1)),
            device_id_type=MESH,
        )

    def send(name, place, link):
        there = seen_from(place, link)
        return pltpu.make_async_remote_copy(
            src_ref=mine[name].at[spots.index(place)],
            dst_ref=inbox[name].at[box[name, there, opposite(link)]],
            send_sem=send_sem.at[ITEMS.index(name), spots.index(place)],
            recv_sem=recv_sem.at[slot[name, there, opposite(link)]],
            device_id=here.device(link),
            device_id_type=MESH,
        )

    def arrival(name, place, link):
        return pltpu.make_async_remote_copy(
            src_ref=inbox[name].at[box[name, place, link]],
            dst_ref=inbox[name].at[box[name, place, link]],
            send_sem=send_sem.at[0, 0],
            recv_sem=recv_sem.at[slot[name, place, link]],
            device_id=here.device(link),
            device_id_type=MESH,
        )

    here.meet()
    for place in order:

        def begin(place=place):
            for name in ITEMS:
                side(name, place).start()
                load(name, place).start()

        guarded(here.inside(place[0]), begin)
    tokens.start()
    for place in order:

        def settle(place=place):
            for name in ITEMS:
                back, onward = links(ROUTES[name], place, chip_count)
                total = mine[name].at[spots.index(place)]
                load(name, place).wait()
                side(name, place).wait_recv()
                add_into(total, theirs[name].at[spots.index(place)])
                for link in onward:

                    def take(link=link):
                        arrival(name, place, link).wait_recv()
                        add_into(total, inbox[name].at[box[name, place, link]])

                    guarded(here.inside(link[1]) if link[0] == "z" else None, take)
                if back is not None:
                    send(name, place, back).start()

        guarded(here.inside(place[0]), settle)
    tokens.receive()
    tokens.drain()
    for name in ITEMS:
        outs[name][...] = mine[name][spots.index((0, 0, 0))].astype(jnp.float32)
    for place in order:

        def finish(place=place):
            for name in ITEMS:
                back, _ = links(ROUTES[name], place, chip_count)
                side(name, place).wait_send()
                if back is not None:
                    send(name, place, back).wait_send()

        guarded(here.inside(place[0]), finish)


def scatter_grads(grads, tokens_grad):
    chips = lax.axis_size("shard")
    spots = len(places(chips))
    widths, blocks, boxes = {}, [], []
    for name in ITEMS:
        shape = grads[name].shape
        if name == "project":
            block = (shape[0], shape[2], shape[3] // 2)
        elif name == "vectors":
            block = shape[1:]
        else:
            block = (shape[1], shape[2] // 2)
        widths[name] = block[-1]
        blocks.append(block)
        boxes.append(sum(len(links(ROUTES[name], place, chips)[1]) for place in places(chips)))
    kinds = [grads[name].dtype for name in ITEMS]
    outs = pl.pallas_call(
        lambda *refs: scatter_kernel(widths, chips, *refs),
        out_shape=[jax.ShapeDtypeStruct(block, jnp.float32) for block in blocks]
        + [jax.ShapeDtypeStruct(tokens_grad.shape, tokens_grad.dtype)],
        in_specs=[pl.BlockSpec(memory_space=pl.ANY)] * (len(ITEMS) + 1),
        out_specs=[pl.BlockSpec(memory_space=pltpu.VMEM)] * len(ITEMS)
        + [pl.BlockSpec(memory_space=pl.ANY)],
        scratch_shapes=(
            [pltpu.VMEM((spots,) + block, kind) for block, kind in zip(blocks, kinds)]
            + [pltpu.VMEM((spots,) + block, kind) for block, kind in zip(blocks, kinds)]
            + [pltpu.VMEM((box,) + block, kind) for box, block, kind in zip(boxes, blocks, kinds)]
            + [
                pltpu.SemaphoreType.DMA((len(ITEMS), spots)),
                pltpu.SemaphoreType.DMA((len(ITEMS), spots)),
                pltpu.SemaphoreType.DMA((len(ITEMS), spots)),
                pltpu.SemaphoreType.DMA((len(ITEMS), spots)),
                pltpu.SemaphoreType.DMA((link_count(chips),)),
            ]
            + exchange_scratch(tokens_grad.shape[0])
        ),
        compiler_params=pltpu.CompilerParams(
            collective_id=1, has_side_effects=True, vmem_limit_bytes=60 << 20
        ),
        name="scatter_grads",
    )(*[grads[name] for name in ITEMS], tokens_grad)
    return dict(zip(ITEMS, outs)), outs[-1]


CHUNK = 512
STEP = 16
UNROLL = 4
ATTEND_BIAS, DOWN_BIAS, FIRST_GAIN, FIRST_SHIFT, SECOND_GAIN, SECOND_SHIFT = range(3, 9)
SUMS = 6


def row_mean(values):
    return jnp.sum(values, axis=-1, keepdims=True) * (1.0 / D)


def fold(values):
    return jnp.sum(values.reshape(values.shape[0] // 8, 8, values.shape[1]), axis=0)


def chunk_at(index):
    return pl.ds(pl.multiple_of(index * CHUNK, CHUNK), CHUNK)


def ffn_kernel(
    shared, a_ref, attend_ref, wide_ref, shift_ref, x_hbm, c_hbm, up_hbm, down_hbm,
    joined_ref, branch_ref, sums_ref, up_sums_ref, out_hbm, up_grad_hbm, down_grad_hbm, attend_grad_hbm,
    x_ref, c_ref, up_ref, down_ref, out_ref, hidden_ref, slope_ref, low_ref, ffn_ref, turned_ref,
    left, right, near, far, first, unit, acc, factor, sums, up_sums, stage, in_sem, out_sem, stage_sem,
    *exchange_sems,
):
    loads = [
        pltpu.make_async_copy(source, target, in_sem.at[i])
        for i, (source, target) in enumerate(
            ((x_hbm, x_ref), (up_hbm, up_ref), (down_hbm, down_ref), (c_hbm, c_ref))
        )
        if not shared or source is not c_hbm
    ]
    for load in loads:
        load.start()
    if shared:
        here = Here()
        barrier = pltpu.get_barrier_semaphore()
        for offset in range(1, here.members):
            pl.semaphore_signal(barrier, inc=1, device_id=here.member(offset), device_id_type=MESH)
        arriving = Exchange(here, c_hbm, c_ref, *exchange_sems[:3])
        leaving = Exchange(here, out_ref, out_hbm, *exchange_sems[3:])
    sums[...] = jnp.zeros_like(sums)
    up_sums[...] = jnp.zeros_like(up_sums)
    pairs = FF // CHUNK // 2

    def vector(index):
        return wide_ref[pl.ds(index, 1), :]

    def add_sum(index, values):
        sums[index - ATTEND_BIAS] += fold(values)

    def rows_loop(body):
        @pl.loop(0, S // STEP, unroll=UNROLL)
        def _(step):
            body(pl.ds(pl.multiple_of(step * STEP, STEP), STEP))

    acc[...] = dot(a_ref[...], attend_ref[...], NT)
    if shared:
        pl.semaphore_wait(barrier, here.members - 1)
        arriving.start()
    loads[0].wait()

    @rows_loop
    def _(rows):
        joined = x_ref[rows, :].astype(jnp.float32) + acc[rows, :] + vector(ATTEND_BIAS)
        centred = joined - row_mean(joined)
        scale = lax.rsqrt(row_mean(centred * centred) + norm_eps)
        normed = centred * scale
        unit[rows, :] = normed
        factor[rows, :] = scale
        result = normed * vector(FIRST_GAIN) + vector(FIRST_SHIFT)
        first[rows, :] = result
        low_ref[rows, :] = result.astype(jnp.bfloat16)

    loads[1].wait()
    loads[2].wait()

    def expand(target, index):
        target[...] = dot(low_ref[...], up_ref[:, chunk_at(index)], NN)

    def activate(source, target, index):
        pre = source[...] + shift_ref[:, chunk_at(index)]
        cumulative = 0.5 + 0.5 * lax.erf(pre * (1.0 / math.sqrt(2.0)))
        density = jnp.exp(-0.5 * pre * pre) * (1.0 / math.sqrt(2.0 * math.pi))
        hidden = (pre * cumulative).astype(jnp.bfloat16)
        target[...] = hidden
        hidden_ref[:, chunk_at(index)] = hidden
        slope_ref[:, chunk_at(index)] = (cumulative + pre * density).astype(jnp.bfloat16)

    def contract(source, index):
        acc[...] += dot(source[...], down_ref[:, chunk_at(index)], NT)

    def forward(pair, last):
        expand(right, 2 * pair + 1)
        activate(left, near, 2 * pair)
        if not last:
            expand(left, 2 * pair + 2)
        contract(near, 2 * pair)
        activate(right, far, 2 * pair + 1)
        contract(far, 2 * pair + 1)

    expand(left, 0)
    acc[...] = jnp.zeros_like(acc)

    @pl.loop(0, pairs - 1)
    def _(pair):
        forward(pair, False)

    forward(pairs - 1, True)
    if shared:
        arriving.receive()
    else:
        loads[3].wait()

    @rows_loop
    def _(rows):
        joined = first[rows, :] + acc[rows, :] + vector(DOWN_BIAS)
        centred = joined - row_mean(joined)
        scale = lax.rsqrt(row_mean(centred * centred) + norm_eps)
        normed = centred * scale
        out_ref[rows, :] = (normed * vector(SECOND_GAIN) + vector(SECOND_SHIFT)).astype(jnp.bfloat16)
        grad = c_ref[rows, :].astype(jnp.float32)
        add_sum(SECOND_GAIN, grad * normed)
        add_sum(SECOND_SHIFT, grad)
        inner = grad * vector(SECOND_GAIN)
        back = scale * (inner - row_mean(inner) - normed * row_mean(inner * normed))
        first[rows, :] = back
        low = back.astype(jnp.bfloat16)
        ffn_ref[rows, :] = low
        add_sum(DOWN_BIAS, low.astype(jnp.float32))

    store = pltpu.make_async_copy(out_ref, out_hbm, out_sem)
    if not shared:
        store.start()

    def stored(slot, target, index):
        return pltpu.make_async_copy(
            stage.at[slot], target.at[:, chunk_at(index)], stage_sem.at[slot]
        )

    def weight_grad(source, target):
        @pl.loop(0, pairs)
        def _(pair):
            for slot in range(2):
                index = 2 * pair + slot

                @pl.when(pair > 0)
                def _():
                    stored(slot, target, index).wait()

                stage[slot] = dot(turned_ref[...], source[:, chunk_at(index)], NN).astype(jnp.bfloat16)
                stored(slot, target, index).start()

        for slot in range(2):
            stored(slot, target, slot).wait()

    turned_ref[...] = jnp.transpose(ffn_ref[...])
    if shared:
        leaving.start()
    weight_grad(hidden_ref, down_grad_hbm)

    def widen(target, index):
        target[...] = dot(ffn_ref[...], down_ref[:, chunk_at(index)], NN)

    def reweigh(source, target, index):
        grad = (source[...] * slope_ref[:, chunk_at(index)].astype(jnp.float32)).astype(jnp.bfloat16)
        target[...] = grad
        hidden_ref[:, chunk_at(index)] = grad
        up_sums[:, chunk_at(index)] += fold(grad.astype(jnp.float32))

    def collect(source, index):
        acc[...] += dot(source[...], up_ref[:, chunk_at(index)], NT)

    def backward(pair, last):
        widen(right, 2 * pair + 1)
        reweigh(left, near, 2 * pair)
        if not last:
            widen(left, 2 * pair + 2)
        collect(near, 2 * pair)
        reweigh(right, far, 2 * pair + 1)
        collect(far, 2 * pair + 1)

    widen(left, 0)
    acc[...] = jnp.zeros_like(acc)

    @pl.loop(0, pairs - 1)
    def _(pair):
        backward(pair, False)

    backward(pairs - 1, True)

    @rows_loop
    def _(rows):
        grad = first[rows, :] + acc[rows, :]
        normed = unit[rows, :]
        add_sum(FIRST_GAIN, grad * normed)
        add_sum(FIRST_SHIFT, grad)
        inner = grad * vector(FIRST_GAIN)
        back = factor[rows, :] * (inner - row_mean(inner) - normed * row_mean(inner * normed))
        low = back.astype(jnp.bfloat16)
        branch_ref[rows, :] = low
        add_sum(ATTEND_BIAS, low.astype(jnp.float32))

    joined_ref[...] = dot(branch_ref[...], attend_ref[...], NN).astype(jnp.bfloat16)
    turned_ref[...] = jnp.transpose(low_ref[...])
    weight_grad(hidden_ref, up_grad_hbm)
    turned_ref[...] = jnp.transpose(branch_ref[...])
    half = D // 2
    for slot in range(2):
        part = stage.at[slot, :, :half]
        stage[slot, :, :half] = dot(
            turned_ref[...], a_ref[:, slot * half : (slot + 1) * half], NN
        ).astype(jnp.bfloat16)
        pltpu.make_async_copy(
            part, attend_grad_hbm.at[:, slot * half : (slot + 1) * half], stage_sem.at[slot]
        ).start()
    for index in range(SUMS):
        sums_ref[pl.ds(index, 1), :] = jnp.sum(sums[index], axis=0, keepdims=True)
    up_sums_ref[...] = jnp.sum(up_sums[...], axis=0, keepdims=True)
    for slot in range(2):
        pltpu.make_async_copy(
            stage.at[slot, :, :half],
            attend_grad_hbm.at[:, slot * half : (slot + 1) * half],
            stage_sem.at[slot],
        ).wait()
    if shared:
        leaving.receive()
        arriving.drain()
        leaving.drain()
    else:
        store.wait()


def feed_forward(attended, x, cotangent, attend_t, up, down_t, wide, up_shift, shared=False):
    vmem, hbm = pl.BlockSpec(memory_space=pltpu.VMEM), pl.BlockSpec(memory_space=pl.ANY)

    def low(*shape):
        return jax.ShapeDtypeStruct(shape, jnp.bfloat16)

    def full(*shape):
        return jax.ShapeDtypeStruct(shape, jnp.float32)

    def scratch(width, kind=jnp.bfloat16):
        return pltpu.VMEM((S, width), kind)

    return pl.pallas_call(
        functools.partial(ffn_kernel, shared),
        in_specs=[vmem] * 4 + [hbm] * 4,
        out_specs=[vmem] * 4 + [hbm] * 4,
        out_shape=[
            low(S, D), low(S, D), full(SUMS, D), full(1, FF), low(*cotangent.shape), low(D, FF), low(D, FF),
            low(D, D),
        ],
        scratch_shapes=[
            scratch(D), scratch(D), pltpu.VMEM((D, FF), jnp.bfloat16), pltpu.VMEM((D, FF), jnp.bfloat16),
            scratch(D), scratch(FF), scratch(FF), scratch(D), scratch(D), pltpu.VMEM((D, S), jnp.bfloat16),
            scratch(CHUNK, jnp.float32), scratch(CHUNK, jnp.float32), scratch(CHUNK), scratch(CHUNK),
            scratch(D, jnp.float32), scratch(D, jnp.float32), scratch(D, jnp.float32),
            scratch(1, jnp.float32),
            pltpu.VMEM((SUMS, 8, D), jnp.float32), pltpu.VMEM((8, FF), jnp.float32),
            pltpu.VMEM((2, D, CHUNK), jnp.bfloat16),
            pltpu.SemaphoreType.DMA((4,)), pltpu.SemaphoreType.DMA, pltpu.SemaphoreType.DMA((2,)),
        ]
        + 2 * (exchange_scratch(cotangent.shape[0]) if shared else []),
        compiler_params=pltpu.CompilerParams(
            vmem_limit_bytes=63 << 20,
            collective_id=2 if shared else None,
            has_side_effects=shared,
        ),
        name="feed_forward",
        cost_estimate=pl.CostEstimate(
            flops=6 * S * D * (D + 2 * FF), bytes_accessed=30 << 20, transcendentals=2 * S * FF
        ),
    )(attended, attend_t, wide, up_shift.reshape(1, FF), x, cotangent, up, down_t)


def fitting(shards, own):
    return own == 1 and lax.axis_size("ctx") == 4 and lax.axis_size("tp") == 2 and shards["up"].shape[0] % 16 == 0


def gather_plain(shards):
    wholes = {}
    for name in ITEMS:
        axis = 1 if name == "project" else 0
        part = lax.all_gather(shards[name], ROWS, axis=axis)
        if name != "vectors":
            part = lax.all_gather(part, "tp", axis=axis + 2, tiled=True)
        wholes[name] = part
    return wholes


def scatter_plain(grads):
    shards = {}
    for name in ITEMS:
        axis = 1 if name == "project" else 0
        part = grads[name]
        if name == "vectors":
            part = lax.psum(part, "tp")
        else:
            part = lax.psum_scatter(part, "tp", scatter_dimension=axis + 2, tiled=True)
        part = lax.psum_scatter(part, ROWS, scatter_dimension=axis, tiled=False)
        shards[name] = part.astype(jnp.float32)
    return shards


def local(
    tokens, project_weight, attend_weight, up_weight, down_weight, project_bias, attend_bias,
    up_bias, down_bias, first_gain, first_shift, second_gain, second_shift, segment_ids, padding,
    cotangent,
):
    seq_count = tokens.shape[0]
    members = lax.axis_size("ctx") * lax.axis_size("tp")
    own = seq_count // members
    rank = lax.axis_index("ctx") * lax.axis_size("tp") + lax.axis_index("tp")
    pieces = lax.axis_size("shard") * lax.axis_size("ctx")
    depth = D // pieces

    def to_sequences(array):
        parts = array.reshape((members, own) + array.shape[1:])
        parts = lax.all_to_all(parts, SEQ, 0, 0, tiled=True)
        return jnp.swapaxes(parts, 0, 1).reshape(own, S, D)

    def to_blocks(array):
        parts = jnp.swapaxes(array.reshape(own, members, S // members, D), 0, 1)
        return lax.all_to_all(parts, SEQ, 0, 0, tiled=True).reshape(tokens.shape)

    segments = lax.dynamic_slice_in_dim(segment_ids, rank * own, own, 0)
    pads = lax.dynamic_slice_in_dim(padding, rank * own, own, 0)

    vectors = jnp.concatenate(
        [
            project_bias,
            attend_bias[None],
            down_bias[None],
            first_gain[None],
            first_shift[None],
            second_gain[None],
            second_shift[None],
            up_bias.reshape(FF // D, depth),
        ],
        axis=0,
    )
    shards = {
        "project": jnp.transpose(project_weight, (1, 0, 2)),
        "up": up_weight,
        "down": jnp.transpose(down_weight),
        "attend": jnp.transpose(attend_weight),
        "vectors": jnp.pad(vectors, ((0, 3), (0, LANES - depth))),
    }
    custom = fitting(shards, own)
    if custom:
        wholes, x = gather_weights(shards, tokens)
        x = x.reshape(own, S, D)
    else:
        wholes, x = gather_plain(shards), to_sequences(tokens)
    project = wholes["project"].reshape(3, D, D)
    up = wholes["up"].reshape(D, FF)
    down_t = wholes["down"].reshape(D, FF)
    attend_t = wholes["attend"].reshape(D, D)
    vectors = wholes["vectors"][:, :13, :depth].astype(jnp.float32)
    wide = jnp.transpose(vectors[:, :9], (1, 0, 2)).reshape(9, D)
    up_shift = vectors[:, 9:].reshape(FF)

    tables = mask_tables(segments, pads)
    cosine, sine = angles()
    query, key, value, attended, level = attend(
        tables[0], tables[1], x, project, wide[:3], cosine, sine, *tables[2:]
    )
    params = (attend_t, up, down_t, wide, up_shift)
    if custom:
        parts = [feed_forward(attended[0], x[0], cotangent, *params, shared=True)]
    else:
        incoming = to_sequences(cotangent)
        parts = [feed_forward(attended[i], x[i], incoming[i], *params) for i in range(own)]
    attended_grad = jnp.stack([part[0] for part in parts])
    branch_grad = jnp.stack([part[1] for part in parts])
    sums = sum(part[2] for part in parts)
    up_bias_grad = sum(part[3] for part in parts)
    output = parts[0][4] if custom else to_blocks(jnp.stack([part[4] for part in parts]))
    up_grad, down_grad, attend_grad = (
        parts[0][k] if own == 1 else sum(part[k].astype(jnp.float32) for part in parts).astype(jnp.bfloat16)
        for k in (5, 6, 7)
    )
    tokens_grad, project_grad, project_bias_grad = attend_back(
        tables[0], tables[1], query, key, value, attended, attended_grad, level, cosine, sine,
        *tables[2:], x, branch_grad, project,
    )
    project_bias_grad = jnp.sum(project_bias_grad, axis=0)
    if own == 1:
        project_grad = project_grad[0]
    else:
        project_grad = jnp.sum(project_grad.astype(jnp.float32), axis=0).astype(jnp.bfloat16)
    sums = jnp.concatenate([project_bias_grad, sums], axis=0)
    sums = jnp.concatenate(
        [
            jnp.transpose(sums.reshape(9, pieces, depth), (1, 0, 2)),
            up_bias_grad.reshape(pieces, FF // D, depth),
        ],
        axis=1,
    )
    grads = {
        "project": project_grad.reshape(3, pieces, depth, D),
        "up": up_grad.reshape(pieces, depth, FF),
        "down": down_grad.reshape(pieces, depth, FF),
        "attend": attend_grad.reshape(pieces, depth, D),
        "vectors": jnp.pad(sums, ((0, 0), (0, 3), (0, LANES - depth))),
    }
    if custom:
        shards, tokens_grad = scatter_grads(grads, tokens_grad.reshape(tokens.shape))
    else:
        shards, tokens_grad = scatter_plain(grads), to_blocks(tokens_grad)
    sums = shards["vectors"][:13, :depth]
    return (
        output,
        tokens_grad,
        jnp.transpose(shards["project"], (1, 0, 2)),
        jnp.transpose(shards["attend"]),
        shards["up"],
        jnp.transpose(shards["down"]),
        sums[:3],
        sums[3],
        sums[9:].reshape(-1),
        sums[4],
        sums[5],
        sums[6],
        sums[7],
        sums[8],
    )


def solution(mesh):
    in_specs = (
        P("shard", ("ctx", "tp"), None),
        P(("shard", "ctx"), None, "tp"),
        P("tp", ("shard", "ctx")),
        P(("shard", "ctx"), "tp"),
        P("tp", ("shard", "ctx")),
        P(None, ("shard", "ctx")),
        P(("shard", "ctx")),
        P(("shard", "ctx")),
        P(("shard", "ctx")),
        P(("shard", "ctx")),
        P(("shard", "ctx")),
        P(("shard", "ctx")),
        P(("shard", "ctx")),
        P("shard", None),
        P("shard", None),
        P("shard", ("ctx", "tp"), None),
    )
    out_specs = (
        P("shard", ("ctx", "tp"), None),
        P("shard", ("ctx", "tp"), None),
        P(("shard", "ctx"), None, "tp"),
        P("tp", ("shard", "ctx")),
        P(("shard", "ctx"), "tp"),
        P("tp", ("shard", "ctx")),
        P(None, ("shard", "ctx")),
        P(("shard", "ctx")),
        P(("shard", "ctx")),
        P(("shard", "ctx")),
        P(("shard", "ctx")),
        P(("shard", "ctx")),
        P(("shard", "ctx")),
        P(("shard", "ctx")),
    )
    return jax.shard_map(local, mesh=mesh, in_specs=in_specs, out_specs=out_specs, check_vma=False)
```

```python
import functools
import math

import jax
import jax.numpy as jnp
from jax import lax
from jax.experimental import pallas as pl
from jax.experimental.pallas import tpu as pltpu
from jax.sharding import PartitionSpec as P

D = 768
HEADS = 12
HEAD_DIM = 64
FF = 3072
S = 1024
LANES = 128
PAIRS = HEADS // 2
Q_ROWS = 128
LONGEST = 512
NARROW = 768

norm_eps = 1e-12
mask_fill = -1000000000.0

NT = (((1,), (1,)), ((), ()))
TN = (((0,), (0,)), ((), ()))
NN = (((1,), (0,)), ((), ()))


def dot(left, right, dims):
    return lax.dot_general(left, right, dims, preferred_element_type=jnp.float32)


def swap_pairs(values):
    lane = lax.broadcasted_iota(jnp.int32, values.shape, 1)
    width = values.shape[1]
    return jnp.where(
        lane % 2 == 0, -pltpu.roll(values, width - 1, 1), pltpu.roll(values, 1, 1)
    )


def stack_heads(rows):
    lane = lax.broadcasted_iota(jnp.int32, rows.shape, 1)
    zero = jnp.zeros_like(rows)
    return jnp.concatenate(
        [jnp.where(lane < HEAD_DIM, rows, zero), jnp.where(lane < HEAD_DIM, zero, rows)], axis=0
    )


def pick_heads(both):
    return jnp.concatenate([both[:HEAD_DIM, :Q_ROWS], both[HEAD_DIM:, Q_ROWS:]], axis=0)


def spread_heads(row):
    return jnp.concatenate(
        [
            jnp.broadcast_to(row[:, :Q_ROWS], (HEAD_DIM, Q_ROWS)),
            jnp.broadcast_to(row[:, Q_ROWS:], (HEAD_DIM, Q_ROWS)),
        ],
        axis=0,
    )


def mask_bias(key_code, query_low, query_high):
    keys = jnp.broadcast_to(key_code, (key_code.shape[0], Q_ROWS))
    allowed = (keys >= query_low) & (keys <= query_high)
    return jnp.where(allowed, 0.0, mask_fill)


def stack_turned(turned):
    feature = lax.broadcasted_iota(jnp.int32, turned.shape, 0)
    zero = jnp.zeros_like(turned)
    return jnp.concatenate(
        [jnp.where(feature < HEAD_DIM, turned, zero), jnp.where(feature < HEAD_DIM, zero, turned)],
        axis=1,
    )


def twice(bias):
    return jnp.concatenate([bias, bias], axis=1)


def for_blocks(body, tick=None):
    blocks = S // Q_ROWS
    reach = (LONGEST + Q_ROWS - 1) // Q_ROWS
    narrow = [i for i in range(blocks) if (i + 1 + reach) * Q_ROWS <= NARROW]
    edge = len(narrow)

    @pl.loop(0, 2 * edge)
    def _(step):
        if tick is not None:
            tick(step)
        late = (step >= edge).astype(jnp.int32)
        block = step + late * (blocks - 2 * edge)
        body(block, pl.multiple_of(late * (S - NARROW), Q_ROWS), NARROW)

    @pl.loop(edge, blocks - edge)
    def _(block):
        if tick is not None:
            tick(block + edge)
        body(block, 0, S)


def weight_columns(w_ref, part, first, width):
    chosen = w_ref.at[part][..., first : first + width]
    return chosen.reshape(D, width)


def project_rows(x_ref, w_ref, b_ref, cos_ref, sin_ref, q_ref, k_ref, v_ref):
    row_tile = 512

    @pl.loop(0, S // row_tile)
    def _(tile):
        rows = pl.ds(pl.multiple_of(tile * row_tile, row_tile), row_tile)
        x = x_ref[rows, :]
        cosine = cos_ref[rows, :]
        sine = sin_ref[rows, :]
        for part, out in enumerate((q_ref, k_ref, v_ref)):
            for pair in range(PAIRS):
                lanes = slice(pair * LANES, (pair + 1) * LANES)
                if pair % 2 == 0:
                    joint = dot(x, weight_columns(w_ref, part, pair * LANES, 2 * LANES), NN)
                piece = joint[:, pair % 2 * LANES : (pair % 2 + 1) * LANES] + b_ref[pl.ds(part, 1), lanes]
                if part < 2:
                    piece = piece * cosine + swap_pairs(piece) * sine
                if part == 0:
                    piece = piece.astype(jnp.bfloat16) * jnp.asarray(HEAD_DIM**-0.5, jnp.bfloat16)
                out[rows, lanes] = piece.astype(jnp.bfloat16)


def attend_kernel(
    x_ref, w_ref, b_ref, cos_ref, sin_ref, code_ref, low_ref, high_ref,
    q_ref, k_ref, v_ref, o_ref, lse_ref, *scratch,
):
    project_rows(x_ref, w_ref, b_ref, cos_ref, sin_ref, q_ref, k_ref, v_ref)
    attend_blocks(q_ref, k_ref, v_ref, o_ref, lse_ref, code_ref, low_ref, high_ref, *scratch)


def attend_scratch():
    return [
        pltpu.VMEM((D, S), jnp.bfloat16),
        pltpu.VMEM((D, S), jnp.bfloat16),
        pltpu.VMEM((S, Q_ROWS), jnp.float32),
        pltpu.VMEM((2, S, 2 * Q_ROWS), jnp.float32),
        pltpu.VMEM((2, S, 2 * Q_ROWS), jnp.bfloat16),
    ]


def attend_blocks(
    q_ref, k_ref, v_ref, o_ref, lse_ref, code_ref, low_ref, high_ref, q_turned, v_turned, bias, scores,
    probs, tick=None,
):
    q_turned[...] = jnp.transpose(q_ref[...])
    v_turned[...] = jnp.transpose(v_ref[...])

    def attend_block(block, first, count):
        rows = pl.ds(pl.multiple_of(block * Q_ROWS, Q_ROWS), Q_ROWS)
        keys = pl.ds(first, count)
        bias[:count] = mask_bias(code_ref[keys, :], low_ref[:, rows], high_ref[:, rows])
        tops = {}

        def score(pair):
            lanes = slice(pair * LANES, (pair + 1) * LANES)
            raw = dot(k_ref[keys, lanes], stack_turned(q_turned[lanes, rows]), NN)
            raw = raw + twice(bias[:count])
            scores[pair % 2, :count] = raw
            tops[pair] = jnp.max(raw, axis=0, keepdims=True)

        def mix(pair):
            lanes = slice(pair * LANES, (pair + 1) * LANES)
            expo = jnp.exp(scores[pair % 2, :count] - tops[pair])
            probs[pair % 2, :count] = expo.astype(jnp.bfloat16)
            total = jnp.sum(expo, axis=0, keepdims=True)
            mixed = dot(v_turned[lanes, keys], probs[pair % 2, :count], NN)
            out = pick_heads(mixed) / spread_heads(total)
            o_ref[rows, lanes] = jnp.transpose(out).astype(jnp.bfloat16)
            lse = tops[pair] + jnp.log(total)
            lse_ref[pl.ds(2 * pair, 1), rows] = lse[:, :Q_ROWS]
            lse_ref[pl.ds(2 * pair + 1, 1), rows] = lse[:, Q_ROWS:]

        score(0)
        for pair in range(PAIRS):
            if pair + 1 < PAIRS:
                score(pair + 1)
            mix(pair)

    for_blocks(attend_block, tick)


def attend_back_kernel(
    q_ref, k_ref, v_ref, o_ref, g_ref, lse_ref, cos_ref, sin_ref, code_ref, low_ref, high_ref,
    x_hbm, branch_hbm, w_hbm, token_ref, weight_ref, sums_ref,
    joint_ref, keys_acc, values_acc, q_turned, k_turned, g_turned, bias, probs, score_grads,
    x_ref, branch_ref, w_ref, turned, sums, sem,
):
    own = pl.program_id(0)
    loads = [
        pltpu.make_async_copy(source, target, sem.at[i])
        for i, (source, target) in enumerate(
            ((x_hbm.at[own], x_ref), (branch_hbm.at[own], branch_ref), (w_hbm, w_ref))
        )
    ]
    for load in loads:
        load.start()
    sums[...] = jnp.zeros_like(sums)
    keys_acc[...] = jnp.zeros_like(keys_acc)
    values_acc[...] = jnp.zeros_like(values_acc)
    q_turned[...] = jnp.transpose(q_ref[...])
    k_turned[...] = jnp.transpose(k_ref[...])
    g_turned[...] = jnp.transpose(g_ref[...])

    def keep(rows, lanes, grad):
        low = grad.astype(jnp.bfloat16)
        joint_ref[rows, lanes] = low
        sums[:, lanes] += jnp.sum(low.astype(jnp.float32).reshape(Q_ROWS // 8, 8, LANES), axis=0)

    def back_block(block, first, count):
        rows = pl.ds(pl.multiple_of(block * Q_ROWS, Q_ROWS), Q_ROWS)
        keys = pl.ds(first, count)
        bias[:count] = mask_bias(code_ref[keys, :], low_ref[:, rows], high_ref[:, rows])
        cosine = cos_ref[rows, :]
        sine = sin_ref[rows, :]

        def slopes(pair):
            lanes = slice(pair * LANES, (pair + 1) * LANES)
            both = g_turned[lanes, rows].astype(jnp.float32) * jnp.transpose(
                o_ref[rows, lanes].astype(jnp.float32)
            )
            delta = jnp.concatenate(
                [
                    jnp.sum(both[:HEAD_DIM], axis=0, keepdims=True),
                    jnp.sum(both[HEAD_DIM:], axis=0, keepdims=True),
                ],
                axis=1,
            )
            level = jnp.concatenate(
                [lse_ref[pl.ds(2 * pair, 1), rows], lse_ref[pl.ds(2 * pair + 1, 1), rows]], axis=1
            )
            raw = dot(k_ref[keys, lanes], stack_turned(q_turned[lanes, rows]), NN)
            prob = jnp.exp(raw + twice(bias[:count]) - level)
            prob_grad = dot(v_ref[keys, lanes], stack_turned(g_turned[lanes, rows]), NN)
            probs[pair % 2, :count] = prob.astype(jnp.bfloat16)
            score_grads[pair % 2, :count] = (prob * (prob_grad - delta)).astype(jnp.bfloat16)

        def gather(pair):
            lanes = slice(pair * LANES, (pair + 1) * LANES)
            values_acc[keys, lanes] += dot(probs[pair % 2, :count], stack_heads(g_ref[rows, lanes]), NN)
            keys_acc[keys, lanes] += dot(
                score_grads[pair % 2, :count], stack_heads(q_ref[rows, lanes]), NN
            )
            query = pick_heads(dot(k_turned[lanes, keys], score_grads[pair % 2, :count], NN))
            query = jnp.transpose(query) * (HEAD_DIM**-0.5)
            keep(rows, lanes, query * cosine - swap_pairs(query) * sine)

        slopes(0)
        for pair in range(PAIRS):
            if pair + 1 < PAIRS:
                slopes(pair + 1)
            gather(pair)

    for_blocks(back_block)

    @pl.loop(0, S // Q_ROWS)
    def _(block):
        rows = pl.ds(pl.multiple_of(block * Q_ROWS, Q_ROWS), Q_ROWS)
        cosine = cos_ref[rows, :]
        sine = sin_ref[rows, :]
        for pair in range(PAIRS):
            lanes = slice(pair * LANES, (pair + 1) * LANES)
            key = keys_acc[rows, lanes]
            keep(
                rows,
                slice(D + pair * LANES, D + (pair + 1) * LANES),
                key * cosine - swap_pairs(key) * sine,
            )
            keep(
                rows,
                slice(2 * D + pair * LANES, 2 * D + (pair + 1) * LANES),
                values_acc[rows, lanes],
            )

    for load in loads:
        load.wait()
    turned[...] = jnp.transpose(x_ref[...])
    for part in range(3):
        columns = slice(part * D, (part + 1) * D)
        weight_ref[part] = dot(turned[...], joint_ref[:, columns], NN).astype(jnp.bfloat16)
        sums_ref[pl.ds(part, 1), :] = jnp.sum(sums[:, columns], axis=0, keepdims=True)

    @pl.loop(0, 2)
    def _(half):
        rows = pl.ds(pl.multiple_of(half * (S // 2), S // 2), S // 2)
        total = branch_ref[rows, :].astype(jnp.float32)
        for part in range(3):
            total += dot(joint_ref[rows, part * D : (part + 1) * D], w_ref[part], NT)
        token_ref[rows, :] = total.astype(jnp.bfloat16)


def whole(*shape):
    return pl.BlockSpec(shape, lambda i, *_: (0,) * len(shape))


def per(*shape):
    return pl.BlockSpec((None,) + shape, lambda i, *_: (i,) + (0,) * len(shape))


def attend(x, weight, bias, cosine, sine, code, low, high):
    own = x.shape[0]
    act = jax.ShapeDtypeStruct((own, S, D), jnp.bfloat16)
    return pl.pallas_call(
        attend_kernel,
        grid=(own,),
        in_specs=[
            per(S, D), whole(3, D, D), whole(16, D), whole(S, LANES), whole(S, LANES),
            per(S, 1), per(1, S), per(1, S),
        ],
        out_specs=[per(S, D), per(S, D), per(S, D), per(S, D), per(HEADS, S)],
        scratch_shapes=attend_scratch(),
        out_shape=[act, act, act, act, jax.ShapeDtypeStruct((own, HEADS, S), jnp.float32)],
        compiler_params=pltpu.CompilerParams(vmem_limit_bytes=60 << 20),
        name="attend",
        cost_estimate=pl.CostEstimate(flops=6 * 10**9, bytes_accessed=12 << 20, transcendentals=6 << 20),
    )(x, weight, bias, cosine, sine, code, low, high)


def attend_back(q, k, v, o, g, lse, cosine, sine, code, low, high, x, branch_grad, weight):
    own = q.shape[0]
    hbm = pl.BlockSpec(memory_space=pl.ANY)
    return pl.pallas_call(
        attend_back_kernel,
        grid=(own,),
        in_specs=[
            per(S, D), per(S, D), per(S, D), per(S, D), per(S, D), per(HEADS, S),
            whole(S, LANES), whole(S, LANES), per(S, 1), per(1, S), per(1, S), hbm, hbm, hbm,
        ],
        out_specs=[per(S, D), per(3, D, D), per(3, D)],
        scratch_shapes=[
            pltpu.VMEM((S, 3 * D), jnp.bfloat16),
            pltpu.VMEM((S, D), jnp.float32),
            pltpu.VMEM((S, D), jnp.float32),
            pltpu.VMEM((D, S), jnp.bfloat16),
            pltpu.VMEM((D, S), jnp.bfloat16),
            pltpu.VMEM((D, S), jnp.bfloat16),
            pltpu.VMEM((S, Q_ROWS), jnp.float32),
            pltpu.VMEM((2, S, 2 * Q_ROWS), jnp.bfloat16),
            pltpu.VMEM((2, S, 2 * Q_ROWS), jnp.bfloat16),
            pltpu.VMEM((S, D), jnp.bfloat16),
            pltpu.VMEM((S, D), jnp.bfloat16),
            pltpu.VMEM((3, D, D), jnp.bfloat16),
            pltpu.VMEM((D, S), jnp.bfloat16),
            pltpu.VMEM((8, 3 * D), jnp.float32),
            pltpu.SemaphoreType.DMA((3,)),
        ],
        out_shape=[
            jax.ShapeDtypeStruct((own, S, D), jnp.bfloat16),
            jax.ShapeDtypeStruct((own, 3, D, D), jnp.bfloat16),
            jax.ShapeDtypeStruct((own, 3, D), jnp.float32),
        ],
        compiler_params=pltpu.CompilerParams(vmem_limit_bytes=60 << 20),
        name="attend_back",
        cost_estimate=pl.CostEstimate(flops=19 * 10**9, bytes_accessed=24 << 20, transcendentals=6 << 20),
    )(q, k, v, o, g, lse, cosine, sine, code, low, high, x, branch_grad, weight)


def mask_tables(segments, padding):
    code = 2 * segments + padding
    low = code
    high = 2 * segments + 1
    return code[:, :, None], low[:, None, :], high[:, None, :]


def angles():
    position = jnp.arange(S, dtype=jnp.int32).astype(jnp.float32)
    column = jnp.arange(LANES, dtype=jnp.int32) % HEAD_DIM // 2
    rate = jnp.exp(column.astype(jnp.float32) * (-2.0 * math.log(10000.0) / HEAD_DIM))
    phase = position[:, None] * rate[None, :]
    return jnp.cos(phase), jnp.sin(phase)


MESH = pl.DeviceIdType.MESH
ROWS = ("shard", "ctx")
EVERY = ("shard", "ctx", "tp")
SEQ = ("ctx", "tp")

PARTS = ("query", "key", "value")
BULK = ("up", "down", "attend")
ITEMS = PARTS + BULK + ("vectors",)
ARRAYS = ("project",) + BULK + ("vectors",)
ROUTES = {
    "query": "xyz", "key": "yxz", "value": "xyz", "up": "zyx", "down": "zxy", "attend": "yxz",
    "vectors": "xyz",
}


def places(depth):
    steps = [0]
    for k in range(1, depth):
        steps += [k, -k]
    return [(k, dy, dx) for k in steps for dy in (0, 1) for dx in (0, 1)]


def hops(place):
    return abs(place[0]) + place[1] + place[2]


def links(route, place, depth):
    apart = {"z": place[0] != 0, "y": place[1], "x": place[2]}
    level = max([i for i, axis in enumerate(route) if apart[axis]], default=-1)
    sign = (place[0] > 0) - (place[0] < 0)
    onward = []
    if level >= 0 and route[level] == "z" and abs(place[0]) + 1 < depth:
        onward.append(("z", -sign))
    for axis in route[level + 1 :]:
        onward += [("z", 1), ("z", -1)] if axis == "z" else [(axis, 1)]
    back = None if level < 0 else (route[level], sign if route[level] == "z" else 1)
    return back, onward


def seen_from(place, link):
    k, dy, dx = place
    axis, way = link
    return {"z": (k - way, dy, dx), "y": (k, 1 - dy, dx), "x": (k, dy, 1 - dx)}[axis]


class Here:
    def __init__(self):
        self.depth = lax.axis_size("shard")
        self.z = lax.axis_index("shard")
        self.c = lax.axis_index("ctx")
        self.t = lax.axis_index("tp")
        self.y = self.c // 2
        self.x = self.c % 2
        self.sides = lax.axis_size("tp")
        self.members = lax.axis_size("ctx") * self.sides
        self.rank = self.c * self.sides + self.t

    def rank_of(self, offset):
        return (self.rank + offset) % self.members

    def member(self, offset):
        rank = self.rank_of(offset)
        return (self.z, rank // self.sides, rank % self.sides)

    def device(self, link):
        axis, way = link
        if axis == "z":
            return (self.z + way, self.c, self.t)
        if axis == "y":
            return (self.z, 2 * (1 - self.y) + self.x, self.t)
        if axis == "x":
            return (self.z, 2 * self.y + (1 - self.x), self.t)
        return (self.z, self.c, 1 - self.t)

    def piece(self, place):
        k, dy, dx = place
        y = 1 - self.y if dy else self.y
        x = 1 - self.x if dx else self.x
        return (self.z + k) * 4 + 2 * y + x

    def inside(self, way):
        if way == 0:
            return None
        return self.z + way < self.depth if way > 0 else self.z + way >= 0

    def meet(self):
        barrier = pltpu.get_barrier_semaphore()
        for offset in range(1, self.members):
            pl.semaphore_signal(
                barrier, inc=1, device_id=self.member(offset), device_id_type=MESH
            )
        for way in (1, -1):

            @pl.when(self.inside(way))
            def _():
                pl.semaphore_signal(
                    barrier, inc=1, device_id=self.device(("z", way)), device_id_type=MESH
                )

        above = (self.z < self.depth - 1).astype(jnp.int32)
        below = (self.z > 0).astype(jnp.int32)
        pl.semaphore_wait(barrier, self.members - 1 + above + below)


class Exchange:
    def __init__(self, here, source, target, send_sem, recv_sem, own_sem):
        self.here, self.source, self.target = here, source, target
        self.send_sem, self.recv_sem, self.own_sem = send_sem, recv_sem, own_sem

    def block(self, ref, index):
        return ref.at[index] if len(ref.shape) == 3 else ref.at[rows_of(index)]

    def copy(self, offset):
        here = self.here
        return pltpu.make_async_remote_copy(
            src_ref=self.block(self.source, here.rank_of(offset)),
            dst_ref=self.block(self.target, here.rank),
            send_sem=self.send_sem.at[offset],
            recv_sem=self.recv_sem.at[offset],
            device_id=here.member(offset),
            device_id_type=MESH,
        )

    def arrival(self, offset):
        here = self.here
        landed = self.block(self.target, here.rank_of(here.members - offset))
        return pltpu.make_async_remote_copy(
            src_ref=landed,
            dst_ref=landed,
            send_sem=self.send_sem.at[offset],
            recv_sem=self.recv_sem.at[offset],
            device_id=here.member(offset),
            device_id_type=MESH,
        )

    def own(self):
        rank = self.here.rank
        return pltpu.make_async_copy(
            self.block(self.source, rank), self.block(self.target, rank), self.own_sem
        )

    def start(self):
        for offset in range(1, self.here.members):
            self.copy(offset).start()
        self.own().start()

    def receive(self):
        for offset in range(1, self.here.members):
            self.arrival(offset).wait_recv()
        self.own().wait()

    def drain(self):
        for offset in range(1, self.here.members):
            self.copy(offset).wait_send()


def rows_of(index):
    return pl.ds(pl.multiple_of(index * Q_ROWS, Q_ROWS), Q_ROWS)


def exchange_scratch(members):
    return [
        pltpu.SemaphoreType.DMA((members,)),
        pltpu.SemaphoreType.DMA((members,)),
        pltpu.SemaphoreType.DMA,
    ]


def guarded(condition, action):
    if condition is None:
        action()
    else:
        pl.when(condition)(action)


def columns(half, width):
    return pl.ds(pl.multiple_of(half * width, LANES), width)


def block_of(name, refs, piece, half, widths):
    if name in PARTS:
        return refs["project"].at[PARTS.index(name), piece, :, columns(half, widths["project"])]
    if name == "vectors":
        return refs[name].at[piece]
    return refs[name].at[piece, :, columns(half, widths[name])]


def shard_of(name, refs):
    return refs["project"].at[PARTS.index(name)] if name in PARTS else refs[name]


def one_hot_rows(vectors_ref):
    pieces = vectors_ref.shape[0]
    depth = D // pieces
    entry = lax.broadcasted_iota(jnp.int32, (LANES, D), 0)
    column = lax.broadcasted_iota(jnp.int32, (LANES, D), 1)

    def add(piece, total):
        chosen = (column == entry + piece * depth) & (entry < depth)
        return total + dot(vectors_ref[piece], jnp.where(chosen, 1.0, 0.0).astype(jnp.bfloat16), NN)

    return lax.fori_loop(0, pieces, add, jnp.zeros((16, D), jnp.float32))


def gather_attend_kernel(
    widths, chip_count, project_hbm, up_hbm, down_hbm, attend_hbm, vectors_hbm, tokens_hbm,
    cos_ref, sin_ref, code_ref, low_ref, high_ref,
    q_ref, k_ref, v_ref, o_ref, lse_ref, wide_ref, vectors_out, project_out, x_out, up_out, down_out, attend_out,
    x_ref, w_ref, vectors_ref, q_turned, v_turned, bias, scores, probs,
    send_sem, recv_sem, side_send, side_recv, own_sem, keep_sem, *exchange_sems,
):
    shards = dict(zip(ARRAYS, (project_hbm, up_hbm, down_hbm, attend_hbm, vectors_hbm)))
    wholes = dict(zip(ARRAYS, (w_ref, up_out, down_out, attend_out, vectors_ref)))
    here = Here()
    tokens = Exchange(here, tokens_hbm, x_ref, *exchange_sems)
    spots = places(chip_count)
    order = sorted(spots, key=hops)
    home = (0, 0, 0)
    slot = {}
    for name in ITEMS:
        for place in spots:
            for link in links(ROUTES[name], place, chip_count)[1]:
                slot[name, place, link] = len(slot)

    def block(name, place, half):
        return block_of(name, wholes, here.piece(place), half, widths)

    def source(name, place, half):
        return shard_of(name, shards) if place == home else block(name, place, half)

    def send(name, place, link):
        return pltpu.make_async_remote_copy(
            src_ref=source(name, place, here.t),
            dst_ref=block(name, place, here.t),
            send_sem=send_sem.at[slot[name, place, link]],
            recv_sem=recv_sem.at[ITEMS.index(name), spots.index(seen_from(place, link))],
            device_id=here.device(link),
            device_id_type=MESH,
        )

    def side(name, place, half):
        return pltpu.make_async_remote_copy(
            src_ref=source(name, place, half) if half is here.t else block(name, place, half),
            dst_ref=block(name, place, half),
            send_sem=side_send.at[ITEMS.index(name), spots.index(place)],
            recv_sem=side_recv.at[ITEMS.index(name), spots.index(place)],
            device_id=here.device(("tp", 1)),
            device_id_type=MESH,
        )

    def arrival(name, place):
        return pltpu.make_async_remote_copy(
            src_ref=block(name, place, here.t),
            dst_ref=block(name, place, here.t),
            send_sem=send_sem.at[0],
            recv_sem=recv_sem.at[ITEMS.index(name), spots.index(place)],
            device_id=here.device(("tp", 1)),
            device_id_type=MESH,
        )

    def own(name):
        return pltpu.make_async_copy(
            shard_of(name, shards), block(name, home, here.t), own_sem.at[ITEMS.index(name)]
        )

    def relay(names, place):
        def pass_on():
            for name in names:
                if place != home:
                    arrival(name, place).wait_recv()
                for link in links(ROUTES[name], place, chip_count)[1]:
                    guarded(
                        here.inside(link[1]) if link[0] == "z" else None,
                        lambda name=name, link=link: send(name, place, link).start(),
                    )
                if name != "vectors":
                    side(name, place, here.t).start()

        guarded(here.inside(place[0]), pass_on)

    def beside(names):
        for place in order:

            def wait(place=place):
                for name in names:
                    side(name, place, 1 - here.t).wait_recv()

            guarded(here.inside(place[0]), wait)

    early = PARTS + ("vectors",)
    here.meet()
    relay(early, home)
    tokens.start()
    for name in ITEMS:
        own(name).start()
    for place in order[1:]:
        relay(early, place)
    relay(BULK, home)
    for name in early:
        own(name).wait()
    wide_ref[...] = one_hot_rows(vectors_ref)
    tokens.receive()
    beside(PARTS)
    keep = [
        pltpu.make_async_copy(w_ref, project_out, keep_sem.at[0]),
        pltpu.make_async_copy(x_ref, x_out, keep_sem.at[1]),
        pltpu.make_async_copy(vectors_ref, vectors_out, keep_sem.at[2]),
    ]
    for copy in keep:
        copy.start()
    project_rows(x_ref, w_ref, wide_ref, cos_ref, sin_ref, q_ref, k_ref, v_ref)
    farthest = max(hops(place) for place in spots)

    def level(distance):
        for place in order:
            if hops(place) == distance:
                relay(BULK, place)

    def tick(step):
        for distance in range(1, farthest):
            pl.when(step == 2 * (distance - 1))(functools.partial(level, distance))

    attend_blocks(
        q_ref, k_ref, v_ref, o_ref, lse_ref, code_ref, low_ref, high_ref, q_turned, v_turned, bias,
        scores, probs, tick,
    )
    level(farthest)
    beside(BULK)
    for name in BULK:
        own(name).wait()
    tokens.drain()
    for copy in keep:
        copy.wait()
    for place in order:

        def finish(place=place):
            for name in ITEMS:
                if name != "vectors":
                    side(name, place, here.t).wait_send()
                for link in links(ROUTES[name], place, chip_count)[1]:
                    guarded(
                        here.inside(link[1]) if link[0] == "z" else None,
                        lambda name=name, link=link: send(name, place, link).wait_send(),
                    )

        guarded(here.inside(place[0]), finish)


def link_count(depth):
    return sum(len(links(ROUTES[name], place, depth)[1]) for name in ITEMS for place in places(depth))


def gather_attend(shards, tokens, cosine, sine, code, low, high):
    chips, pieces = lax.axis_size("shard"), lax.axis_size("shard") * lax.axis_size("ctx")
    members = tokens.shape[0]
    widths = {name: shards[name].shape[-1] for name in ARRAYS}
    depth = shards["up"].shape[0]
    spots = len(places(chips))
    vmem, hbm = pl.BlockSpec(memory_space=pltpu.VMEM), pl.BlockSpec(memory_space=pl.ANY)

    def act(*shape):
        return jax.ShapeDtypeStruct(shape, jnp.bfloat16)

    def gathered(name):
        return act(pieces, depth, 2 * widths[name])

    whole_vectors = (pieces,) + shards["vectors"].shape
    whole_project = (3, pieces, depth, D)
    outs = pl.pallas_call(
        functools.partial(gather_attend_kernel, widths, chips),
        out_shape=[
            act(S, D), act(S, D), act(S, D), act(S, D), jax.ShapeDtypeStruct((HEADS, S), jnp.float32),
            jax.ShapeDtypeStruct((16, D), jnp.float32), act(*whole_vectors), act(*whole_project), act(S, D),
            gathered("up"), gathered("down"), gathered("attend"),
        ],
        in_specs=[hbm] * 6 + [vmem] * 5,
        out_specs=[vmem] * 6 + [hbm] * 6,
        scratch_shapes=[
            pltpu.VMEM((S, D), jnp.bfloat16),
            pltpu.VMEM(whole_project, jnp.bfloat16),
            pltpu.VMEM(whole_vectors, jnp.bfloat16),
        ]
        + attend_scratch()
        + [
            pltpu.SemaphoreType.DMA((link_count(chips),)),
            pltpu.SemaphoreType.DMA((len(ITEMS), spots)),
            pltpu.SemaphoreType.DMA((len(ITEMS), spots)),
            pltpu.SemaphoreType.DMA((len(ITEMS), spots)),
            pltpu.SemaphoreType.DMA((len(ITEMS),)),
            pltpu.SemaphoreType.DMA((3,)),
        ]
        + exchange_scratch(members),
        compiler_params=pltpu.CompilerParams(
            collective_id=0, has_side_effects=True, vmem_limit_bytes=60 << 20
        ),
        name="gather_attend",
    )(*[shards[name] for name in ARRAYS], tokens, cosine, sine, code, low, high)
    query, key, value, attended, level, wide, vectors, project, x = outs[:9]
    wholes = dict(zip(BULK, outs[9:]), project=project, vectors=vectors)
    return query, key, value, attended, level, wide, x, wholes


def add_into(target, addend):
    lead = target.shape[:-2]
    for index in range(math.prod(lead)):
        at = (index,) if lead else ()
        height = 16 if target.shape[-2] % 16 == 0 else 8

        @pl.loop(0, target.shape[-2] // height)
        def _(step):
            rows = pl.ds(pl.multiple_of(step * height, height), height)
            where = at + (rows, slice(None))
            total = target[where].astype(jnp.float32) + addend[where].astype(jnp.float32)
            target[where] = total.astype(target.dtype)


def scatter_kernel(widths, chip_count, *refs):
    count = len(ARRAYS)
    grads = dict(zip(ARRAYS, refs[:count]))
    outs = dict(zip(ARRAYS, refs[count + 1 : 2 * count + 1]))
    rest = refs[2 * count + 2 :]
    count = len(ITEMS)
    mine = dict(zip(ITEMS, rest[:count]))
    theirs = dict(zip(ITEMS, rest[count : 2 * count]))
    inbox = dict(zip(ITEMS, rest[2 * count : 3 * count]))
    load_sem, side_send, side_recv, send_sem, recv_sem = rest[3 * count : 3 * count + 5]
    here = Here()
    tokens = Exchange(here, refs[len(ARRAYS)], refs[2 * len(ARRAYS) + 1], *rest[3 * count + 5 :])
    spots = places(chip_count)
    order = sorted(spots, key=hops, reverse=True)
    slot = {}
    box = {}
    for name in ITEMS:
        local = 0
        for place in spots:
            for link in links(ROUTES[name], place, chip_count)[1]:
                slot[name, place, link] = len(slot)
                box[name, place, link] = local
                local += 1

    def opposite(link):
        return (link[0], -link[1]) if link[0] == "z" else link

    def load(name, place):
        return pltpu.make_async_copy(
            block_of(name, grads, here.piece(place), here.t, widths),
            mine[name].at[spots.index(place)],
            load_sem.at[ITEMS.index(name), spots.index(place)],
        )

    def side(name, place):
        return pltpu.make_async_remote_copy(
            src_ref=block_of(name, grads, here.piece(place), 1 - here.t, widths),
            dst_ref=theirs[name].at[spots.index(place)],
            send_sem=side_send.at[ITEMS.index(name), spots.index(place)],
            recv_sem=side_recv.at[ITEMS.index(name), spots.index(place)],
            device_id=here.device(("tp", 1)),
            device_id_type=MESH,
        )

    def send(name, place, link):
        there = seen_from(place, link)
        return pltpu.make_async_remote_copy(
            src_ref=mine[name].at[spots.index(place)],
            dst_ref=inbox[name].at[box[name, there, opposite(link)]],
            send_sem=send_sem.at[ITEMS.index(name), spots.index(place)],
            recv_sem=recv_sem.at[slot[name, there, opposite(link)]],
            device_id=here.device(link),
            device_id_type=MESH,
        )

    def arrival(name, place, link):
        return pltpu.make_async_remote_copy(
            src_ref=inbox[name].at[box[name, place, link]],
            dst_ref=inbox[name].at[box[name, place, link]],
            send_sem=send_sem.at[0, 0],
            recv_sem=recv_sem.at[slot[name, place, link]],
            device_id=here.device(link),
            device_id_type=MESH,
        )

    here.meet()
    for place in order:

        def begin(place=place):
            for name in ITEMS:
                side(name, place).start()
                load(name, place).start()

        guarded(here.inside(place[0]), begin)
    tokens.start()
    for place in order:

        def settle(place=place):
            for name in ITEMS:
                back, onward = links(ROUTES[name], place, chip_count)
                total = mine[name].at[spots.index(place)]
                load(name, place).wait()
                side(name, place).wait_recv()
                add_into(total, theirs[name].at[spots.index(place)])
                for link in onward:

                    def take(link=link):
                        arrival(name, place, link).wait_recv()
                        add_into(total, inbox[name].at[box[name, place, link]])

                    guarded(here.inside(link[1]) if link[0] == "z" else None, take)
                if back is not None:
                    send(name, place, back).start()

        guarded(here.inside(place[0]), settle)
    tokens.receive()
    tokens.drain()
    for name in ITEMS:
        shard_of(name, outs)[...] = mine[name][spots.index((0, 0, 0))].astype(jnp.float32)
    for place in order:

        def finish(place=place):
            for name in ITEMS:
                back, _ = links(ROUTES[name], place, chip_count)
                side(name, place).wait_send()
                if back is not None:
                    send(name, place, back).wait_send()

        guarded(here.inside(place[0]), finish)


def scatter_grads(grads, tokens_grad):
    chips = lax.axis_size("shard")
    spots = len(places(chips))
    widths, blocks, boxes = {}, [], []
    for name in ITEMS:
        shape = grads["project" if name in PARTS else name].shape
        block = shape[1:] if name == "vectors" else shape[-2:-1] + (shape[-1] // 2,)
        widths["project" if name in PARTS else name] = block[-1]
        blocks.append(block)
        boxes.append(sum(len(links(ROUTES[name], place, chips)[1]) for place in places(chips)))
    depth = grads["up"].shape[1]
    results = [(3, depth, widths["project"])] + blocks[len(PARTS) :]
    kinds = [jnp.float32 if name == "vectors" else jnp.bfloat16 for name in ITEMS]
    outs = pl.pallas_call(
        lambda *refs: scatter_kernel(widths, chips, *refs),
        out_shape=[jax.ShapeDtypeStruct(block, jnp.float32) for block in results]
        + [jax.ShapeDtypeStruct(tokens_grad.shape, tokens_grad.dtype)],
        in_specs=[pl.BlockSpec(memory_space=pl.ANY)] * (len(ARRAYS) + 1),
        out_specs=[pl.BlockSpec(memory_space=pltpu.VMEM)] * len(ARRAYS)
        + [pl.BlockSpec(memory_space=pl.ANY)],
        scratch_shapes=(
            [pltpu.VMEM((spots,) + block, kind) for block, kind in zip(blocks, kinds)]
            + [pltpu.VMEM((spots,) + block, kind) for block, kind in zip(blocks, kinds)]
            + [pltpu.VMEM((box,) + block, kind) for box, block, kind in zip(boxes, blocks, kinds)]
            + [
                pltpu.SemaphoreType.DMA((len(ITEMS), spots)),
                pltpu.SemaphoreType.DMA((len(ITEMS), spots)),
                pltpu.SemaphoreType.DMA((len(ITEMS), spots)),
                pltpu.SemaphoreType.DMA((len(ITEMS), spots)),
                pltpu.SemaphoreType.DMA((link_count(chips),)),
            ]
            + exchange_scratch(tokens_grad.shape[0])
        ),
        compiler_params=pltpu.CompilerParams(
            collective_id=1, has_side_effects=True, vmem_limit_bytes=60 << 20
        ),
        name="scatter_grads",
    )(*[grads[name] for name in ARRAYS], tokens_grad)
    return dict(zip(ARRAYS, outs)), outs[-1]


CHUNK = 512
STEP = 16
UNROLL = 4
ATTEND_BIAS, DOWN_BIAS, FIRST_GAIN, FIRST_SHIFT, SECOND_GAIN, SECOND_SHIFT = range(3, 9)
SUMS = 6


def row_mean(values):
    return jnp.sum(values, axis=-1, keepdims=True) * (1.0 / D)


def fold(values):
    return jnp.sum(values.reshape(values.shape[0] // 8, 8, values.shape[1]), axis=0)


def chunk_at(index):
    return pl.ds(pl.multiple_of(index * CHUNK, CHUNK), CHUNK)


def ffn_kernel(
    shared, a_ref, attend_ref, wide_ref, shift_ref, x_hbm, c_hbm, up_hbm, down_hbm,
    joined_ref, branch_ref, sums_ref, up_sums_ref, out_hbm, up_grad_hbm, down_grad_hbm, attend_grad_hbm,
    x_ref, c_ref, up_ref, down_ref, out_ref, hidden_ref, slope_ref, low_ref, ffn_ref, turned_ref,
    left, right, near, far, first, unit, acc, factor, sums, up_sums, stage, in_sem, out_sem, stage_sem,
    *exchange_sems,
):
    loads = [
        pltpu.make_async_copy(source, target, in_sem.at[i])
        for i, (source, target) in enumerate(
            ((x_hbm, x_ref), (up_hbm, up_ref), (down_hbm, down_ref), (c_hbm, c_ref))
        )
        if not shared or source is not c_hbm
    ]
    for load in loads:
        load.start()
    if shared:
        here = Here()
        barrier = pltpu.get_barrier_semaphore()
        for offset in range(1, here.members):
            pl.semaphore_signal(barrier, inc=1, device_id=here.member(offset), device_id_type=MESH)
        arriving = Exchange(here, c_hbm, c_ref, *exchange_sems[:3])
        leaving = Exchange(here, out_ref, out_hbm, *exchange_sems[3:])
    sums[...] = jnp.zeros_like(sums)
    up_sums[...] = jnp.zeros_like(up_sums)
    pairs = FF // CHUNK // 2

    def vector(index):
        return wide_ref[pl.ds(index, 1), :]

    def add_sum(index, values):
        sums[index - ATTEND_BIAS] += fold(values)

    def rows_loop(body):
        @pl.loop(0, S // STEP, unroll=UNROLL)
        def _(step):
            body(pl.ds(pl.multiple_of(step * STEP, STEP), STEP))

    acc[...] = dot(a_ref[...], attend_ref[...], NT)
    if shared:
        pl.semaphore_wait(barrier, here.members - 1)
        arriving.start()
    loads[0].wait()

    @rows_loop
    def _(rows):
        joined = x_ref[rows, :].astype(jnp.float32) + acc[rows, :] + vector(ATTEND_BIAS)
        centred = joined - row_mean(joined)
        scale = lax.rsqrt(row_mean(centred * centred) + norm_eps)
        normed = centred * scale
        unit[rows, :] = normed
        factor[rows, :] = scale
        result = normed * vector(FIRST_GAIN) + vector(FIRST_SHIFT)
        first[rows, :] = result
        low_ref[rows, :] = result.astype(jnp.bfloat16)

    loads[1].wait()
    loads[2].wait()

    def expand(target, index):
        target[...] = dot(low_ref[...], up_ref[:, chunk_at(index)], NN)

    def activate(source, target, index):
        pre = source[...] + shift_ref[:, chunk_at(index)]
        cumulative = 0.5 + 0.5 * lax.erf(pre * (1.0 / math.sqrt(2.0)))
        density = jnp.exp(-0.5 * pre * pre) * (1.0 / math.sqrt(2.0 * math.pi))
        hidden = (pre * cumulative).astype(jnp.bfloat16)
        target[...] = hidden
        hidden_ref[:, chunk_at(index)] = hidden
        slope_ref[:, chunk_at(index)] = (cumulative + pre * density).astype(jnp.bfloat16)

    def contract(source, index):
        acc[...] += dot(source[...], down_ref[:, chunk_at(index)], NT)

    def forward(pair, last):
        expand(right, 2 * pair + 1)
        activate(left, near, 2 * pair)
        if not last:
            expand(left, 2 * pair + 2)
        contract(near, 2 * pair)
        activate(right, far, 2 * pair + 1)
        contract(far, 2 * pair + 1)

    expand(left, 0)
    acc[...] = jnp.zeros_like(acc)

    @pl.loop(0, pairs - 1)
    def _(pair):
        forward(pair, False)

    forward(pairs - 1, True)
    if shared:
        arriving.receive()
    else:
        loads[3].wait()

    @rows_loop
    def _(rows):
        joined = first[rows, :] + acc[rows, :] + vector(DOWN_BIAS)
        centred = joined - row_mean(joined)
        scale = lax.rsqrt(row_mean(centred * centred) + norm_eps)
        normed = centred * scale
        out_ref[rows, :] = (normed * vector(SECOND_GAIN) + vector(SECOND_SHIFT)).astype(jnp.bfloat16)
        grad = c_ref[rows, :].astype(jnp.float32)
        add_sum(SECOND_GAIN, grad * normed)
        add_sum(SECOND_SHIFT, grad)
        inner = grad * vector(SECOND_GAIN)
        back = scale * (inner - row_mean(inner) - normed * row_mean(inner * normed))
        first[rows, :] = back
        low = back.astype(jnp.bfloat16)
        ffn_ref[rows, :] = low
        add_sum(DOWN_BIAS, low.astype(jnp.float32))

    store = pltpu.make_async_copy(out_ref, out_hbm, out_sem)
    if not shared:
        store.start()

    def stored(slot, target, index):
        return pltpu.make_async_copy(
            stage.at[slot], target.at[:, chunk_at(index)], stage_sem.at[slot]
        )

    def weight_grad(source, target):
        @pl.loop(0, pairs)
        def _(pair):
            for slot in range(2):
                index = 2 * pair + slot

                @pl.when(pair > 0)
                def _():
                    stored(slot, target, index).wait()

                stage[slot] = dot(turned_ref[...], source[:, chunk_at(index)], NN).astype(jnp.bfloat16)
                stored(slot, target, index).start()

        for slot in range(2):
            stored(slot, target, slot).wait()

    turned_ref[...] = jnp.transpose(ffn_ref[...])
    if shared:
        leaving.start()
    weight_grad(hidden_ref, down_grad_hbm)

    def widen(target, index):
        target[...] = dot(ffn_ref[...], down_ref[:, chunk_at(index)], NN)

    def reweigh(source, target, index):
        grad = (source[...] * slope_ref[:, chunk_at(index)].astype(jnp.float32)).astype(jnp.bfloat16)
        target[...] = grad
        hidden_ref[:, chunk_at(index)] = grad
        up_sums[:, chunk_at(index)] += fold(grad.astype(jnp.float32))

    def collect(source, index):
        acc[...] += dot(source[...], up_ref[:, chunk_at(index)], NT)

    def backward(pair, last):
        widen(right, 2 * pair + 1)
        reweigh(left, near, 2 * pair)
        if not last:
            widen(left, 2 * pair + 2)
        collect(near, 2 * pair)
        reweigh(right, far, 2 * pair + 1)
        collect(far, 2 * pair + 1)

    widen(left, 0)
    acc[...] = jnp.zeros_like(acc)

    @pl.loop(0, pairs - 1)
    def _(pair):
        backward(pair, False)

    backward(pairs - 1, True)

    @rows_loop
    def _(rows):
        grad = first[rows, :] + acc[rows, :]
        normed = unit[rows, :]
        add_sum(FIRST_GAIN, grad * normed)
        add_sum(FIRST_SHIFT, grad)
        inner = grad * vector(FIRST_GAIN)
        back = factor[rows, :] * (inner - row_mean(inner) - normed * row_mean(inner * normed))
        low = back.astype(jnp.bfloat16)
        branch_ref[rows, :] = low
        add_sum(ATTEND_BIAS, low.astype(jnp.float32))

    joined_ref[...] = dot(branch_ref[...], attend_ref[...], NN).astype(jnp.bfloat16)
    turned_ref[...] = jnp.transpose(low_ref[...])
    weight_grad(hidden_ref, up_grad_hbm)
    turned_ref[...] = jnp.transpose(branch_ref[...])
    half = D // 2
    for slot in range(2):
        part = stage.at[slot, :, :half]
        stage[slot, :, :half] = dot(
            turned_ref[...], a_ref[:, slot * half : (slot + 1) * half], NN
        ).astype(jnp.bfloat16)
        pltpu.make_async_copy(
            part, attend_grad_hbm.at[:, slot * half : (slot + 1) * half], stage_sem.at[slot]
        ).start()
    for index in range(SUMS):
        sums_ref[pl.ds(index, 1), :] = jnp.sum(sums[index], axis=0, keepdims=True)
    up_sums_ref[...] = jnp.sum(up_sums[...], axis=0, keepdims=True)
    for slot in range(2):
        pltpu.make_async_copy(
            stage.at[slot, :, :half],
            attend_grad_hbm.at[:, slot * half : (slot + 1) * half],
            stage_sem.at[slot],
        ).wait()
    if shared:
        leaving.receive()
        arriving.drain()
        leaving.drain()
    else:
        store.wait()


def feed_forward(attended, x, cotangent, attend_t, up, down_t, wide, up_shift, shared=False):
    vmem, hbm = pl.BlockSpec(memory_space=pltpu.VMEM), pl.BlockSpec(memory_space=pl.ANY)

    def low(*shape):
        return jax.ShapeDtypeStruct(shape, jnp.bfloat16)

    def full(*shape):
        return jax.ShapeDtypeStruct(shape, jnp.float32)

    def scratch(width, kind=jnp.bfloat16):
        return pltpu.VMEM((S, width), kind)

    return pl.pallas_call(
        functools.partial(ffn_kernel, shared),
        in_specs=[vmem] * 4 + [hbm] * 4,
        out_specs=[vmem] * 4 + [hbm] * 4,
        out_shape=[
            low(S, D), low(S, D), full(SUMS, D), full(1, FF), low(*cotangent.shape), low(D, FF), low(D, FF),
            low(D, D),
        ],
        scratch_shapes=[
            scratch(D), scratch(D), pltpu.VMEM((D, FF), jnp.bfloat16), pltpu.VMEM((D, FF), jnp.bfloat16),
            scratch(D), scratch(FF), scratch(FF), scratch(D), scratch(D), pltpu.VMEM((D, S), jnp.bfloat16),
            scratch(CHUNK, jnp.float32), scratch(CHUNK, jnp.float32), scratch(CHUNK), scratch(CHUNK),
            scratch(D, jnp.float32), scratch(D, jnp.float32), scratch(D, jnp.float32),
            scratch(1, jnp.float32),
            pltpu.VMEM((SUMS, 8, D), jnp.float32), pltpu.VMEM((8, FF), jnp.float32),
            pltpu.VMEM((2, D, CHUNK), jnp.bfloat16),
            pltpu.SemaphoreType.DMA((4,)), pltpu.SemaphoreType.DMA, pltpu.SemaphoreType.DMA((2,)),
        ]
        + 2 * (exchange_scratch(cotangent.shape[0]) if shared else []),
        compiler_params=pltpu.CompilerParams(
            vmem_limit_bytes=63 << 20,
            collective_id=2 if shared else None,
            has_side_effects=shared,
        ),
        name="feed_forward",
        cost_estimate=pl.CostEstimate(
            flops=6 * S * D * (D + 2 * FF), bytes_accessed=30 << 20, transcendentals=2 * S * FF
        ),
    )(attended, attend_t, wide, up_shift.reshape(1, FF), x, cotangent, up, down_t)


def fitting(shards, own):
    return own == 1 and lax.axis_size("ctx") == 4 and lax.axis_size("tp") == 2 and shards["up"].shape[0] % 16 == 0


def gather_plain(shards):
    wholes = {}
    for name in ARRAYS:
        axis = 1 if name == "project" else 0
        part = lax.all_gather(shards[name], ROWS, axis=axis)
        if name != "vectors":
            part = lax.all_gather(part, "tp", axis=axis + 2, tiled=True)
        wholes[name] = part
    return wholes


def scatter_plain(grads):
    shards = {}
    for name in ARRAYS:
        axis = 1 if name == "project" else 0
        part = grads[name]
        if name == "vectors":
            part = lax.psum(part, "tp")
        else:
            part = lax.psum_scatter(part, "tp", scatter_dimension=axis + 2, tiled=True)
        part = lax.psum_scatter(part, ROWS, scatter_dimension=axis, tiled=False)
        shards[name] = part.astype(jnp.float32)
    return shards


def local(
    tokens, project_weight, attend_weight, up_weight, down_weight, project_bias, attend_bias,
    up_bias, down_bias, first_gain, first_shift, second_gain, second_shift, segment_ids, padding,
    cotangent,
):
    seq_count = tokens.shape[0]
    members = lax.axis_size("ctx") * lax.axis_size("tp")
    own = seq_count // members
    rank = lax.axis_index("ctx") * lax.axis_size("tp") + lax.axis_index("tp")
    pieces = lax.axis_size("shard") * lax.axis_size("ctx")
    depth = D // pieces

    def to_sequences(array):
        parts = array.reshape((members, own) + array.shape[1:])
        parts = lax.all_to_all(parts, SEQ, 0, 0, tiled=True)
        return jnp.swapaxes(parts, 0, 1).reshape(own, S, D)

    def to_blocks(array):
        parts = jnp.swapaxes(array.reshape(own, members, S // members, D), 0, 1)
        return lax.all_to_all(parts, SEQ, 0, 0, tiled=True).reshape(tokens.shape)

    segments = lax.dynamic_slice_in_dim(segment_ids, rank * own, own, 0)
    pads = lax.dynamic_slice_in_dim(padding, rank * own, own, 0)

    vectors = jnp.concatenate(
        [
            project_bias,
            attend_bias[None],
            down_bias[None],
            first_gain[None],
            first_shift[None],
            second_gain[None],
            second_shift[None],
            up_bias.reshape(FF // D, depth),
        ],
        axis=0,
    )
    shards = {
        "project": jnp.transpose(project_weight, (1, 0, 2)),
        "up": up_weight,
        "down": jnp.transpose(down_weight),
        "attend": jnp.transpose(attend_weight),
        "vectors": jnp.pad(vectors, ((0, 3), (0, LANES - depth))),
    }
    custom = fitting(shards, own)
    tables = mask_tables(segments, pads)
    cosine, sine = angles()
    if custom:
        *saved, wide, x, wholes = gather_attend(
            shards, tokens, cosine, sine, *[table[0] for table in tables]
        )
        query, key, value, attended, level, x = [array[None] for array in saved + [x]]
    else:
        wholes, x = gather_plain(shards), to_sequences(tokens)
    vectors = wholes["vectors"][:, :13, :depth].astype(jnp.float32)
    up_shift = vectors[:, 9:].reshape(FF)
    project = wholes["project"].reshape(3, D, D)
    up = wholes["up"].reshape(D, FF)
    down_t = wholes["down"].reshape(D, FF)
    attend_t = wholes["attend"].reshape(D, D)
    if not custom:
        wide = jnp.transpose(vectors[:, :9], (1, 0, 2)).reshape(9, D)
        wide = jnp.pad(wide, ((0, 7), (0, 0)))
        query, key, value, attended, level = attend(x, project, wide, cosine, sine, *tables)
    params = (attend_t, up, down_t, wide, up_shift)
    if custom:
        parts = [feed_forward(attended[0], x[0], cotangent, *params, shared=True)]
    else:
        incoming = to_sequences(cotangent)
        parts = [feed_forward(attended[i], x[i], incoming[i], *params) for i in range(own)]
    attended_grad = jnp.stack([part[0] for part in parts])
    branch_grad = jnp.stack([part[1] for part in parts])
    sums = sum(part[2] for part in parts)
    up_bias_grad = sum(part[3] for part in parts)
    output = parts[0][4] if custom else to_blocks(jnp.stack([part[4] for part in parts]))
    up_grad, down_grad, attend_grad = (
        parts[0][k] if own == 1 else sum(part[k].astype(jnp.float32) for part in parts).astype(jnp.bfloat16)
        for k in (5, 6, 7)
    )
    tokens_grad, project_grad, project_bias_grad = attend_back(
        query, key, value, attended, attended_grad, level, cosine, sine, *tables, x, branch_grad,
        project,
    )
    project_bias_grad = jnp.sum(project_bias_grad, axis=0)
    if own == 1:
        project_grad = project_grad[0]
    else:
        project_grad = jnp.sum(project_grad.astype(jnp.float32), axis=0).astype(jnp.bfloat16)
    sums = jnp.concatenate([project_bias_grad, sums], axis=0)
    sums = jnp.concatenate(
        [
            jnp.transpose(sums.reshape(9, pieces, depth), (1, 0, 2)),
            up_bias_grad.reshape(pieces, FF // D, depth),
        ],
        axis=1,
    )
    grads = {
        "project": project_grad.reshape(3, pieces, depth, D),
        "up": up_grad.reshape(pieces, depth, FF),
        "down": down_grad.reshape(pieces, depth, FF),
        "attend": attend_grad.reshape(pieces, depth, D),
        "vectors": jnp.pad(sums, ((0, 0), (0, 3), (0, LANES - depth))),
    }
    if custom:
        shards, tokens_grad = scatter_grads(grads, tokens_grad.reshape(tokens.shape))
    else:
        shards, tokens_grad = scatter_plain(grads), to_blocks(tokens_grad)
    sums = shards["vectors"][:13, :depth]
    return (
        output,
        tokens_grad,
        jnp.transpose(shards["project"], (1, 0, 2)),
        jnp.transpose(shards["attend"]),
        shards["up"],
        jnp.transpose(shards["down"]),
        sums[:3],
        sums[3],
        sums[9:].reshape(-1),
        sums[4],
        sums[5],
        sums[6],
        sums[7],
        sums[8],
    )


def solution(mesh):
    in_specs = (
        P("shard", ("ctx", "tp"), None),
        P(("shard", "ctx"), None, "tp"),
        P("tp", ("shard", "ctx")),
        P(("shard", "ctx"), "tp"),
        P("tp", ("shard", "ctx")),
        P(None, ("shard", "ctx")),
        P(("shard", "ctx")),
        P(("shard", "ctx")),
        P(("shard", "ctx")),
        P(("shard", "ctx")),
        P(("shard", "ctx")),
        P(("shard", "ctx")),
        P(("shard", "ctx")),
        P("shard", None),
        P("shard", None),
        P("shard", ("ctx", "tp"), None),
    )
    out_specs = (
        P("shard", ("ctx", "tp"), None),
        P("shard", ("ctx", "tp"), None),
        P(("shard", "ctx"), None, "tp"),
        P("tp", ("shard", "ctx")),
        P(("shard", "ctx"), "tp"),
        P("tp", ("shard", "ctx")),
        P(None, ("shard", "ctx")),
        P(("shard", "ctx")),
        P(("shard", "ctx")),
        P(("shard", "ctx")),
        P(("shard", "ctx")),
        P(("shard", "ctx")),
        P(("shard", "ctx")),
        P(("shard", "ctx")),
    )
    return jax.shard_map(local, mesh=mesh, in_specs=in_specs, out_specs=out_specs, check_vma=False)
```

```python
import functools
import math

import jax
import jax.numpy as jnp
from jax import lax
from jax.experimental import pallas as pl
from jax.experimental.pallas import tpu as pltpu
from jax.sharding import PartitionSpec as P

D = 768
HEADS = 12
HEAD_DIM = 64
FF = 3072
S = 1024
LANES = 128
PAIRS = HEADS // 2
Q_ROWS = 128
LONGEST = 512
NARROW = 768

HALF = D // 2
PACKED = 3 * HALF + LANES
RISE = FF // 2
UPPER = RISE + HALF

norm_eps = 1e-12
mask_fill = -1000000000.0

NT = (((1,), (1,)), ((), ()))
TN = (((0,), (0,)), ((), ()))
NN = (((1,), (0,)), ((), ()))


def dot(left, right, dims):
    return lax.dot_general(left, right, dims, preferred_element_type=jnp.float32)


def swap_pairs(values):
    lane = lax.broadcasted_iota(jnp.int32, values.shape, 1)
    width = values.shape[1]
    return jnp.where(
        lane % 2 == 0, -pltpu.roll(values, width - 1, 1), pltpu.roll(values, 1, 1)
    )


def stack_heads(rows):
    lane = lax.broadcasted_iota(jnp.int32, rows.shape, 1)
    zero = jnp.zeros_like(rows)
    return jnp.concatenate(
        [jnp.where(lane < HEAD_DIM, rows, zero), jnp.where(lane < HEAD_DIM, zero, rows)], axis=0
    )


def pick_heads(both):
    return jnp.concatenate([both[:HEAD_DIM, :Q_ROWS], both[HEAD_DIM:, Q_ROWS:]], axis=0)


def spread_heads(row):
    return jnp.concatenate(
        [
            jnp.broadcast_to(row[:, :Q_ROWS], (HEAD_DIM, Q_ROWS)),
            jnp.broadcast_to(row[:, Q_ROWS:], (HEAD_DIM, Q_ROWS)),
        ],
        axis=0,
    )


def mask_bias(key_code, query_low, query_high):
    keys = jnp.broadcast_to(key_code, (key_code.shape[0], Q_ROWS))
    allowed = (keys >= query_low) & (keys <= query_high)
    return jnp.where(allowed, 0.0, mask_fill)


def stack_turned(turned):
    feature = lax.broadcasted_iota(jnp.int32, turned.shape, 0)
    zero = jnp.zeros_like(turned)
    return jnp.concatenate(
        [jnp.where(feature < HEAD_DIM, turned, zero), jnp.where(feature < HEAD_DIM, zero, turned)],
        axis=1,
    )


def twice(bias):
    return jnp.concatenate([bias, bias], axis=1)


def for_blocks(body, tick=None):
    blocks = S // Q_ROWS
    reach = (LONGEST + Q_ROWS - 1) // Q_ROWS
    narrow = [i for i in range(blocks) if (i + 1 + reach) * Q_ROWS <= NARROW]
    edge = len(narrow)

    @pl.loop(0, 2 * edge)
    def _(step):
        if tick is not None:
            tick(step)
        late = (step >= edge).astype(jnp.int32)
        block = step + late * (blocks - 2 * edge)
        body(block, pl.multiple_of(late * (S - NARROW), Q_ROWS), NARROW)

    @pl.loop(edge, blocks - edge)
    def _(block):
        if tick is not None:
            tick(block + edge)
        body(block, 0, S)


def packed(part, half):
    first = half * PACKED + part * HALF
    return slice(first, first + HALF)


def packed_weight(w_ref, part, half):
    return w_ref[..., packed(part, half)].reshape(D, HALF)


def project_rows(x_ref, w_ref, b_ref, cos_ref, sin_ref, q_ref, k_ref, v_ref):
    row_tile = 512

    @pl.loop(0, S // row_tile)
    def _(tile):
        rows = pl.ds(pl.multiple_of(tile * row_tile, row_tile), row_tile)
        x = x_ref[rows, :]
        cosine = cos_ref[rows, :]
        sine = sin_ref[rows, :]
        for part, out in enumerate((q_ref, k_ref, v_ref)):
            for pair in range(PAIRS):
                lanes = slice(pair * LANES, (pair + 1) * LANES)
                half, place = divmod(pair, PAIRS // 2)
                if place == 0:
                    joint = dot(x, packed_weight(w_ref, part, half), NN)
                piece = joint[:, place * LANES : (place + 1) * LANES] + b_ref[pl.ds(part, 1), lanes]
                if part < 2:
                    piece = piece * cosine + swap_pairs(piece) * sine
                if part == 0:
                    piece = piece.astype(jnp.bfloat16) * jnp.asarray(HEAD_DIM**-0.5, jnp.bfloat16)
                out[rows, lanes] = piece.astype(jnp.bfloat16)


def attend_kernel(
    x_ref, w_ref, b_ref, cos_ref, sin_ref, code_ref, low_ref, high_ref,
    q_ref, k_ref, v_ref, o_ref, lse_ref, *scratch,
):
    project_rows(x_ref, w_ref, b_ref, cos_ref, sin_ref, q_ref, k_ref, v_ref)
    attend_blocks(q_ref, k_ref, v_ref, o_ref, lse_ref, code_ref, low_ref, high_ref, *scratch)


def attend_scratch():
    return [
        pltpu.VMEM((D, S), jnp.bfloat16),
        pltpu.VMEM((D, S), jnp.bfloat16),
        pltpu.VMEM((S, Q_ROWS), jnp.float32),
        pltpu.VMEM((2, S, 2 * Q_ROWS), jnp.float32),
        pltpu.VMEM((2, S, 2 * Q_ROWS), jnp.bfloat16),
    ]


def attend_blocks(
    q_ref, k_ref, v_ref, o_ref, lse_ref, code_ref, low_ref, high_ref, q_turned, v_turned, bias, scores,
    probs, tick=None,
):
    q_turned[...] = jnp.transpose(q_ref[...])
    v_turned[...] = jnp.transpose(v_ref[...])

    def attend_block(block, first, count):
        rows = pl.ds(pl.multiple_of(block * Q_ROWS, Q_ROWS), Q_ROWS)
        keys = pl.ds(first, count)
        bias[:count] = mask_bias(code_ref[keys, :], low_ref[:, rows], high_ref[:, rows])
        tops = {}

        def score(pair):
            lanes = slice(pair * LANES, (pair + 1) * LANES)
            raw = dot(k_ref[keys, lanes], stack_turned(q_turned[lanes, rows]), NN)
            raw = raw + twice(bias[:count])
            scores[pair % 2, :count] = raw
            tops[pair] = jnp.max(raw, axis=0, keepdims=True)

        def mix(pair):
            lanes = slice(pair * LANES, (pair + 1) * LANES)
            expo = jnp.exp(scores[pair % 2, :count] - tops[pair])
            probs[pair % 2, :count] = expo.astype(jnp.bfloat16)
            total = jnp.sum(expo, axis=0, keepdims=True)
            mixed = dot(v_turned[lanes, keys], probs[pair % 2, :count], NN)
            out = pick_heads(mixed) / spread_heads(total)
            o_ref[rows, lanes] = jnp.transpose(out).astype(jnp.bfloat16)
            lse = tops[pair] + jnp.log(total)
            lse_ref[pl.ds(2 * pair, 1), rows] = lse[:, :Q_ROWS]
            lse_ref[pl.ds(2 * pair + 1, 1), rows] = lse[:, Q_ROWS:]

        score(0)
        for pair in range(PAIRS):
            if pair + 1 < PAIRS:
                score(pair + 1)
            mix(pair)

    for_blocks(attend_block, tick)


def attend_back_kernel(
    q_ref, k_ref, v_ref, o_ref, g_ref, lse_ref, cos_ref, sin_ref, code_ref, low_ref, high_ref,
    x_hbm, branch_hbm, w_hbm, given_ref, *rest,
):
    own = pl.program_id(0)
    attend_back_body(
        q_ref, k_ref, v_ref, o_ref, g_ref, lse_ref, cos_ref, sin_ref, code_ref, low_ref, high_ref,
        x_hbm.at[own], branch_hbm.at[own], w_hbm, given_ref, *rest,
    )


def attend_back_scratch():
    return [
        pltpu.VMEM((S, 3 * D), jnp.bfloat16),
        pltpu.VMEM((S, D), jnp.float32),
        pltpu.VMEM((S, D), jnp.float32),
        pltpu.VMEM((D, S), jnp.bfloat16),
        pltpu.VMEM((D, S), jnp.bfloat16),
        pltpu.VMEM((D, S), jnp.bfloat16),
        pltpu.VMEM((S, Q_ROWS), jnp.float32),
        pltpu.VMEM((2, S, 2 * Q_ROWS), jnp.bfloat16),
        pltpu.VMEM((2, S, 2 * Q_ROWS), jnp.bfloat16),
        pltpu.VMEM((S, D), jnp.bfloat16),
        pltpu.VMEM((S, D), jnp.bfloat16),
        pltpu.VMEM((D, 2 * PACKED), jnp.bfloat16),
        pltpu.VMEM((8, 3 * D), jnp.float32),
        pltpu.VMEM((LANES, D), jnp.float32),
        pltpu.SemaphoreType.DMA((3,)),
    ]


def attend_back_body(
    q_ref, k_ref, v_ref, o_ref, g_ref, lse_ref, cos_ref, sin_ref, code_ref, low_ref, high_ref,
    x_hbm, branch_hbm, w_hbm, given_ref, token_ref, weight_ref,
    joint_ref, keys_acc, values_acc, q_turned, k_turned, g_turned, bias, probs, score_grads,
    x_ref, branch_ref, w_ref, sums, vectors, sem, tick=None, after=None,
):
    loads = [
        pltpu.make_async_copy(source, target, sem.at[i])
        for i, (source, target) in enumerate(
            ((x_hbm, x_ref), (branch_hbm, branch_ref), (w_hbm, w_ref))
        )
    ]
    for load in loads:
        load.start()
    sums[...] = jnp.zeros_like(sums)
    keys_acc[...] = jnp.zeros_like(keys_acc)
    values_acc[...] = jnp.zeros_like(values_acc)
    q_turned[...] = jnp.transpose(q_ref[...])
    k_turned[...] = jnp.transpose(k_ref[...])
    g_turned[...] = jnp.transpose(g_ref[...])

    def keep(rows, lanes, grad):
        low = grad.astype(jnp.bfloat16)
        joint_ref[rows, lanes] = low
        sums[:, lanes] += jnp.sum(low.astype(jnp.float32).reshape(Q_ROWS // 8, 8, LANES), axis=0)

    def back_block(block, first, count):
        rows = pl.ds(pl.multiple_of(block * Q_ROWS, Q_ROWS), Q_ROWS)
        keys = pl.ds(first, count)
        bias[:count] = mask_bias(code_ref[keys, :], low_ref[:, rows], high_ref[:, rows])
        cosine = cos_ref[rows, :]
        sine = sin_ref[rows, :]

        def slopes(pair):
            lanes = slice(pair * LANES, (pair + 1) * LANES)
            both = g_turned[lanes, rows].astype(jnp.float32) * jnp.transpose(
                o_ref[rows, lanes].astype(jnp.float32)
            )
            delta = jnp.concatenate(
                [
                    jnp.sum(both[:HEAD_DIM], axis=0, keepdims=True),
                    jnp.sum(both[HEAD_DIM:], axis=0, keepdims=True),
                ],
                axis=1,
            )
            level = jnp.concatenate(
                [lse_ref[pl.ds(2 * pair, 1), rows], lse_ref[pl.ds(2 * pair + 1, 1), rows]], axis=1
            )
            raw = dot(k_ref[keys, lanes], stack_turned(q_turned[lanes, rows]), NN)
            prob = jnp.exp(raw + twice(bias[:count]) - level)
            prob_grad = dot(v_ref[keys, lanes], stack_turned(g_turned[lanes, rows]), NN)
            probs[pair % 2, :count] = prob.astype(jnp.bfloat16)
            score_grads[pair % 2, :count] = (prob * (prob_grad - delta)).astype(jnp.bfloat16)

        def gather(pair):
            lanes = slice(pair * LANES, (pair + 1) * LANES)
            values_acc[keys, lanes] += dot(probs[pair % 2, :count], stack_heads(g_ref[rows, lanes]), NN)
            keys_acc[keys, lanes] += dot(
                score_grads[pair % 2, :count], stack_heads(q_ref[rows, lanes]), NN
            )
            query = pick_heads(dot(k_turned[lanes, keys], score_grads[pair % 2, :count], NN))
            query = jnp.transpose(query) * (HEAD_DIM**-0.5)
            keep(rows, lanes, query * cosine - swap_pairs(query) * sine)

        slopes(0)
        for pair in range(PAIRS):
            if pair + 1 < PAIRS:
                slopes(pair + 1)
            gather(pair)

    for_blocks(back_block, tick)
    if after is not None:
        after()

    @pl.loop(0, S // Q_ROWS)
    def _(block):
        rows = pl.ds(pl.multiple_of(block * Q_ROWS, Q_ROWS), Q_ROWS)
        cosine = cos_ref[rows, :]
        sine = sin_ref[rows, :]
        for pair in range(PAIRS):
            lanes = slice(pair * LANES, (pair + 1) * LANES)
            key = keys_acc[rows, lanes]
            keep(
                rows,
                slice(D + pair * LANES, D + (pair + 1) * LANES),
                key * cosine - swap_pairs(key) * sine,
            )
            keep(
                rows,
                slice(2 * D + pair * LANES, 2 * D + (pair + 1) * LANES),
                values_acc[rows, lanes],
            )

    for load in loads:
        load.wait()
    q_turned[...] = jnp.transpose(x_ref[...])
    vectors[...] = jnp.zeros_like(vectors)
    vectors[: given_ref.shape[0], :] = given_ref[...]
    for part in range(3):
        columns = slice(part * D, (part + 1) * D)
        vectors[pl.ds(part, 1), :] = jnp.sum(sums[:, columns], axis=0, keepdims=True)
        for half in range(2):
            grad = joint_ref[:, part * D + half * HALF : part * D + (half + 1) * HALF]
            weight_ref[:, packed(part, half)] = dot(q_turned[...], grad, NN).astype(jnp.bfloat16)
    turned = jnp.transpose(vectors[...]).astype(jnp.bfloat16)
    for half in range(2):
        weight_ref[:, half * PACKED + 3 * HALF : (half + 1) * PACKED] = turned

    @pl.loop(0, 2)
    def _(half):
        rows = pl.ds(pl.multiple_of(half * (S // 2), S // 2), S // 2)
        total = branch_ref[rows, :].astype(jnp.float32)
        for part in range(3):
            for side in range(2):
                first = part * D + side * HALF
                total += dot(joint_ref[rows, first : first + HALF], w_ref[:, packed(part, side)], NT)
        token_ref[rows, :] = total.astype(jnp.bfloat16)


def whole(*shape):
    return pl.BlockSpec(shape, lambda i, *_: (0,) * len(shape))


def per(*shape):
    return pl.BlockSpec((None,) + shape, lambda i, *_: (i,) + (0,) * len(shape))


def attend(x, weight, bias, cosine, sine, code, low, high):
    own = x.shape[0]
    act = jax.ShapeDtypeStruct((own, S, D), jnp.bfloat16)
    return pl.pallas_call(
        attend_kernel,
        grid=(own,),
        in_specs=[
            per(S, D), whole(D, 2 * PACKED), whole(16, D), whole(S, LANES), whole(S, LANES),
            per(S, 1), per(1, S), per(1, S),
        ],
        out_specs=[per(S, D), per(S, D), per(S, D), per(S, D), per(HEADS, S)],
        scratch_shapes=attend_scratch(),
        out_shape=[act, act, act, act, jax.ShapeDtypeStruct((own, HEADS, S), jnp.float32)],
        compiler_params=pltpu.CompilerParams(vmem_limit_bytes=60 << 20),
        name="attend",
        cost_estimate=pl.CostEstimate(flops=6 * 10**9, bytes_accessed=12 << 20, transcendentals=6 << 20),
    )(x, weight, bias, cosine, sine, code, low, high)


def attend_back(q, k, v, o, g, lse, cosine, sine, code, low, high, x, branch_grad, weight, given):
    own = q.shape[0]
    hbm = pl.BlockSpec(memory_space=pl.ANY)
    return pl.pallas_call(
        attend_back_kernel,
        grid=(own,),
        in_specs=[
            per(S, D), per(S, D), per(S, D), per(S, D), per(S, D), per(HEADS, S),
            whole(S, LANES), whole(S, LANES), per(S, 1), per(1, S), per(1, S), hbm, hbm, hbm,
            per(16, D),
        ],
        out_specs=[per(S, D), per(D, 2 * PACKED)],
        scratch_shapes=attend_back_scratch(),
        out_shape=[
            jax.ShapeDtypeStruct((own, S, D), jnp.bfloat16),
            jax.ShapeDtypeStruct((own, D, 2 * PACKED), jnp.bfloat16),
        ],
        compiler_params=pltpu.CompilerParams(vmem_limit_bytes=60 << 20),
        name="attend_back",
        cost_estimate=pl.CostEstimate(flops=19 * 10**9, bytes_accessed=24 << 20, transcendentals=6 << 20),
    )(q, k, v, o, g, lse, cosine, sine, code, low, high, x, branch_grad, weight, given)


def mask_tables(segments, padding):
    code = 2 * segments + padding
    low = code
    high = 2 * segments + 1
    return code[:, :, None], low[:, None, :], high[:, None, :]


def angles():
    position = jnp.arange(S, dtype=jnp.int32).astype(jnp.float32)
    column = jnp.arange(LANES, dtype=jnp.int32) % HEAD_DIM // 2
    rate = jnp.exp(column.astype(jnp.float32) * (-2.0 * math.log(10000.0) / HEAD_DIM))
    phase = position[:, None] * rate[None, :]
    return jnp.cos(phase), jnp.sin(phase)


MESH = pl.DeviceIdType.MESH
ROWS = ("shard", "ctx")
EVERY = ("shard", "ctx", "tp")
SEQ = ("ctx", "tp")

BULK = ("upper", "down")
ITEMS = ("project",) + BULK
ROUTES = {"project": "zyx", "upper": "xyz", "down": "zxy"}
BEFORE = (('upper', None, 0), ('project', 1, None), ('project', 2, None), ('down', 1, None), ('project', 3, None), ('upper', None, 1), ('project', 4, None), ('down', 2, None), ('project', 5, None))
DURING = ((0, 'upper', None, 2), (1, 'down', 3, None), (4, 'down', 4, None))
AFTER = (('down', 5, None), ('upper', None, 3))
SUM_ROUTES = {"project": "xyz", "upper": "zyx", "down": "xzy"}


def places(depth):
    steps = [0]
    for k in range(1, depth):
        steps += [k, -k]
    return [(k, dy, dx) for k in steps for dy in (0, 1) for dx in (0, 1)]


def hops(place):
    return abs(place[0]) + place[1] + place[2]


def links(route, place, depth):
    apart = {"z": place[0] != 0, "y": place[1], "x": place[2]}
    level = max([i for i, axis in enumerate(route) if apart[axis]], default=-1)
    sign = (place[0] > 0) - (place[0] < 0)
    onward = []
    if level >= 0 and route[level] == "z" and abs(place[0]) + 1 < depth:
        onward.append(("z", -sign))
    for axis in route[level + 1 :]:
        onward += [("z", 1), ("z", -1)] if axis == "z" else [(axis, 1)]
    back = None if level < 0 else (route[level], sign if route[level] == "z" else 1)
    return back, onward


def seen_from(place, link):
    k, dy, dx = place
    axis, way = link
    return {"z": (k - way, dy, dx), "y": (k, 1 - dy, dx), "x": (k, dy, 1 - dx)}[axis]


class Here:
    def __init__(self):
        self.depth = lax.axis_size("shard")
        self.z = lax.axis_index("shard")
        self.c = lax.axis_index("ctx")
        self.t = lax.axis_index("tp")
        self.y = self.c // 2
        self.x = self.c % 2
        self.sides = lax.axis_size("tp")
        self.members = lax.axis_size("ctx") * self.sides
        self.rank = self.c * self.sides + self.t

    def rank_of(self, offset):
        return (self.rank + offset) % self.members

    def member(self, offset):
        rank = self.rank_of(offset)
        return (self.z, rank // self.sides, rank % self.sides)

    def device(self, link):
        axis, way = link
        if axis == "z":
            return (self.z + way, self.c, self.t)
        if axis == "y":
            return (self.z, 2 * (1 - self.y) + self.x, self.t)
        if axis == "x":
            return (self.z, 2 * self.y + (1 - self.x), self.t)
        return (self.z, self.c, 1 - self.t)

    def piece(self, place):
        k, dy, dx = place
        y = 1 - self.y if dy else self.y
        x = 1 - self.x if dx else self.x
        return (self.z + k) * 4 + 2 * y + x

    def inside(self, way):
        if way == 0:
            return None
        return self.z + way < self.depth if way > 0 else self.z + way >= 0

    def meet(self):
        barrier = pltpu.get_barrier_semaphore()
        for offset in range(1, self.members):
            pl.semaphore_signal(
                barrier, inc=1, device_id=self.member(offset), device_id_type=MESH
            )
        for way in (1, -1):

            @pl.when(self.inside(way))
            def _():
                pl.semaphore_signal(
                    barrier, inc=1, device_id=self.device(("z", way)), device_id_type=MESH
                )

        above = (self.z < self.depth - 1).astype(jnp.int32)
        below = (self.z > 0).astype(jnp.int32)
        pl.semaphore_wait(barrier, self.members - 1 + above + below)


class Exchange:
    def __init__(self, here, source, target, send_sem, recv_sem, own_sem):
        self.here, self.source, self.target = here, source, target
        self.send_sem, self.recv_sem, self.own_sem = send_sem, recv_sem, own_sem

    def block(self, ref, index):
        return ref.at[index] if len(ref.shape) == 3 else ref.at[rows_of(index)]

    def copy(self, offset):
        here = self.here
        return pltpu.make_async_remote_copy(
            src_ref=self.block(self.source, here.rank_of(offset)),
            dst_ref=self.block(self.target, here.rank),
            send_sem=self.send_sem.at[offset],
            recv_sem=self.recv_sem.at[offset],
            device_id=here.member(offset),
            device_id_type=MESH,
        )

    def arrival(self, offset):
        here = self.here
        landed = self.block(self.target, here.rank_of(here.members - offset))
        return pltpu.make_async_remote_copy(
            src_ref=landed,
            dst_ref=landed,
            send_sem=self.send_sem.at[offset],
            recv_sem=self.recv_sem.at[offset],
            device_id=here.member(offset),
            device_id_type=MESH,
        )

    def own(self):
        rank = self.here.rank
        return pltpu.make_async_copy(
            self.block(self.source, rank), self.block(self.target, rank), self.own_sem
        )

    def start(self):
        for offset in range(1, self.here.members):
            self.copy(offset).start()
        self.own().start()

    def receive(self):
        for offset in range(1, self.here.members):
            self.arrival(offset).wait_recv()
        self.own().wait()

    def drain(self):
        for offset in range(1, self.here.members):
            self.copy(offset).wait_send()


def rows_of(index):
    return pl.ds(pl.multiple_of(index * Q_ROWS, Q_ROWS), Q_ROWS)


def exchange_scratch(members):
    return [
        pltpu.SemaphoreType.DMA((members,)),
        pltpu.SemaphoreType.DMA((members,)),
        pltpu.SemaphoreType.DMA,
    ]


def guarded(condition, action):
    if condition is None:
        action()
    else:
        pl.when(condition)(action)


def columns(half, width):
    return pl.ds(pl.multiple_of(half * width, LANES), width)


def block_of(name, refs, piece, half, widths):
    return refs[name].at[piece, :, columns(half, widths[name])]


def gather_attend_kernel(
    widths, chip_count, project_hbm, upper_hbm, down_hbm, tokens_hbm,
    cos_ref, sin_ref, code_ref, low_ref, high_ref,
    q_ref, k_ref, v_ref, o_ref, lse_ref, wide_ref, project_out, x_out, upper_out, down_out,
    x_ref, w_ref, q_turned, v_turned, bias, scores, probs,
    send_sem, recv_sem, side_send, side_recv, own_sem, keep_sem, *exchange_sems,
):
    shards = dict(zip(ITEMS, (project_hbm, upper_hbm, down_hbm)))
    wholes = dict(zip(ITEMS, (w_ref, upper_out, down_out)))
    here = Here()
    tokens = Exchange(here, tokens_hbm, x_ref, *exchange_sems)
    spots = places(chip_count)
    order = sorted(spots, key=hops)
    home = (0, 0, 0)
    slot = {}
    for name in ITEMS:
        for place in spots:
            for link in links(ROUTES[name], place, chip_count)[1]:
                slot[name, place, link] = len(slot)

    def block(name, place, half):
        return block_of(name, wholes, here.piece(place), half, widths)

    def source(name, place, half):
        return shards[name] if place == home else block(name, place, half)

    def send(name, place, link):
        return pltpu.make_async_remote_copy(
            src_ref=source(name, place, here.t),
            dst_ref=block(name, place, here.t),
            send_sem=send_sem.at[slot[name, place, link]],
            recv_sem=recv_sem.at[ITEMS.index(name), spots.index(seen_from(place, link))],
            device_id=here.device(link),
            device_id_type=MESH,
        )

    def side(name, place, half):
        return pltpu.make_async_remote_copy(
            src_ref=source(name, place, half) if half is here.t else block(name, place, half),
            dst_ref=block(name, place, half),
            send_sem=side_send.at[ITEMS.index(name), spots.index(place)],
            recv_sem=side_recv.at[ITEMS.index(name), spots.index(place)],
            device_id=here.device(("tp", 1)),
            device_id_type=MESH,
        )

    def arrival(name, place):
        return pltpu.make_async_remote_copy(
            src_ref=block(name, place, here.t),
            dst_ref=block(name, place, here.t),
            send_sem=send_sem.at[0],
            recv_sem=recv_sem.at[ITEMS.index(name), spots.index(place)],
            device_id=here.device(("tp", 1)),
            device_id_type=MESH,
        )

    def own(name):
        return pltpu.make_async_copy(
            shards[name], block(name, home, here.t), own_sem.at[ITEMS.index(name)]
        )

    def relay(names, place):
        def pass_on():
            for name in names:
                if place != home:
                    arrival(name, place).wait_recv()
                for link in links(ROUTES[name], place, chip_count)[1]:
                    guarded(
                        here.inside(link[1]) if link[0] == "z" else None,
                        lambda name=name, link=link: send(name, place, link).start(),
                    )
                side(name, place, here.t).start()

        guarded(here.inside(place[0]), pass_on)

    def beside(names):
        for place in order:

            def wait(place=place):
                for name in names:
                    side(name, place, 1 - here.t).wait_recv()

            guarded(here.inside(place[0]), wait)

    def wave(name, far, near):
        for place in order[1:]:
            if (hops(place) == far if far is not None else abs(place[0]) == near):
                relay((name,), place)

    early = ITEMS[:1]
    here.meet()
    relay(ITEMS, home)
    tokens.start()
    for name in ITEMS:
        own(name).start()
    for stage in BEFORE:
        wave(*stage)
    own("project").wait()
    tokens.receive()
    beside(early)
    vectors = w_ref[:, :, 3 * HALF : PACKED].reshape(D, LANES).astype(jnp.float32)
    wide_ref[...] = jnp.transpose(vectors)[: wide_ref.shape[0]]
    keep = [
        pltpu.make_async_copy(w_ref, project_out, keep_sem.at[0]),
        pltpu.make_async_copy(x_ref, x_out, keep_sem.at[1]),
    ]
    for copy in keep:
        copy.start()
    project_rows(x_ref, w_ref, wide_ref, cos_ref, sin_ref, q_ref, k_ref, v_ref)

    def tick(step):
        for when, *stage in DURING:
            pl.when(step == when)(functools.partial(wave, *stage))

    attend_blocks(
        q_ref, k_ref, v_ref, o_ref, lse_ref, code_ref, low_ref, high_ref, q_turned, v_turned, bias,
        scores, probs, tick,
    )
    for stage in AFTER:
        wave(*stage)
    beside(BULK)
    for name in BULK:
        own(name).wait()
    tokens.drain()
    for copy in keep:
        copy.wait()
    for place in order:

        def finish(place=place):
            for name in ITEMS:
                side(name, place, here.t).wait_send()
                for link in links(ROUTES[name], place, chip_count)[1]:
                    guarded(
                        here.inside(link[1]) if link[0] == "z" else None,
                        lambda name=name, link=link: send(name, place, link).wait_send(),
                    )

        guarded(here.inside(place[0]), finish)


def link_count(depth):
    return sum(len(links(ROUTES[name], place, depth)[1]) for name in ITEMS for place in places(depth))


def gather_attend(shards, tokens, cosine, sine, code, low, high):
    chips, pieces = lax.axis_size("shard"), lax.axis_size("shard") * lax.axis_size("ctx")
    members = tokens.shape[0]
    widths = {name: shards[name].shape[-1] for name in ITEMS}
    depth = shards["upper"].shape[0]
    spots = len(places(chips))
    vmem, hbm = pl.BlockSpec(memory_space=pltpu.VMEM), pl.BlockSpec(memory_space=pl.ANY)

    def act(*shape):
        return jax.ShapeDtypeStruct(shape, jnp.bfloat16)

    def gathered(name):
        return act(pieces, depth, 2 * widths[name])

    per_place = pltpu.SemaphoreType.DMA((len(ITEMS), spots))
    outs = pl.pallas_call(
        functools.partial(gather_attend_kernel, widths, chips),
        out_shape=[
            act(S, D), act(S, D), act(S, D), act(S, D), jax.ShapeDtypeStruct((HEADS, S), jnp.float32),
            jax.ShapeDtypeStruct((16, D), jnp.float32), gathered("project"), act(S, D),
            gathered("upper"), gathered("down"),
        ],
        in_specs=[hbm] * 4 + [vmem] * 5,
        out_specs=[vmem] * 6 + [hbm] * 4,
        scratch_shapes=[
            pltpu.VMEM((S, D), jnp.bfloat16),
            pltpu.VMEM((pieces, depth, 2 * widths["project"]), jnp.bfloat16),
        ]
        + attend_scratch()
        + [
            pltpu.SemaphoreType.DMA((link_count(chips),)),
            per_place,
            per_place,
            per_place,
            pltpu.SemaphoreType.DMA((len(ITEMS),)),
            pltpu.SemaphoreType.DMA((2,)),
        ]
        + exchange_scratch(members),
        compiler_params=pltpu.CompilerParams(
            collective_id=0, has_side_effects=True, vmem_limit_bytes=60 << 20
        ),
        name="gather_attend",
    )(*[shards[name] for name in ITEMS], tokens, cosine, sine, code, low, high)
    query, key, value, attended, level, wide, project, x, upper, down = outs
    return query, key, value, attended, level, wide, x, dict(project=project, upper=upper, down=down)


def add_into(target, addend):
    height = 16

    @pl.loop(0, target.shape[0] // height)
    def _(step):
        rows = pl.ds(pl.multiple_of(step * height, height), height)
        total = target[rows, :].astype(jnp.float32) + addend[rows, :].astype(jnp.float32)
        target[rows, :] = total.astype(target.dtype)


class Sums:
    def __init__(self, here, names, routes, chip_count, widths, grads, mine, theirs, inbox, sems):
        self.here, self.names, self.routes, self.chip_count = here, names, routes, chip_count
        self.widths, self.grads, self.mine, self.theirs, self.inbox = widths, grads, mine, theirs, inbox
        self.load_sem, self.side_send, self.side_recv, self.send_sem, self.recv_sem = sems
        self.spots = places(chip_count)
        self.order = sorted(self.spots, key=hops, reverse=True)
        self.slot, self.box = {}, {}
        for name in names:
            local = 0
            for place in self.spots:
                for link in links(routes[name], place, chip_count)[1]:
                    self.slot[name, place, link] = len(self.slot)
                    self.box[name, place, link] = local
                    local += 1

    def at(self, name, place):
        return self.names.index(name), self.spots.index(place)

    def total(self, name, place):
        return self.mine[name].at[self.here.piece(place)]

    def other(self, name, place):
        return self.theirs[name].at[self.here.piece(place)]

    def load(self, name, place):
        source = block_of(name, self.grads, self.here.piece(place), self.here.t, self.widths)
        return pltpu.make_async_copy(
            source, self.total(name, place), self.load_sem.at[self.at(name, place)]
        )

    def side(self, name, place):
        here = self.here
        return pltpu.make_async_remote_copy(
            src_ref=block_of(name, self.grads, here.piece(place), 1 - here.t, self.widths),
            dst_ref=self.other(name, place),
            send_sem=self.side_send.at[self.at(name, place)],
            recv_sem=self.side_recv.at[self.at(name, place)],
            device_id=here.device(("tp", 1)),
            device_id_type=MESH,
        )

    def send(self, name, place, link):
        there = seen_from(place, link)
        back = (link[0], -link[1]) if link[0] == "z" else link
        return pltpu.make_async_remote_copy(
            src_ref=self.total(name, place),
            dst_ref=self.inbox[name].at[self.box[name, there, back]],
            send_sem=self.send_sem.at[self.at(name, place)],
            recv_sem=self.recv_sem.at[self.slot[name, there, back]],
            device_id=self.here.device(link),
            device_id_type=MESH,
        )

    def arrival(self, name, place, link):
        landed = self.inbox[name].at[self.box[name, place, link]]
        return pltpu.make_async_remote_copy(
            src_ref=landed,
            dst_ref=landed,
            send_sem=self.send_sem.at[0, 0],
            recv_sem=self.recv_sem.at[self.slot[name, place, link]],
            device_id=self.here.device(link),
            device_id_type=MESH,
        )

    def start(self):
        for place in self.order:

            def begin(place=place):
                for name in self.names:
                    self.side(name, place).start()
                    self.load(name, place).start()

            guarded(self.here.inside(place[0]), begin)

    def settle(self, distance):
        for place in self.order:
            if hops(place) != distance:
                continue

            def work(place=place):
                for name in self.names:
                    back, onward = links(self.routes[name], place, self.chip_count)
                    total = self.total(name, place)
                    self.load(name, place).wait()
                    self.side(name, place).wait_recv()
                    add_into(total, self.other(name, place))
                    for link in onward:

                        def take(link=link):
                            self.arrival(name, place, link).wait_recv()
                            add_into(total, self.inbox[name].at[self.box[name, place, link]])

                        guarded(self.here.inside(link[1]) if link[0] == "z" else None, take)
                    if back is not None:
                        self.send(name, place, back).start()

            guarded(self.here.inside(place[0]), work)

    def result(self, name):
        return self.total(name, (0, 0, 0))[...].astype(jnp.float32)

    def drain(self):
        for place in self.order:

            def finish(place=place):
                for name in self.names:
                    back, _ = links(self.routes[name], place, self.chip_count)
                    self.side(name, place).wait_send()
                    if back is not None:
                        self.send(name, place, back).wait_send()

            guarded(self.here.inside(place[0]), finish)


def sums_scratch(names, routes, chips, pieces, blocks, kinds):
    spots = places(chips)
    boxes = [sum(len(links(routes[name], place, chips)[1]) for place in spots) for name in names]
    per_place = pltpu.SemaphoreType.DMA((len(names), len(spots)))
    return (
        [pltpu.VMEM((pieces,) + block, kind) for block, kind in zip(blocks, kinds)] * 2
        + [pltpu.VMEM((box,) + block, kind) for box, block, kind in zip(boxes, blocks, kinds)]
        + [per_place] * 4
        + [pltpu.SemaphoreType.DMA((sum(boxes),))]
    )


def sums_of(here, names, routes, chip_count, widths, grads, refs):
    count = len(names)
    groups = [dict(zip(names, refs[i * count : (i + 1) * count])) for i in range(3)]
    return Sums(here, names, routes, chip_count, widths, grads, *groups, refs[3 * count :])


def back_scatter_kernel(
    widths, chip_count, *refs,
):
    body, bulk, outs = refs[:15], refs[15:17], refs[17:21]
    scratch = len(attend_back_scratch())
    local, rest = refs[21 : 21 + scratch], refs[21 + scratch :]
    here = Here()
    grads = dict(zip(BULK, bulk))
    sums = sums_of(here, BULK, SUM_ROUTES, chip_count, widths, grads, rest)
    here.meet()
    sums.start()
    farthest = max(hops(place) for place in sums.spots)
    steps = (0, 1, 2, 4, 6)

    def tick(step):
        for i, when in enumerate(steps):
            pl.when(step == when)(functools.partial(sums.settle, farthest - i))

    def after():
        for distance in range(farthest - len(steps), 0, -1):
            sums.settle(distance)

    attend_back_body(*body, *outs[:2], *local, tick=tick, after=after)
    sums.settle(0)
    for name, out in zip(BULK, outs[2:]):
        out[...] = sums.result(name)
    sums.drain()


def back_scatter(q, k, v, o, g, lse, cosine, sine, code, low, high, x, branch_grad, weight, given, grads):
    chips, pieces = lax.axis_size("shard"), lax.axis_size("shard") * lax.axis_size("ctx")
    vmem, hbm = pl.BlockSpec(memory_space=pltpu.VMEM), pl.BlockSpec(memory_space=pl.ANY)
    blocks = [(grads[name].shape[1], grads[name].shape[2] // 2) for name in BULK]
    widths = {name: block[-1] for name, block in zip(BULK, blocks)}
    outs = pl.pallas_call(
        functools.partial(back_scatter_kernel, widths, chips),
        out_shape=[
            jax.ShapeDtypeStruct((S, D), jnp.bfloat16),
            jax.ShapeDtypeStruct((D, 2 * PACKED), jnp.bfloat16),
        ]
        + [jax.ShapeDtypeStruct(block, jnp.float32) for block in blocks],
        in_specs=[vmem] * 11 + [hbm] * 3 + [vmem] + [hbm] * 2,
        out_specs=[vmem] * 4,
        scratch_shapes=attend_back_scratch()
        + sums_scratch(BULK, SUM_ROUTES, chips, pieces, blocks, [jnp.bfloat16] * len(BULK)),
        compiler_params=pltpu.CompilerParams(
            collective_id=3, has_side_effects=True, vmem_limit_bytes=67043328
        ),
        name="back_scatter",
    )(
        q, k, v, o, g, lse, cosine, sine, code, low, high, x, branch_grad, weight, given,
        *[grads[name] for name in BULK],
    )
    return outs[:2], dict(zip(BULK, outs[2:]))


LAST = ("project",)


def scatter_kernel(widths, chip_count, project_hbm, tokens_hbm, project_ref, tokens_out, *rest):
    here = Here()
    sums = sums_of(here, LAST, SUM_ROUTES, chip_count, widths, {"project": project_hbm}, rest[:-3])
    tokens = Exchange(here, tokens_hbm, tokens_out, *rest[-3:])
    here.meet()
    sums.start()
    farthest = max(hops(place) for place in sums.spots)
    for distance in range(farthest, -1, -1):
        sums.settle(distance)
        if distance == farthest - 1:
            tokens.start()
    project_ref[...] = sums.result("project")
    tokens.receive()
    tokens.drain()
    sums.drain()


def scatter_last(project, tokens_grad):
    chips, pieces = lax.axis_size("shard"), lax.axis_size("shard") * lax.axis_size("ctx")
    vmem, hbm = pl.BlockSpec(memory_space=pltpu.VMEM), pl.BlockSpec(memory_space=pl.ANY)
    block = (project.shape[1], project.shape[2] // 2)
    return pl.pallas_call(
        functools.partial(scatter_kernel, {"project": block[-1]}, chips),
        out_shape=[
            jax.ShapeDtypeStruct(block, jnp.float32),
            jax.ShapeDtypeStruct(tokens_grad.shape, tokens_grad.dtype),
        ],
        in_specs=[hbm] * 2,
        out_specs=[vmem, hbm],
        scratch_shapes=sums_scratch(LAST, SUM_ROUTES, chips, pieces, [block], [jnp.bfloat16])
        + exchange_scratch(tokens_grad.shape[0]),
        compiler_params=pltpu.CompilerParams(
            collective_id=1, has_side_effects=True, vmem_limit_bytes=60 << 20
        ),
        name="scatter_last",
    )(project, tokens_grad)


CHUNK = 512
STEP = 16
UNROLL = 4
ATTEND_BIAS, DOWN_BIAS, FIRST_GAIN, FIRST_SHIFT, SECOND_GAIN, SECOND_SHIFT = range(3, 9)
SUMS = 6


def row_mean(values):
    return jnp.sum(values, axis=-1, keepdims=True) * (1.0 / D)


def fold(values):
    return jnp.sum(values.reshape(values.shape[0] // 8, 8, values.shape[1]), axis=0)


def chunk_at(index):
    return pl.ds(pl.multiple_of(index * CHUNK, CHUNK), CHUNK)


def ffn_kernel(
    shared, a_ref, wide_ref, shift_ref, x_hbm, c_hbm, upper_hbm, down_hbm,
    joined_ref, branch_ref, sums_ref, up_sums_ref, out_hbm, upper_grad_hbm, down_grad_hbm,
    x_ref, c_ref, attend_ref, up_ref, down_ref, out_ref, hidden_ref, slope_ref, low_ref, ffn_ref, turned_ref,
    left, right, near, far, first, unit, acc, factor, sums, up_sums, stage, in_sem, out_sem, stage_sem,
    *exchange_sems,
):
    halves = [(half * UPPER, half * RISE, half * HALF) for half in range(2)]
    copies = [
        (upper_hbm.at[:, start + RISE : start + UPPER], attend_ref.at[:, low : low + HALF])
        for start, _, low in halves
    ]
    copies.append((x_hbm, x_ref))
    copies += [
        (upper_hbm.at[:, start : start + RISE], up_ref.at[:, rise : rise + RISE])
        for start, rise, _ in halves
    ]
    copies.append((down_hbm, down_ref))
    if not shared:
        copies.append((c_hbm, c_ref))
    loads = [
        pltpu.make_async_copy(source, target, in_sem.at[i]) for i, (source, target) in enumerate(copies)
    ]
    for load in loads:
        load.start()
    if shared:
        here = Here()
        barrier = pltpu.get_barrier_semaphore()
        for offset in range(1, here.members):
            pl.semaphore_signal(barrier, inc=1, device_id=here.member(offset), device_id_type=MESH)
        arriving = Exchange(here, c_hbm, c_ref, *exchange_sems[:3])
        leaving = Exchange(here, out_ref, out_hbm, *exchange_sems[3:])
    sums[...] = jnp.zeros_like(sums)
    up_sums[...] = jnp.zeros_like(up_sums)
    pairs = FF // CHUNK // 2

    def vector(index):
        return wide_ref[pl.ds(index, 1), :]

    def add_sum(index, values):
        sums[index - ATTEND_BIAS] += fold(values)

    def rows_loop(body):
        @pl.loop(0, S // STEP, unroll=UNROLL)
        def _(step):
            body(pl.ds(pl.multiple_of(step * STEP, STEP), STEP))

    loads[0].wait()
    loads[1].wait()
    acc[...] = dot(a_ref[...], attend_ref[...], NT)
    if shared:
        pl.semaphore_wait(barrier, here.members - 1)
        arriving.start()
    loads[2].wait()

    @rows_loop
    def _(rows):
        joined = x_ref[rows, :].astype(jnp.float32) + acc[rows, :] + vector(ATTEND_BIAS)
        centred = joined - row_mean(joined)
        scale = lax.rsqrt(row_mean(centred * centred) + norm_eps)
        normed = centred * scale
        unit[rows, :] = normed
        factor[rows, :] = scale
        result = normed * vector(FIRST_GAIN) + vector(FIRST_SHIFT)
        first[rows, :] = result
        low_ref[rows, :] = result.astype(jnp.bfloat16)

    for load in loads[3:6]:
        load.wait()

    def expand(target, index):
        target[...] = dot(low_ref[...], up_ref[:, chunk_at(index)], NN)

    def activate(source, target, index):
        pre = source[...] + shift_ref[:, chunk_at(index)]
        cumulative = 0.5 + 0.5 * lax.erf(pre * (1.0 / math.sqrt(2.0)))
        density = jnp.exp(-0.5 * pre * pre) * (1.0 / math.sqrt(2.0 * math.pi))
        hidden = (pre * cumulative).astype(jnp.bfloat16)
        target[...] = hidden
        hidden_ref[:, chunk_at(index)] = hidden
        slope_ref[:, chunk_at(index)] = (cumulative + pre * density).astype(jnp.bfloat16)

    def contract(source, index):
        acc[...] += dot(source[...], down_ref[:, chunk_at(index)], NT)

    def forward(pair, last):
        expand(right, 2 * pair + 1)
        activate(left, near, 2 * pair)
        if not last:
            expand(left, 2 * pair + 2)
        contract(near, 2 * pair)
        activate(right, far, 2 * pair + 1)
        contract(far, 2 * pair + 1)

    expand(left, 0)
    acc[...] = jnp.zeros_like(acc)

    @pl.loop(0, pairs - 1)
    def _(pair):
        forward(pair, False)

    forward(pairs - 1, True)
    if shared:
        arriving.receive()
    else:
        loads[6].wait()

    @rows_loop
    def _(rows):
        joined = first[rows, :] + acc[rows, :] + vector(DOWN_BIAS)
        centred = joined - row_mean(joined)
        scale = lax.rsqrt(row_mean(centred * centred) + norm_eps)
        normed = centred * scale
        out_ref[rows, :] = (normed * vector(SECOND_GAIN) + vector(SECOND_SHIFT)).astype(jnp.bfloat16)
        grad = c_ref[rows, :].astype(jnp.float32)
        add_sum(SECOND_GAIN, grad * normed)
        add_sum(SECOND_SHIFT, grad)
        inner = grad * vector(SECOND_GAIN)
        back = scale * (inner - row_mean(inner) - normed * row_mean(inner * normed))
        first[rows, :] = back
        low = back.astype(jnp.bfloat16)
        ffn_ref[rows, :] = low
        add_sum(DOWN_BIAS, low.astype(jnp.float32))

    if not shared:
        store = pltpu.make_async_copy(out_ref, out_hbm, out_sem)
        store.start()

    def stored(slot, target, index, spread):
        first = index * CHUNK + index // pairs * spread
        return pltpu.make_async_copy(
            stage.at[slot],
            target.at[:, pl.ds(pl.multiple_of(first, LANES), CHUNK)],
            stage_sem.at[slot],
        )

    def weight_grad(source, target, spread):
        @pl.loop(0, pairs)
        def _(pair):
            for slot in range(2):
                index = 2 * pair + slot

                @pl.when(pair > 0)
                def _():
                    stored(slot, target, index, spread).wait()

                stage[slot] = dot(turned_ref[...], source[:, chunk_at(index)], NN).astype(jnp.bfloat16)
                stored(slot, target, index, spread).start()

        for slot in range(2):
            stored(slot, target, slot, spread).wait()

    turned_ref[...] = jnp.transpose(ffn_ref[...])
    if shared:
        leaving.start()
    weight_grad(hidden_ref, down_grad_hbm, 0)

    def widen(target, index):
        target[...] = dot(ffn_ref[...], down_ref[:, chunk_at(index)], NN)

    def reweigh(source, target, index):
        grad = (source[...] * slope_ref[:, chunk_at(index)].astype(jnp.float32)).astype(jnp.bfloat16)
        target[...] = grad
        hidden_ref[:, chunk_at(index)] = grad
        up_sums[:, chunk_at(index)] += fold(grad.astype(jnp.float32))

    def collect(source, index):
        acc[...] += dot(source[...], up_ref[:, chunk_at(index)], NT)

    def backward(pair, last):
        widen(right, 2 * pair + 1)
        reweigh(left, near, 2 * pair)
        if not last:
            widen(left, 2 * pair + 2)
        collect(near, 2 * pair)
        reweigh(right, far, 2 * pair + 1)
        collect(far, 2 * pair + 1)

    widen(left, 0)
    acc[...] = jnp.zeros_like(acc)

    @pl.loop(0, pairs - 1)
    def _(pair):
        backward(pair, False)

    backward(pairs - 1, True)

    @rows_loop
    def _(rows):
        grad = first[rows, :] + acc[rows, :]
        normed = unit[rows, :]
        add_sum(FIRST_GAIN, grad * normed)
        add_sum(FIRST_SHIFT, grad)
        inner = grad * vector(FIRST_GAIN)
        back = factor[rows, :] * (inner - row_mean(inner) - normed * row_mean(inner * normed))
        low = back.astype(jnp.bfloat16)
        branch_ref[rows, :] = low
        add_sum(ATTEND_BIAS, low.astype(jnp.float32))

    joined_ref[...] = dot(branch_ref[...], attend_ref[...], NN).astype(jnp.bfloat16)
    turned_ref[...] = jnp.transpose(low_ref[...])
    weight_grad(hidden_ref, upper_grad_hbm, HALF)
    turned_ref[...] = jnp.transpose(branch_ref[...])

    def attend_stored(slot):
        first = slot * UPPER + RISE
        return pltpu.make_async_copy(
            stage.at[slot, :, :HALF], upper_grad_hbm.at[:, first : first + HALF], stage_sem.at[slot]
        )

    for slot in range(2):
        stage[slot, :, :HALF] = dot(
            turned_ref[...], a_ref[:, slot * HALF : (slot + 1) * HALF], NN
        ).astype(jnp.bfloat16)
        attend_stored(slot).start()
    for index in range(SUMS):
        sums_ref[pl.ds(index, 1), :] = jnp.sum(sums[index], axis=0, keepdims=True)
    up_sums_ref[...] = jnp.sum(up_sums[...], axis=0, keepdims=True)
    for slot in range(2):
        attend_stored(slot).wait()
    if shared:
        leaving.receive()
        arriving.drain()
        leaving.drain()
    else:
        store.wait()


def feed_forward(attended, x, cotangent, upper, down_t, wide, up_shift, shared=False):
    vmem, hbm = pl.BlockSpec(memory_space=pltpu.VMEM), pl.BlockSpec(memory_space=pl.ANY)

    def low(*shape):
        return jax.ShapeDtypeStruct(shape, jnp.bfloat16)

    def full(*shape):
        return jax.ShapeDtypeStruct(shape, jnp.float32)

    def scratch(width, kind=jnp.bfloat16):
        return pltpu.VMEM((S, width), kind)

    return pl.pallas_call(
        functools.partial(ffn_kernel, shared),
        in_specs=[vmem] * 3 + [hbm] * 4,
        out_specs=[vmem] * 4 + [hbm] * 3,
        out_shape=[
            low(S, D), low(S, D), full(SUMS, D), full(1, FF), low(*cotangent.shape),
            low(D, 2 * UPPER), low(D, FF),
        ],
        scratch_shapes=[
            scratch(D), scratch(D), pltpu.VMEM((D, D), jnp.bfloat16), pltpu.VMEM((D, FF), jnp.bfloat16),
            pltpu.VMEM((D, FF), jnp.bfloat16),
            scratch(D), scratch(FF), scratch(FF), scratch(D), scratch(D), pltpu.VMEM((D, S), jnp.bfloat16),
            scratch(CHUNK, jnp.float32), scratch(CHUNK, jnp.float32), scratch(CHUNK), scratch(CHUNK),
            scratch(D, jnp.float32), scratch(D, jnp.float32), scratch(D, jnp.float32),
            scratch(1, jnp.float32),
            pltpu.VMEM((SUMS, 8, D), jnp.float32), pltpu.VMEM((8, FF), jnp.float32),
            pltpu.VMEM((2, D, CHUNK), jnp.bfloat16),
            pltpu.SemaphoreType.DMA((7,)), pltpu.SemaphoreType.DMA, pltpu.SemaphoreType.DMA((2,)),
        ]
        + 2 * (exchange_scratch(cotangent.shape[0]) if shared else []),
        compiler_params=pltpu.CompilerParams(
            vmem_limit_bytes=63 << 20,
            collective_id=2 if shared else None,
            has_side_effects=shared,
        ),
        name="feed_forward",
        cost_estimate=pl.CostEstimate(
            flops=6 * S * D * (D + 2 * FF), bytes_accessed=30 << 20, transcendentals=2 * S * FF
        ),
    )(attended, wide, up_shift.reshape(1, FF), x, cotangent, upper, down_t)


def fitting(shards, own):
    return own == 1 and lax.axis_size("ctx") == 4 and lax.axis_size("tp") == 2 and shards["upper"].shape[0] % 16 == 0


def gather_plain(shards):
    return {
        name: lax.all_gather(
            lax.all_gather(shards[name], ROWS, axis=0), "tp", axis=2, tiled=True
        )
        for name in ITEMS
    }


def scatter_plain(grads):
    shards = {}
    for name in ITEMS:
        part = lax.psum_scatter(grads[name], "tp", scatter_dimension=2, tiled=True)
        part = lax.psum_scatter(part, ROWS, scatter_dimension=0, tiled=False)
        shards[name] = part.astype(jnp.float32)
    return shards


def local(
    tokens, project_weight, attend_weight, up_weight, down_weight, project_bias, attend_bias,
    up_bias, down_bias, first_gain, first_shift, second_gain, second_shift, segment_ids, padding,
    cotangent,
):
    seq_count = tokens.shape[0]
    members = lax.axis_size("ctx") * lax.axis_size("tp")
    own = seq_count // members
    rank = lax.axis_index("ctx") * lax.axis_size("tp") + lax.axis_index("tp")
    pieces = lax.axis_size("shard") * lax.axis_size("ctx")
    depth = D // pieces

    def to_sequences(array):
        parts = array.reshape((members, own) + array.shape[1:])
        parts = lax.all_to_all(parts, SEQ, 0, 0, tiled=True)
        return jnp.swapaxes(parts, 0, 1).reshape(own, S, D)

    def to_blocks(array):
        parts = jnp.swapaxes(array.reshape(own, members, S // members, D), 0, 1)
        return lax.all_to_all(parts, SEQ, 0, 0, tiled=True).reshape(tokens.shape)

    segments = lax.dynamic_slice_in_dim(segment_ids, rank * own, own, 0)
    pads = lax.dynamic_slice_in_dim(padding, rank * own, own, 0)

    vectors = jnp.concatenate(
        [
            project_bias,
            attend_bias[None],
            down_bias[None],
            first_gain[None],
            first_shift[None],
            second_gain[None],
            second_shift[None],
            up_bias.reshape(FF // D, depth),
        ],
        axis=0,
    )
    shards = {
        "project": jnp.concatenate(
            [
                project_weight.reshape(depth, 3 * HALF),
                jnp.pad(jnp.transpose(vectors), ((0, 0), (0, LANES - vectors.shape[0]))),
            ],
            axis=1,
        ),
        "upper": jnp.concatenate([up_weight, jnp.transpose(attend_weight)], axis=1),
        "down": jnp.transpose(down_weight),
    }
    custom = fitting(shards, own)
    tables = mask_tables(segments, pads)
    cosine, sine = angles()
    if custom:
        *saved, wide, x, wholes = gather_attend(
            shards, tokens, cosine, sine, *[table[0] for table in tables]
        )
        query, key, value, attended, level, x = [array[None] for array in saved + [x]]
    else:
        wholes, x = gather_plain(shards), to_sequences(tokens)
    project = wholes["project"].reshape(D, 2 * PACKED)
    upper = wholes["upper"].reshape(D, 2 * UPPER)
    down_t = wholes["down"].reshape(D, FF)
    if not custom:
        wide = jnp.transpose(project[:, 3 * HALF : 3 * HALF + 16]).astype(jnp.float32)
        query, key, value, attended, level = attend(x, project, wide, cosine, sine, *tables)
    up_shift = jnp.swapaxes(wide[9:13].reshape(FF // D, pieces, depth), 0, 1).reshape(FF)
    params = (upper, down_t, wide, up_shift)
    if custom:
        parts = [feed_forward(attended[0], x[0], cotangent, *params, shared=True)]
    else:
        incoming = to_sequences(cotangent)
        parts = [feed_forward(attended[i], x[i], incoming[i], *params) for i in range(own)]
    attended_grad = jnp.stack([part[0] for part in parts])
    branch_grad = jnp.stack([part[1] for part in parts])
    sums = sum(part[2] for part in parts)
    up_bias_grad = sum(part[3] for part in parts)
    output = parts[0][4] if custom else to_blocks(jnp.stack([part[4] for part in parts]))
    upper_grad, down_grad = (
        parts[0][k] if own == 1 else sum(part[k].astype(jnp.float32) for part in parts).astype(jnp.bfloat16)
        for k in (5, 6)
    )
    up_bias_grad = jnp.swapaxes(up_bias_grad.reshape(pieces, FF // D, depth), 0, 1).reshape(FF // D, D)
    given = jnp.concatenate([jnp.zeros((3, D), jnp.float32), sums, up_bias_grad, jnp.zeros((3, D), jnp.float32)])
    grads = {
        "upper": upper_grad.reshape(pieces, depth, 2 * UPPER),
        "down": down_grad.reshape(pieces, depth, FF),
    }
    inputs = (query, key, value, attended, attended_grad, level)
    if custom:
        (tokens_grad, project_grad), shards = back_scatter(
            *[array[0] for array in inputs], cosine, sine, *[table[0] for table in tables], x[0],
            branch_grad[0], project, given, grads,
        )
        shards["project"], tokens_grad = scatter_last(
            project_grad.reshape(pieces, depth, 2 * PACKED), tokens_grad.reshape(tokens.shape)
        )
    else:
        given = jnp.concatenate([given[None], jnp.zeros((own - 1,) + given.shape, jnp.float32)])
        tokens_grad, project_grad = attend_back(
            *inputs, cosine, sine, *tables, x, branch_grad, project, given
        )
        project_grad = jnp.sum(project_grad.astype(jnp.float32), axis=0).astype(jnp.bfloat16)
        grads["project"] = project_grad.reshape(pieces, depth, 2 * PACKED)
        shards, tokens_grad = scatter_plain(grads), to_blocks(tokens_grad)
    sums = jnp.transpose(shards["project"][:, 3 * HALF : 3 * HALF + 13])
    return (
        output,
        tokens_grad,
        shards["project"][:, : 3 * HALF].reshape(depth, 3, HALF),
        jnp.transpose(shards["upper"][:, RISE:]),
        shards["upper"][:, :RISE],
        jnp.transpose(shards["down"]),
        sums[:3],
        sums[3],
        sums[9:].reshape(-1),
        sums[4],
        sums[5],
        sums[6],
        sums[7],
        sums[8],
    )


def solution(mesh):
    in_specs = (
        P("shard", ("ctx", "tp"), None),
        P(("shard", "ctx"), None, "tp"),
        P("tp", ("shard", "ctx")),
        P(("shard", "ctx"), "tp"),
        P("tp", ("shard", "ctx")),
        P(None, ("shard", "ctx")),
        P(("shard", "ctx")),
        P(("shard", "ctx")),
        P(("shard", "ctx")),
        P(("shard", "ctx")),
        P(("shard", "ctx")),
        P(("shard", "ctx")),
        P(("shard", "ctx")),
        P("shard", None),
        P("shard", None),
        P("shard", ("ctx", "tp"), None),
    )
    out_specs = (
        P("shard", ("ctx", "tp"), None),
        P("shard", ("ctx", "tp"), None),
        P(("shard", "ctx"), None, "tp"),
        P("tp", ("shard", "ctx")),
        P(("shard", "ctx"), "tp"),
        P("tp", ("shard", "ctx")),
        P(None, ("shard", "ctx")),
        P(("shard", "ctx")),
        P(("shard", "ctx")),
        P(("shard", "ctx")),
        P(("shard", "ctx")),
        P(("shard", "ctx")),
        P(("shard", "ctx")),
        P(("shard", "ctx")),
    )
    return jax.shard_map(local, mesh=mesh, in_specs=in_specs, out_specs=out_specs, check_vma=False)
```

```python
import functools
import math

import jax
import jax.numpy as jnp
from jax import lax
from jax.experimental import pallas as pl
from jax.experimental.pallas import tpu as pltpu
from jax.sharding import PartitionSpec as P

D = 768
HEADS = 12
HEAD_DIM = 64
FF = 3072
S = 1024
LANES = 128
PAIRS = HEADS // 2
Q_ROWS = 128

HALF = D // 2
PACKED = 3 * HALF + LANES
RISE = FF // 2
UPPER = RISE + HALF

norm_eps = 1e-12
mask_fill = -1000000000.0

NT = (((1,), (1,)), ((), ()))
TN = (((0,), (0,)), ((), ()))
NN = (((1,), (0,)), ((), ()))


def dot(left, right, dims):
    return lax.dot_general(left, right, dims, preferred_element_type=jnp.float32)


def swap_pairs(values):
    lane = lax.broadcasted_iota(jnp.int32, values.shape, 1)
    width = values.shape[1]
    return jnp.where(
        lane % 2 == 0, -pltpu.roll(values, width - 1, 1), pltpu.roll(values, 1, 1)
    )


def turn(target, source):
    @pl.loop(0, source.shape[1] // LANES)
    def _(step):
        part = pl.ds(pl.multiple_of(step * LANES, LANES), LANES)
        target[part, :] = jnp.transpose(source[:, part])


def stack_heads(rows):
    lane = lax.broadcasted_iota(jnp.int32, rows.shape, 1)
    zero = jnp.zeros_like(rows)
    return jnp.concatenate(
        [jnp.where(lane < HEAD_DIM, rows, zero), jnp.where(lane < HEAD_DIM, zero, rows)], axis=0
    )


def pick_heads(both):
    return jnp.concatenate([both[:HEAD_DIM, :Q_ROWS], both[HEAD_DIM:, Q_ROWS:]], axis=0)


def spread_heads(row):
    return jnp.concatenate(
        [
            jnp.broadcast_to(row[:, :Q_ROWS], (HEAD_DIM, Q_ROWS)),
            jnp.broadcast_to(row[:, Q_ROWS:], (HEAD_DIM, Q_ROWS)),
        ],
        axis=0,
    )


def mask_bias(key_code, query_low, query_high):
    keys = jnp.broadcast_to(key_code, (key_code.shape[0], Q_ROWS))
    allowed = (keys >= query_low) & (keys <= query_high)
    return jnp.where(allowed, 0.0, mask_fill)


def stack_turned(turned):
    feature = lax.broadcasted_iota(jnp.int32, turned.shape, 0)
    zero = jnp.zeros_like(turned)
    return jnp.concatenate(
        [jnp.where(feature < HEAD_DIM, turned, zero), jnp.where(feature < HEAD_DIM, zero, turned)],
        axis=1,
    )


def twice(bias):
    return jnp.concatenate([bias, bias], axis=1)


def for_blocks(body, tick=None):
    @pl.loop(0, S // Q_ROWS)
    def _(block):
        if tick is not None:
            tick(block)
        body(block)


def packed(part, half):
    first = half * PACKED + part * HALF
    return slice(first, first + HALF)


def packed_weight(w_ref, part, half):
    return w_ref[..., packed(part, half)].reshape(D, HALF)


def project_rows(x_ref, w_ref, b_ref, cos_ref, sin_ref, q_ref, k_ref, v_ref):
    row_tile = 512

    @pl.loop(0, S // row_tile)
    def _(tile):
        rows = pl.ds(pl.multiple_of(tile * row_tile, row_tile), row_tile)
        x = x_ref[rows, :]
        cosine = cos_ref[rows, :]
        sine = sin_ref[rows, :]
        for part, out in enumerate((q_ref, k_ref, v_ref)):
            for pair in range(PAIRS):
                lanes = slice(pair * LANES, (pair + 1) * LANES)
                half, place = divmod(pair, PAIRS // 2)
                if place == 0:
                    joint = dot(x, packed_weight(w_ref, part, half), NN)
                piece = joint[:, place * LANES : (place + 1) * LANES] + b_ref[pl.ds(part, 1), lanes]
                if part < 2:
                    piece = piece * cosine + swap_pairs(piece) * sine
                if part == 0:
                    piece = piece.astype(jnp.bfloat16) * jnp.asarray(HEAD_DIM**-0.5, jnp.bfloat16)
                out[rows, lanes] = piece.astype(jnp.bfloat16)


def attend_kernel(
    x_ref, w_ref, b_ref, cos_ref, sin_ref, code_ref, low_ref, high_ref,
    q_ref, k_ref, v_ref, o_ref, lse_ref, *scratch,
):
    project_rows(x_ref, w_ref, b_ref, cos_ref, sin_ref, q_ref, k_ref, v_ref)
    attend_blocks(q_ref, k_ref, v_ref, o_ref, lse_ref, code_ref, low_ref, high_ref, *scratch)


def attend_scratch():
    return [
        pltpu.VMEM((D, S), jnp.bfloat16),
        pltpu.VMEM((D, S), jnp.bfloat16),
        pltpu.VMEM((S, Q_ROWS), jnp.float32),
        pltpu.VMEM((2, S, 2 * Q_ROWS), jnp.float32),
        pltpu.VMEM((2, S, 2 * Q_ROWS), jnp.bfloat16),
    ]


def attend_blocks(
    q_ref, k_ref, v_ref, o_ref, lse_ref, code_ref, low_ref, high_ref, q_turned, v_turned, bias, scores,
    probs, tick=None,
):
    turn(q_turned, q_ref)
    turn(v_turned, v_ref)

    def attend_block(block):
        rows = pl.ds(pl.multiple_of(block * Q_ROWS, Q_ROWS), Q_ROWS)
        bias[...] = mask_bias(code_ref[...], low_ref[:, rows], high_ref[:, rows])
        tops = {}

        def score(pair):
            lanes = slice(pair * LANES, (pair + 1) * LANES)
            raw = dot(k_ref[:, lanes], stack_turned(q_turned[lanes, rows]), NN)
            raw = raw + twice(bias[...])
            scores[pair % 2] = raw
            tops[pair] = jnp.max(raw, axis=0, keepdims=True)

        def mix(pair):
            lanes = slice(pair * LANES, (pair + 1) * LANES)
            expo = jnp.exp(scores[pair % 2] - tops[pair])
            probs[pair % 2] = expo.astype(jnp.bfloat16)
            total = jnp.sum(expo, axis=0, keepdims=True)
            mixed = dot(v_turned[lanes, :], probs[pair % 2], NN)
            out = pick_heads(mixed) / spread_heads(total)
            o_ref[rows, lanes] = jnp.transpose(out).astype(jnp.bfloat16)
            lse = tops[pair] + jnp.log(total)
            lse_ref[pl.ds(2 * pair, 1), rows] = lse[:, :Q_ROWS]
            lse_ref[pl.ds(2 * pair + 1, 1), rows] = lse[:, Q_ROWS:]

        score(0)
        for pair in range(PAIRS):
            if pair + 1 < PAIRS:
                score(pair + 1)
            mix(pair)

    for_blocks(attend_block, tick)


def attend_back_kernel(
    q_ref, k_ref, v_ref, o_ref, g_ref, lse_ref, cos_ref, sin_ref, code_ref, low_ref, high_ref,
    x_hbm, branch_hbm, w_hbm, given_ref, *rest,
):
    own = pl.program_id(0)
    attend_back_body(
        q_ref, k_ref, v_ref, o_ref, g_ref, lse_ref, cos_ref, sin_ref, code_ref, low_ref, high_ref,
        x_hbm.at[own], branch_hbm.at[own], w_hbm, given_ref, *rest,
    )


def attend_back_scratch():
    return [
        pltpu.VMEM((S, 3 * D), jnp.bfloat16),
        pltpu.VMEM((S, D), jnp.float32),
        pltpu.VMEM((S, D), jnp.float32),
        pltpu.VMEM((D, S), jnp.bfloat16),
        pltpu.VMEM((D, S), jnp.bfloat16),
        pltpu.VMEM((D, S), jnp.bfloat16),
        pltpu.VMEM((S, Q_ROWS), jnp.float32),
        pltpu.VMEM((2, S, 2 * Q_ROWS), jnp.bfloat16),
        pltpu.VMEM((2, S, 2 * Q_ROWS), jnp.bfloat16),
        pltpu.VMEM((S, D), jnp.bfloat16),
        pltpu.VMEM((S, D), jnp.bfloat16),
        pltpu.VMEM((D, 2 * PACKED), jnp.bfloat16),
        pltpu.VMEM((8, 3 * D), jnp.float32),
        pltpu.VMEM((LANES, D), jnp.float32),
        pltpu.SemaphoreType.DMA((3,)),
    ]


def attend_back_body(
    q_ref, k_ref, v_ref, o_ref, g_ref, lse_ref, cos_ref, sin_ref, code_ref, low_ref, high_ref,
    x_hbm, branch_hbm, w_hbm, given_ref, token_ref, weight_ref,
    joint_ref, keys_acc, values_acc, q_turned, k_turned, g_turned, bias, probs, score_grads,
    x_ref, branch_ref, w_ref, sums, vectors, sem, tick=None, after=None,
):
    loads = [
        pltpu.make_async_copy(source, target, sem.at[i])
        for i, (source, target) in enumerate(
            ((x_hbm, x_ref), (branch_hbm, branch_ref), (w_hbm, w_ref))
        )
    ]
    for load in loads:
        load.start()
    sums[...] = jnp.zeros_like(sums)
    keys_acc[...] = jnp.zeros_like(keys_acc)
    values_acc[...] = jnp.zeros_like(values_acc)
    turn(q_turned, q_ref)
    turn(k_turned, k_ref)
    turn(g_turned, g_ref)

    def keep(rows, lanes, grad):
        low = grad.astype(jnp.bfloat16)
        joint_ref[rows, lanes] = low
        sums[:, lanes] += jnp.sum(low.astype(jnp.float32).reshape(Q_ROWS // 8, 8, LANES), axis=0)

    def back_block(block):
        rows = pl.ds(pl.multiple_of(block * Q_ROWS, Q_ROWS), Q_ROWS)
        bias[...] = mask_bias(code_ref[...], low_ref[:, rows], high_ref[:, rows])
        cosine = cos_ref[rows, :]
        sine = sin_ref[rows, :]

        def slopes(pair):
            lanes = slice(pair * LANES, (pair + 1) * LANES)
            both = g_turned[lanes, rows].astype(jnp.float32) * jnp.transpose(
                o_ref[rows, lanes].astype(jnp.float32)
            )
            delta = jnp.concatenate(
                [
                    jnp.sum(both[:HEAD_DIM], axis=0, keepdims=True),
                    jnp.sum(both[HEAD_DIM:], axis=0, keepdims=True),
                ],
                axis=1,
            )
            level = jnp.concatenate(
                [lse_ref[pl.ds(2 * pair, 1), rows], lse_ref[pl.ds(2 * pair + 1, 1), rows]], axis=1
            )
            raw = dot(k_ref[:, lanes], stack_turned(q_turned[lanes, rows]), NN)
            prob = jnp.exp(raw + twice(bias[...]) - level)
            prob_grad = dot(v_ref[:, lanes], stack_turned(g_turned[lanes, rows]), NN)
            probs[pair % 2] = prob.astype(jnp.bfloat16)
            score_grads[pair % 2] = (prob * (prob_grad - delta)).astype(jnp.bfloat16)

        def gather(pair):
            lanes = slice(pair * LANES, (pair + 1) * LANES)
            values_acc[:, lanes] += dot(probs[pair % 2], stack_heads(g_ref[rows, lanes]), NN)
            keys_acc[:, lanes] += dot(
                score_grads[pair % 2], stack_heads(q_ref[rows, lanes]), NN
            )
            query = pick_heads(dot(k_turned[lanes, :], score_grads[pair % 2], NN))
            query = jnp.transpose(query) * (HEAD_DIM**-0.5)
            keep(rows, lanes, query * cosine - swap_pairs(query) * sine)

        slopes(0)
        for pair in range(PAIRS):
            if pair + 1 < PAIRS:
                slopes(pair + 1)
            gather(pair)

    for_blocks(back_block, tick)
    if after is not None:
        after()

    @pl.loop(0, S // Q_ROWS)
    def _(block):
        rows = pl.ds(pl.multiple_of(block * Q_ROWS, Q_ROWS), Q_ROWS)
        cosine = cos_ref[rows, :]
        sine = sin_ref[rows, :]
        for pair in range(PAIRS):
            lanes = slice(pair * LANES, (pair + 1) * LANES)
            key = keys_acc[rows, lanes]
            keep(
                rows,
                slice(D + pair * LANES, D + (pair + 1) * LANES),
                key * cosine - swap_pairs(key) * sine,
            )
            keep(
                rows,
                slice(2 * D + pair * LANES, 2 * D + (pair + 1) * LANES),
                values_acc[rows, lanes],
            )

    for load in loads:
        load.wait()
    turn(q_turned, x_ref)
    vectors[...] = jnp.zeros_like(vectors)
    vectors[: given_ref.shape[0], :] = given_ref[...]
    for part in range(3):
        columns = slice(part * D, (part + 1) * D)
        vectors[pl.ds(part, 1), :] = jnp.sum(sums[:, columns], axis=0, keepdims=True)

    def thirds(index):
        first = index % 2 * PACKED + index // 2 * HALF
        return (
            pl.ds(pl.multiple_of(index * HALF, LANES), HALF),
            pl.ds(pl.multiple_of(first, LANES), HALF),
        )

    keys_acc[...] = branch_ref[...].astype(jnp.float32)

    @pl.loop(0, 6)
    def _(index):
        plain, spread = thirds(index)
        grad = joint_ref[:, plain]
        weight_ref[:, spread] = dot(q_turned[...], grad, NN).astype(jnp.bfloat16)
        keys_acc[...] += dot(grad, w_ref[:, spread], NT)

    token_ref[...] = keys_acc[...].astype(jnp.bfloat16)
    turned = jnp.transpose(vectors[...]).astype(jnp.bfloat16)
    for half in range(2):
        weight_ref[:, half * PACKED + 3 * HALF : (half + 1) * PACKED] = turned


def whole(*shape):
    return pl.BlockSpec(shape, lambda i, *_: (0,) * len(shape))


def per(*shape):
    return pl.BlockSpec((None,) + shape, lambda i, *_: (i,) + (0,) * len(shape))


def attend(x, weight, bias, cosine, sine, code, low, high):
    own = x.shape[0]
    act = jax.ShapeDtypeStruct((own, S, D), jnp.bfloat16)
    return pl.pallas_call(
        attend_kernel,
        grid=(own,),
        in_specs=[
            per(S, D), whole(D, 2 * PACKED), whole(16, D), whole(S, LANES), whole(S, LANES),
            per(S, 1), per(1, S), per(1, S),
        ],
        out_specs=[per(S, D), per(S, D), per(S, D), per(S, D), per(HEADS, S)],
        scratch_shapes=attend_scratch(),
        out_shape=[act, act, act, act, jax.ShapeDtypeStruct((own, HEADS, S), jnp.float32)],
        compiler_params=pltpu.CompilerParams(vmem_limit_bytes=60 << 20),
        name="attend",
        cost_estimate=pl.CostEstimate(flops=6 * 10**9, bytes_accessed=12 << 20, transcendentals=6 << 20),
    )(x, weight, bias, cosine, sine, code, low, high)


def attend_back(q, k, v, o, g, lse, cosine, sine, code, low, high, x, branch_grad, weight, given):
    own = q.shape[0]
    hbm = pl.BlockSpec(memory_space=pl.ANY)
    return pl.pallas_call(
        attend_back_kernel,
        grid=(own,),
        in_specs=[
            per(S, D), per(S, D), per(S, D), per(S, D), per(S, D), per(HEADS, S),
            whole(S, LANES), whole(S, LANES), per(S, 1), per(1, S), per(1, S), hbm, hbm, hbm,
            per(16, D),
        ],
        out_specs=[per(S, D), per(D, 2 * PACKED)],
        scratch_shapes=attend_back_scratch(),
        out_shape=[
            jax.ShapeDtypeStruct((own, S, D), jnp.bfloat16),
            jax.ShapeDtypeStruct((own, D, 2 * PACKED), jnp.bfloat16),
        ],
        compiler_params=pltpu.CompilerParams(vmem_limit_bytes=60 << 20),
        name="attend_back",
        cost_estimate=pl.CostEstimate(flops=19 * 10**9, bytes_accessed=24 << 20, transcendentals=6 << 20),
    )(q, k, v, o, g, lse, cosine, sine, code, low, high, x, branch_grad, weight, given)


def mask_tables(segments, padding):
    code = 2 * segments + padding
    low = code
    high = 2 * segments + 1
    return code[:, :, None], low[:, None, :], high[:, None, :]


def angles():
    position = jnp.arange(S, dtype=jnp.int32).astype(jnp.float32)
    column = jnp.arange(LANES, dtype=jnp.int32) % HEAD_DIM // 2
    rate = jnp.exp(column.astype(jnp.float32) * (-2.0 * math.log(10000.0) / HEAD_DIM))
    phase = position[:, None] * rate[None, :]
    return jnp.cos(phase), jnp.sin(phase)


MESH = pl.DeviceIdType.MESH
ROWS = ("shard", "ctx")
EVERY = ("shard", "ctx", "tp")
SEQ = ("ctx", "tp")

BULK = ("upper", "down")
ITEMS = ("project",) + BULK
ROUTES = {"project": "zyx", "upper": "xyz", "down": "zxy"}
BEFORE = (('upper', None, 0), ('project', 1, None), ('project', 2, None), ('down', 1, None), ('project', 3, None), ('upper', None, 1), ('project', 4, None), ('down', 2, None), ('project', 5, None))
DURING = ((1, 'upper', None, 2), (3, 'down', 3, None), (6, 'down', 4, None))
AFTER = (('down', 5, None), ('upper', None, 3))
SUM_ROUTES = {"project": "xyz", "upper": "zyx", "down": "xzy"}


def places(depth):
    steps = [0]
    for k in range(1, depth):
        steps += [k, -k]
    return [(k, dy, dx) for k in steps for dy in (0, 1) for dx in (0, 1)]


def hops(place):
    return abs(place[0]) + place[1] + place[2]


def links(route, place, depth):
    apart = {"z": place[0] != 0, "y": place[1], "x": place[2]}
    level = max([i for i, axis in enumerate(route) if apart[axis]], default=-1)
    sign = (place[0] > 0) - (place[0] < 0)
    onward = []
    if level >= 0 and route[level] == "z" and abs(place[0]) + 1 < depth:
        onward.append(("z", -sign))
    for axis in route[level + 1 :]:
        onward += [("z", 1), ("z", -1)] if axis == "z" else [(axis, 1)]
    back = None if level < 0 else (route[level], sign if route[level] == "z" else 1)
    return back, onward


def seen_from(place, link):
    k, dy, dx = place
    axis, way = link
    return {"z": (k - way, dy, dx), "y": (k, 1 - dy, dx), "x": (k, dy, 1 - dx)}[axis]


class Here:
    def __init__(self):
        self.depth = lax.axis_size("shard")
        self.z = lax.axis_index("shard")
        self.c = lax.axis_index("ctx")
        self.t = lax.axis_index("tp")
        self.y = self.c // 2
        self.x = self.c % 2
        self.sides = lax.axis_size("tp")
        self.members = lax.axis_size("ctx") * self.sides
        self.rank = self.c * self.sides + self.t

    def rank_of(self, offset):
        return (self.rank + offset) % self.members

    def member(self, offset):
        rank = self.rank_of(offset)
        return (self.z, rank // self.sides, rank % self.sides)

    def device(self, link):
        axis, way = link
        if axis == "z":
            return (self.z + way, self.c, self.t)
        if axis == "y":
            return (self.z, 2 * (1 - self.y) + self.x, self.t)
        if axis == "x":
            return (self.z, 2 * self.y + (1 - self.x), self.t)
        return (self.z, self.c, 1 - self.t)

    def piece(self, place):
        k, dy, dx = place
        y = 1 - self.y if dy else self.y
        x = 1 - self.x if dx else self.x
        return (self.z + k) * 4 + 2 * y + x

    def inside(self, way):
        if way == 0:
            return None
        return self.z + way < self.depth if way > 0 else self.z + way >= 0

    def meet(self):
        barrier = pltpu.get_barrier_semaphore()
        for offset in range(1, self.members):
            pl.semaphore_signal(
                barrier, inc=1, device_id=self.member(offset), device_id_type=MESH
            )
        for way in (1, -1):

            @pl.when(self.inside(way))
            def _():
                pl.semaphore_signal(
                    barrier, inc=1, device_id=self.device(("z", way)), device_id_type=MESH
                )

        above = (self.z < self.depth - 1).astype(jnp.int32)
        below = (self.z > 0).astype(jnp.int32)
        pl.semaphore_wait(barrier, self.members - 1 + above + below)


class Exchange:
    def __init__(self, here, source, target, send_sem, recv_sem, own_sem):
        self.here, self.source, self.target = here, source, target
        self.send_sem, self.recv_sem, self.own_sem = send_sem, recv_sem, own_sem

    def block(self, ref, index):
        return ref.at[index] if len(ref.shape) == 3 else ref.at[rows_of(index)]

    def copy(self, offset):
        here = self.here
        return pltpu.make_async_remote_copy(
            src_ref=self.block(self.source, here.rank_of(offset)),
            dst_ref=self.block(self.target, here.rank),
            send_sem=self.send_sem.at[offset],
            recv_sem=self.recv_sem.at[offset],
            device_id=here.member(offset),
            device_id_type=MESH,
        )

    def arrival(self, offset):
        here = self.here
        landed = self.block(self.target, here.rank_of(here.members - offset))
        return pltpu.make_async_remote_copy(
            src_ref=landed,
            dst_ref=landed,
            send_sem=self.send_sem.at[offset],
            recv_sem=self.recv_sem.at[offset],
            device_id=here.member(offset),
            device_id_type=MESH,
        )

    def own(self):
        rank = self.here.rank
        return pltpu.make_async_copy(
            self.block(self.source, rank), self.block(self.target, rank), self.own_sem
        )

    def start(self):
        for offset in range(1, self.here.members):
            self.copy(offset).start()
        self.own().start()

    def receive(self):
        for offset in range(1, self.here.members):
            self.arrival(offset).wait_recv()
        self.own().wait()

    def drain(self):
        for offset in range(1, self.here.members):
            self.copy(offset).wait_send()


def rows_of(index):
    return pl.ds(pl.multiple_of(index * Q_ROWS, Q_ROWS), Q_ROWS)


def exchange_scratch(members):
    return [
        pltpu.SemaphoreType.DMA((members,)),
        pltpu.SemaphoreType.DMA((members,)),
        pltpu.SemaphoreType.DMA,
    ]


def guarded(condition, action):
    if condition is None:
        action()
    else:
        pl.when(condition)(action)


def columns(half, width):
    return pl.ds(pl.multiple_of(half * width, LANES), width)


def block_of(name, refs, piece, half, widths):
    return refs[name].at[piece, :, columns(half, widths[name])]


def gather_attend_kernel(
    widths, chip_count, project_hbm, upper_hbm, down_hbm, tokens_hbm,
    cos_ref, sin_ref, code_ref, low_ref, high_ref,
    q_ref, k_ref, v_ref, o_ref, lse_ref, wide_ref, project_out, x_out, upper_out, down_out,
    x_ref, w_ref, q_turned, v_turned, bias, scores, probs,
    send_sem, recv_sem, side_send, side_recv, own_sem, keep_sem, *exchange_sems,
):
    shards = dict(zip(ITEMS, (project_hbm, upper_hbm, down_hbm)))
    wholes = dict(zip(ITEMS, (w_ref, upper_out, down_out)))
    here = Here()
    tokens = Exchange(here, tokens_hbm, x_ref, *exchange_sems)
    spots = places(chip_count)
    order = sorted(spots, key=hops)
    home = (0, 0, 0)
    slot = {}
    for name in ITEMS:
        for place in spots:
            for link in links(ROUTES[name], place, chip_count)[1]:
                slot[name, place, link] = len(slot)

    def block(name, place, half):
        return block_of(name, wholes, here.piece(place), half, widths)

    def source(name, place, half):
        return shards[name] if place == home else block(name, place, half)

    def send(name, place, link):
        return pltpu.make_async_remote_copy(
            src_ref=source(name, place, here.t),
            dst_ref=block(name, place, here.t),
            send_sem=send_sem.at[slot[name, place, link]],
            recv_sem=recv_sem.at[ITEMS.index(name), spots.index(seen_from(place, link))],
            device_id=here.device(link),
            device_id_type=MESH,
        )

    def side(name, place, half):
        return pltpu.make_async_remote_copy(
            src_ref=source(name, place, half) if half is here.t else block(name, place, half),
            dst_ref=block(name, place, half),
            send_sem=side_send.at[ITEMS.index(name), spots.index(place)],
            recv_sem=side_recv.at[ITEMS.index(name), spots.index(place)],
            device_id=here.device(("tp", 1)),
            device_id_type=MESH,
        )

    def arrival(name, place):
        return pltpu.make_async_remote_copy(
            src_ref=block(name, place, here.t),
            dst_ref=block(name, place, here.t),
            send_sem=send_sem.at[0],
            recv_sem=recv_sem.at[ITEMS.index(name), spots.index(place)],
            device_id=here.device(("tp", 1)),
            device_id_type=MESH,
        )

    def own(name):
        return pltpu.make_async_copy(
            shards[name], block(name, home, here.t), own_sem.at[ITEMS.index(name)]
        )

    def relay(names, place):
        def pass_on():
            for name in names:
                if place != home:
                    arrival(name, place).wait_recv()
                for link in links(ROUTES[name], place, chip_count)[1]:
                    guarded(
                        here.inside(link[1]) if link[0] == "z" else None,
                        lambda name=name, link=link: send(name, place, link).start(),
                    )
                side(name, place, here.t).start()

        guarded(here.inside(place[0]), pass_on)

    def beside(names):
        for place in order:

            def wait(place=place):
                for name in names:
                    side(name, place, 1 - here.t).wait_recv()

            guarded(here.inside(place[0]), wait)

    def wave(name, far, near):
        for place in order[1:]:
            if (hops(place) == far if far is not None else abs(place[0]) == near):
                relay((name,), place)

    early = ITEMS[:1]
    here.meet()
    relay(ITEMS, home)
    tokens.start()
    for name in ITEMS:
        own(name).start()
    for stage in BEFORE:
        wave(*stage)
    own("project").wait()
    tokens.receive()
    beside(early)
    vectors = w_ref[:, :, 3 * HALF : PACKED].reshape(D, LANES).astype(jnp.float32)
    wide_ref[...] = jnp.transpose(vectors)[: wide_ref.shape[0]]
    keep = [
        pltpu.make_async_copy(w_ref, project_out, keep_sem.at[0]),
        pltpu.make_async_copy(x_ref, x_out, keep_sem.at[1]),
    ]
    for copy in keep:
        copy.start()
    project_rows(x_ref, w_ref, wide_ref, cos_ref, sin_ref, q_ref, k_ref, v_ref)

    def tick(step):
        for when, *stage in DURING:
            pl.when(step == when)(functools.partial(wave, *stage))

    attend_blocks(
        q_ref, k_ref, v_ref, o_ref, lse_ref, code_ref, low_ref, high_ref, q_turned, v_turned, bias,
        scores, probs, tick,
    )
    for stage in AFTER:
        wave(*stage)
    beside(BULK)
    for name in BULK:
        own(name).wait()
    tokens.drain()
    for copy in keep:
        copy.wait()
    for place in order:

        def finish(place=place):
            for name in ITEMS:
                side(name, place, here.t).wait_send()
                for link in links(ROUTES[name], place, chip_count)[1]:
                    guarded(
                        here.inside(link[1]) if link[0] == "z" else None,
                        lambda name=name, link=link: send(name, place, link).wait_send(),
                    )

        guarded(here.inside(place[0]), finish)


def link_count(depth):
    return sum(len(links(ROUTES[name], place, depth)[1]) for name in ITEMS for place in places(depth))


def gather_attend(shards, tokens, cosine, sine, code, low, high):
    chips, pieces = lax.axis_size("shard"), lax.axis_size("shard") * lax.axis_size("ctx")
    members = tokens.shape[0]
    widths = {name: shards[name].shape[-1] for name in ITEMS}
    depth = shards["upper"].shape[0]
    spots = len(places(chips))
    vmem, hbm = pl.BlockSpec(memory_space=pltpu.VMEM), pl.BlockSpec(memory_space=pl.ANY)

    def act(*shape):
        return jax.ShapeDtypeStruct(shape, jnp.bfloat16)

    def gathered(name):
        return act(pieces, depth, 2 * widths[name])

    per_place = pltpu.SemaphoreType.DMA((len(ITEMS), spots))
    outs = pl.pallas_call(
        functools.partial(gather_attend_kernel, widths, chips),
        out_shape=[
            act(S, D), act(S, D), act(S, D), act(S, D), jax.ShapeDtypeStruct((HEADS, S), jnp.float32),
            jax.ShapeDtypeStruct((16, D), jnp.float32), gathered("project"), act(S, D),
            gathered("upper"), gathered("down"),
        ],
        in_specs=[hbm] * 4 + [vmem] * 5,
        out_specs=[vmem] * 6 + [hbm] * 4,
        scratch_shapes=[
            pltpu.VMEM((S, D), jnp.bfloat16),
            pltpu.VMEM((pieces, depth, 2 * widths["project"]), jnp.bfloat16),
        ]
        + attend_scratch()
        + [
            pltpu.SemaphoreType.DMA((link_count(chips),)),
            per_place,
            per_place,
            per_place,
            pltpu.SemaphoreType.DMA((len(ITEMS),)),
            pltpu.SemaphoreType.DMA((2,)),
        ]
        + exchange_scratch(members),
        compiler_params=pltpu.CompilerParams(
            collective_id=0, has_side_effects=True, vmem_limit_bytes=60 << 20
        ),
        name="gather_attend",
    )(*[shards[name] for name in ITEMS], tokens, cosine, sine, code, low, high)
    query, key, value, attended, level, wide, project, x, upper, down = outs
    return query, key, value, attended, level, wide, x, dict(project=project, upper=upper, down=down)


def add_into(target, addend):
    height = 16

    @pl.loop(0, target.shape[0] // height)
    def _(step):
        rows = pl.ds(pl.multiple_of(step * height, height), height)
        total = target[rows, :].astype(jnp.float32) + addend[rows, :].astype(jnp.float32)
        target[rows, :] = total.astype(target.dtype)


class Sums:
    def __init__(self, here, names, routes, chip_count, widths, grads, mine, theirs, inbox, sems):
        self.here, self.names, self.routes, self.chip_count = here, names, routes, chip_count
        self.widths, self.grads, self.mine, self.theirs, self.inbox = widths, grads, mine, theirs, inbox
        self.load_sem, self.side_send, self.side_recv, self.send_sem, self.recv_sem = sems
        self.spots = places(chip_count)
        self.order = sorted(self.spots, key=hops, reverse=True)
        self.slot, self.box = {}, {}
        for name in names:
            local = 0
            for place in self.spots:
                for link in links(routes[name], place, chip_count)[1]:
                    self.slot[name, place, link] = len(self.slot)
                    self.box[name, place, link] = local
                    local += 1

    def at(self, name, place):
        return self.names.index(name), self.spots.index(place)

    def total(self, name, place):
        return self.mine[name].at[self.here.piece(place)]

    def other(self, name, place):
        return self.theirs[name].at[self.here.piece(place)]

    def load(self, name, place):
        source = block_of(name, self.grads, self.here.piece(place), self.here.t, self.widths)
        return pltpu.make_async_copy(
            source, self.total(name, place), self.load_sem.at[self.at(name, place)]
        )

    def side(self, name, place):
        here = self.here
        return pltpu.make_async_remote_copy(
            src_ref=block_of(name, self.grads, here.piece(place), 1 - here.t, self.widths),
            dst_ref=self.other(name, place),
            send_sem=self.side_send.at[self.at(name, place)],
            recv_sem=self.side_recv.at[self.at(name, place)],
            device_id=here.device(("tp", 1)),
            device_id_type=MESH,
        )

    def send(self, name, place, link):
        there = seen_from(place, link)
        back = (link[0], -link[1]) if link[0] == "z" else link
        return pltpu.make_async_remote_copy(
            src_ref=self.total(name, place),
            dst_ref=self.inbox[name].at[self.box[name, there, back]],
            send_sem=self.send_sem.at[self.at(name, place)],
            recv_sem=self.recv_sem.at[self.slot[name, there, back]],
            device_id=self.here.device(link),
            device_id_type=MESH,
        )

    def arrival(self, name, place, link):
        landed = self.inbox[name].at[self.box[name, place, link]]
        return pltpu.make_async_remote_copy(
            src_ref=landed,
            dst_ref=landed,
            send_sem=self.send_sem.at[0, 0],
            recv_sem=self.recv_sem.at[self.slot[name, place, link]],
            device_id=self.here.device(link),
            device_id_type=MESH,
        )

    def start(self):
        for place in self.order:

            def begin(place=place):
                for name in self.names:
                    self.side(name, place).start()
                    self.load(name, place).start()

            guarded(self.here.inside(place[0]), begin)

    def settle(self, distance):
        for place in self.order:
            if hops(place) != distance:
                continue

            def work(place=place):
                for name in self.names:
                    back, onward = links(self.routes[name], place, self.chip_count)
                    total = self.total(name, place)
                    self.load(name, place).wait()
                    self.side(name, place).wait_recv()
                    add_into(total, self.other(name, place))
                    for link in onward:

                        def take(link=link):
                            self.arrival(name, place, link).wait_recv()
                            add_into(total, self.inbox[name].at[self.box[name, place, link]])

                        guarded(self.here.inside(link[1]) if link[0] == "z" else None, take)
                    if back is not None:
                        self.send(name, place, back).start()

            guarded(self.here.inside(place[0]), work)

    def result(self, name):
        return self.total(name, (0, 0, 0))[...].astype(jnp.float32)

    def drain(self):
        for place in self.order:

            def finish(place=place):
                for name in self.names:
                    back, _ = links(self.routes[name], place, self.chip_count)
                    self.side(name, place).wait_send()
                    if back is not None:
                        self.send(name, place, back).wait_send()

            guarded(self.here.inside(place[0]), finish)


def sums_scratch(names, routes, chips, pieces, blocks, kinds):
    spots = places(chips)
    boxes = [sum(len(links(routes[name], place, chips)[1]) for place in spots) for name in names]
    per_place = pltpu.SemaphoreType.DMA((len(names), len(spots)))
    return (
        [pltpu.VMEM((pieces,) + block, kind) for block, kind in zip(blocks, kinds)] * 2
        + [pltpu.VMEM((box,) + block, kind) for box, block, kind in zip(boxes, blocks, kinds)]
        + [per_place] * 4
        + [pltpu.SemaphoreType.DMA((sum(boxes),))]
    )


def sums_of(here, names, routes, chip_count, widths, grads, refs):
    count = len(names)
    groups = [dict(zip(names, refs[i * count : (i + 1) * count])) for i in range(3)]
    return Sums(here, names, routes, chip_count, widths, grads, *groups, refs[3 * count :])


def back_scatter_kernel(
    widths, chip_count, *refs,
):
    body, bulk, outs = refs[:15], refs[15:17], refs[17:21]
    scratch = len(attend_back_scratch())
    local, rest = refs[21 : 21 + scratch], refs[21 + scratch :]
    here = Here()
    grads = dict(zip(BULK, bulk))
    sums = sums_of(here, BULK, SUM_ROUTES, chip_count, widths, grads, rest)
    here.meet()
    sums.start()
    farthest = max(hops(place) for place in sums.spots)
    steps = (1, 2, 3, 5, 7)

    def tick(step):
        for i, when in enumerate(steps):
            pl.when(step == when)(functools.partial(sums.settle, farthest - i))

    def after():
        for distance in range(farthest - len(steps), 0, -1):
            sums.settle(distance)

    attend_back_body(*body, *outs[:2], *local, tick=tick, after=after)
    sums.settle(0)
    for name, out in zip(BULK, outs[2:]):
        out[...] = sums.result(name)
    sums.drain()


def back_scatter(q, k, v, o, g, lse, cosine, sine, code, low, high, x, branch_grad, weight, given, grads):
    chips, pieces = lax.axis_size("shard"), lax.axis_size("shard") * lax.axis_size("ctx")
    vmem, hbm = pl.BlockSpec(memory_space=pltpu.VMEM), pl.BlockSpec(memory_space=pl.ANY)
    blocks = [(grads[name].shape[1], grads[name].shape[2] // 2) for name in BULK]
    widths = {name: block[-1] for name, block in zip(BULK, blocks)}
    outs = pl.pallas_call(
        functools.partial(back_scatter_kernel, widths, chips),
        out_shape=[
            jax.ShapeDtypeStruct((S, D), jnp.bfloat16),
            jax.ShapeDtypeStruct((D, 2 * PACKED), jnp.bfloat16),
        ]
        + [jax.ShapeDtypeStruct(block, jnp.float32) for block in blocks],
        in_specs=[vmem] * 11 + [hbm] * 3 + [vmem] + [hbm] * 2,
        out_specs=[vmem] * 4,
        scratch_shapes=attend_back_scratch()
        + sums_scratch(BULK, SUM_ROUTES, chips, pieces, blocks, [jnp.bfloat16] * len(BULK)),
        compiler_params=pltpu.CompilerParams(
            collective_id=3, has_side_effects=True, vmem_limit_bytes=67043328
        ),
        name="back_scatter",
    )(
        q, k, v, o, g, lse, cosine, sine, code, low, high, x, branch_grad, weight, given,
        *[grads[name] for name in BULK],
    )
    return outs[:2], dict(zip(BULK, outs[2:]))


LAST = ("project",)


def scatter_kernel(widths, chip_count, project_hbm, tokens_hbm, project_ref, tokens_out, *rest):
    here = Here()
    sums = sums_of(here, LAST, SUM_ROUTES, chip_count, widths, {"project": project_hbm}, rest[:-3])
    tokens = Exchange(here, tokens_hbm, tokens_out, *rest[-3:])
    here.meet()
    sums.start()
    farthest = max(hops(place) for place in sums.spots)
    for distance in range(farthest, -1, -1):
        sums.settle(distance)
        if distance == farthest - 1:
            tokens.start()
    project_ref[...] = sums.result("project")
    tokens.receive()
    tokens.drain()
    sums.drain()


def scatter_last(project, tokens_grad):
    chips, pieces = lax.axis_size("shard"), lax.axis_size("shard") * lax.axis_size("ctx")
    vmem, hbm = pl.BlockSpec(memory_space=pltpu.VMEM), pl.BlockSpec(memory_space=pl.ANY)
    block = (project.shape[1], project.shape[2] // 2)
    return pl.pallas_call(
        functools.partial(scatter_kernel, {"project": block[-1]}, chips),
        out_shape=[
            jax.ShapeDtypeStruct(block, jnp.float32),
            jax.ShapeDtypeStruct(tokens_grad.shape, tokens_grad.dtype),
        ],
        in_specs=[hbm] * 2,
        out_specs=[vmem, hbm],
        scratch_shapes=sums_scratch(LAST, SUM_ROUTES, chips, pieces, [block], [jnp.bfloat16])
        + exchange_scratch(tokens_grad.shape[0]),
        compiler_params=pltpu.CompilerParams(
            collective_id=1, has_side_effects=True, vmem_limit_bytes=60 << 20
        ),
        name="scatter_last",
    )(project, tokens_grad)


CHUNK = 512
STEP = 16
UNROLL = 4
ATTEND_BIAS, DOWN_BIAS, FIRST_GAIN, FIRST_SHIFT, SECOND_GAIN, SECOND_SHIFT = range(3, 9)
SUMS = 6


def row_mean(values):
    return jnp.sum(values, axis=-1, keepdims=True) * (1.0 / D)


def fold(values):
    return jnp.sum(values.reshape(values.shape[0] // 8, 8, values.shape[1]), axis=0)


def chunk_at(index):
    return pl.ds(pl.multiple_of(index * CHUNK, CHUNK), CHUNK)


def ffn_kernel(
    shared, a_ref, wide_ref, shift_ref, x_hbm, c_hbm, upper_hbm, down_hbm,
    joined_ref, branch_ref, sums_ref, up_sums_ref, out_hbm, upper_grad_hbm, down_grad_hbm,
    x_ref, c_ref, attend_ref, up_ref, down_ref, out_ref, hidden_ref, slope_ref, low_ref, ffn_ref, turned_ref,
    left, right, near, far, first, unit, acc, factor, sums, up_sums, stage, in_sem, out_sem, stage_sem,
    *exchange_sems,
):
    halves = [(half * UPPER, half * RISE, half * HALF) for half in range(2)]
    copies = [
        (upper_hbm.at[:, start + RISE : start + UPPER], attend_ref.at[:, low : low + HALF])
        for start, _, low in halves
    ]
    copies.append((x_hbm, x_ref))
    copies += [
        (upper_hbm.at[:, start : start + RISE], up_ref.at[:, rise : rise + RISE])
        for start, rise, _ in halves
    ]
    copies.append((down_hbm, down_ref))
    if not shared:
        copies.append((c_hbm, c_ref))
    loads = [
        pltpu.make_async_copy(source, target, in_sem.at[i]) for i, (source, target) in enumerate(copies)
    ]
    for load in loads:
        load.start()
    if shared:
        here = Here()
        barrier = pltpu.get_barrier_semaphore()
        for offset in range(1, here.members):
            pl.semaphore_signal(barrier, inc=1, device_id=here.member(offset), device_id_type=MESH)
        arriving = Exchange(here, c_hbm, c_ref, *exchange_sems[:3])
        leaving = Exchange(here, out_ref, out_hbm, *exchange_sems[3:])
    sums[...] = jnp.zeros_like(sums)
    up_sums[...] = jnp.zeros_like(up_sums)
    pairs = FF // CHUNK // 2

    def vector(index):
        return wide_ref[pl.ds(index, 1), :]

    def add_sum(index, values):
        sums[index - ATTEND_BIAS] += fold(values)

    def rows_loop(body):
        @pl.loop(0, S // STEP, unroll=UNROLL)
        def _(step):
            body(pl.ds(pl.multiple_of(step * STEP, STEP), STEP))

    loads[0].wait()
    loads[1].wait()
    acc[...] = dot(a_ref[...], attend_ref[...], NT)
    if shared:
        pl.semaphore_wait(barrier, here.members - 1)
        arriving.start()
    loads[2].wait()

    @rows_loop
    def _(rows):
        joined = x_ref[rows, :].astype(jnp.float32) + acc[rows, :] + vector(ATTEND_BIAS)
        centred = joined - row_mean(joined)
        scale = lax.rsqrt(row_mean(centred * centred) + norm_eps)
        normed = centred * scale
        unit[rows, :] = normed
        factor[rows, :] = scale
        result = normed * vector(FIRST_GAIN) + vector(FIRST_SHIFT)
        first[rows, :] = result
        low_ref[rows, :] = result.astype(jnp.bfloat16)

    for load in loads[3:6]:
        load.wait()

    def expand(target, index):
        target[...] = dot(low_ref[...], up_ref[:, chunk_at(index)], NN)

    def activate(source, target, index):
        pre = source[...] + shift_ref[:, chunk_at(index)]
        cumulative = 0.5 + 0.5 * lax.erf(pre * (1.0 / math.sqrt(2.0)))
        density = jnp.exp(-0.5 * pre * pre) * (1.0 / math.sqrt(2.0 * math.pi))
        hidden = (pre * cumulative).astype(jnp.bfloat16)
        target[...] = hidden
        hidden_ref[:, chunk_at(index)] = hidden
        slope_ref[:, chunk_at(index)] = (cumulative + pre * density).astype(jnp.bfloat16)

    def contract(source, index):
        acc[...] += dot(source[...], down_ref[:, chunk_at(index)], NT)

    def forward(pair):
        expand(right, 2 * pair + 1)
        activate(left, near, 2 * pair)
        expand(left, jnp.minimum(2 * pair + 2, 2 * pairs - 1))
        contract(near, 2 * pair)
        activate(right, far, 2 * pair + 1)
        contract(far, 2 * pair + 1)

    expand(left, 0)
    acc[...] = jnp.zeros_like(acc)

    pl.loop(0, pairs)(forward)
    if shared:
        arriving.receive()
    else:
        loads[6].wait()

    @rows_loop
    def _(rows):
        joined = first[rows, :] + acc[rows, :] + vector(DOWN_BIAS)
        centred = joined - row_mean(joined)
        scale = lax.rsqrt(row_mean(centred * centred) + norm_eps)
        normed = centred * scale
        out_ref[rows, :] = (normed * vector(SECOND_GAIN) + vector(SECOND_SHIFT)).astype(jnp.bfloat16)
        grad = c_ref[rows, :].astype(jnp.float32)
        add_sum(SECOND_GAIN, grad * normed)
        add_sum(SECOND_SHIFT, grad)
        inner = grad * vector(SECOND_GAIN)
        back = scale * (inner - row_mean(inner) - normed * row_mean(inner * normed))
        first[rows, :] = back
        low = back.astype(jnp.bfloat16)
        ffn_ref[rows, :] = low
        add_sum(DOWN_BIAS, low.astype(jnp.float32))

    if not shared:
        store = pltpu.make_async_copy(out_ref, out_hbm, out_sem)
        store.start()

    def stored(slot, target, index, spread):
        first = index * CHUNK + index // pairs * spread
        return pltpu.make_async_copy(
            stage.at[slot],
            target.at[:, pl.ds(pl.multiple_of(first, LANES), CHUNK)],
            stage_sem.at[slot],
        )

    def weight_grad(source, target, spread):
        @pl.loop(0, 2 * pairs)
        def _(index):
            slot = index % 2

            @pl.when(index > 1)
            def _():
                stored(slot, target, index, spread).wait()

            stage[slot] = dot(turned_ref[...], source[:, chunk_at(index)], NN).astype(jnp.bfloat16)
            stored(slot, target, index, spread).start()

        for slot in range(2):
            stored(slot, target, slot, spread).wait()

    turn(turned_ref, ffn_ref)
    if shared:
        leaving.start()
    weight_grad(hidden_ref, down_grad_hbm, 0)

    def widen(target, index):
        target[...] = dot(ffn_ref[...], down_ref[:, chunk_at(index)], NN)

    def reweigh(source, target, index):
        grad = (source[...] * slope_ref[:, chunk_at(index)].astype(jnp.float32)).astype(jnp.bfloat16)
        target[...] = grad
        hidden_ref[:, chunk_at(index)] = grad
        up_sums[:, chunk_at(index)] += fold(grad.astype(jnp.float32))

    def collect(source, index):
        acc[...] += dot(source[...], up_ref[:, chunk_at(index)], NT)

    def backward(pair):
        widen(right, 2 * pair + 1)
        reweigh(left, near, 2 * pair)
        widen(left, jnp.minimum(2 * pair + 2, 2 * pairs - 1))
        collect(near, 2 * pair)
        reweigh(right, far, 2 * pair + 1)
        collect(far, 2 * pair + 1)

    widen(left, 0)
    acc[...] = jnp.zeros_like(acc)

    pl.loop(0, pairs)(backward)

    @rows_loop
    def _(rows):
        grad = first[rows, :] + acc[rows, :]
        normed = unit[rows, :]
        add_sum(FIRST_GAIN, grad * normed)
        add_sum(FIRST_SHIFT, grad)
        inner = grad * vector(FIRST_GAIN)
        back = factor[rows, :] * (inner - row_mean(inner) - normed * row_mean(inner * normed))
        low = back.astype(jnp.bfloat16)
        branch_ref[rows, :] = low
        add_sum(ATTEND_BIAS, low.astype(jnp.float32))

    joined_ref[...] = dot(branch_ref[...], attend_ref[...], NN).astype(jnp.bfloat16)
    turn(turned_ref, low_ref)
    weight_grad(hidden_ref, upper_grad_hbm, HALF)
    turn(turned_ref, branch_ref)

    def attend_stored(slot):
        first = slot * UPPER + RISE
        return pltpu.make_async_copy(
            stage.at[slot, :, :HALF], upper_grad_hbm.at[:, first : first + HALF], stage_sem.at[slot]
        )

    for slot in range(2):
        stage[slot, :, :HALF] = dot(
            turned_ref[...], a_ref[:, slot * HALF : (slot + 1) * HALF], NN
        ).astype(jnp.bfloat16)
        attend_stored(slot).start()
    for index in range(SUMS):
        sums_ref[pl.ds(index, 1), :] = jnp.sum(sums[index], axis=0, keepdims=True)
    up_sums_ref[...] = jnp.sum(up_sums[...], axis=0, keepdims=True)
    for slot in range(2):
        attend_stored(slot).wait()
    if shared:
        leaving.receive()
        arriving.drain()
        leaving.drain()
    else:
        store.wait()


def feed_forward(attended, x, cotangent, upper, down_t, wide, up_shift, shared=False):
    vmem, hbm = pl.BlockSpec(memory_space=pltpu.VMEM), pl.BlockSpec(memory_space=pl.ANY)

    def low(*shape):
        return jax.ShapeDtypeStruct(shape, jnp.bfloat16)

    def full(*shape):
        return jax.ShapeDtypeStruct(shape, jnp.float32)

    def scratch(width, kind=jnp.bfloat16):
        return pltpu.VMEM((S, width), kind)

    return pl.pallas_call(
        functools.partial(ffn_kernel, shared),
        in_specs=[vmem] * 3 + [hbm] * 4,
        out_specs=[vmem] * 4 + [hbm] * 3,
        out_shape=[
            low(S, D), low(S, D), full(SUMS, D), full(1, FF), low(*cotangent.shape),
            low(D, 2 * UPPER), low(D, FF),
        ],
        scratch_shapes=[
            scratch(D), scratch(D), pltpu.VMEM((D, D), jnp.bfloat16), pltpu.VMEM((D, FF), jnp.bfloat16),
            pltpu.VMEM((D, FF), jnp.bfloat16),
            scratch(D), scratch(FF), scratch(FF), scratch(D), scratch(D), pltpu.VMEM((D, S), jnp.bfloat16),
            scratch(CHUNK, jnp.float32), scratch(CHUNK, jnp.float32), scratch(CHUNK), scratch(CHUNK),
            scratch(D, jnp.float32), scratch(D, jnp.float32), scratch(D, jnp.float32),
            scratch(1, jnp.float32),
            pltpu.VMEM((SUMS, 8, D), jnp.float32), pltpu.VMEM((8, FF), jnp.float32),
            pltpu.VMEM((2, D, CHUNK), jnp.bfloat16),
            pltpu.SemaphoreType.DMA((7,)), pltpu.SemaphoreType.DMA, pltpu.SemaphoreType.DMA((2,)),
        ]
        + 2 * (exchange_scratch(cotangent.shape[0]) if shared else []),
        compiler_params=pltpu.CompilerParams(
            vmem_limit_bytes=63 << 20,
            collective_id=2 if shared else None,
            has_side_effects=shared,
        ),
        name="feed_forward",
        cost_estimate=pl.CostEstimate(
            flops=6 * S * D * (D + 2 * FF), bytes_accessed=30 << 20, transcendentals=2 * S * FF
        ),
    )(attended, wide, up_shift.reshape(1, FF), x, cotangent, upper, down_t)


def fitting(shards, own):
    return own == 1 and lax.axis_size("ctx") == 4 and lax.axis_size("tp") == 2 and shards["upper"].shape[0] % 16 == 0


def gather_plain(shards):
    return {
        name: lax.all_gather(
            lax.all_gather(shards[name], ROWS, axis=0), "tp", axis=2, tiled=True
        )
        for name in ITEMS
    }


def scatter_plain(grads):
    shards = {}
    for name in ITEMS:
        part = lax.psum_scatter(grads[name], "tp", scatter_dimension=2, tiled=True)
        part = lax.psum_scatter(part, ROWS, scatter_dimension=0, tiled=False)
        shards[name] = part.astype(jnp.float32)
    return shards


def local(
    tokens, project_weight, attend_weight, up_weight, down_weight, project_bias, attend_bias,
    up_bias, down_bias, first_gain, first_shift, second_gain, second_shift, segment_ids, padding,
    cotangent,
):
    seq_count = tokens.shape[0]
    members = lax.axis_size("ctx") * lax.axis_size("tp")
    own = seq_count // members
    rank = lax.axis_index("ctx") * lax.axis_size("tp") + lax.axis_index("tp")
    pieces = lax.axis_size("shard") * lax.axis_size("ctx")
    depth = D // pieces

    def to_sequences(array):
        parts = array.reshape((members, own) + array.shape[1:])
        parts = lax.all_to_all(parts, SEQ, 0, 0, tiled=True)
        return jnp.swapaxes(parts, 0, 1).reshape(own, S, D)

    def to_blocks(array):
        parts = jnp.swapaxes(array.reshape(own, members, S // members, D), 0, 1)
        return lax.all_to_all(parts, SEQ, 0, 0, tiled=True).reshape(tokens.shape)

    segments = lax.dynamic_slice_in_dim(segment_ids, rank * own, own, 0)
    pads = lax.dynamic_slice_in_dim(padding, rank * own, own, 0)

    vectors = jnp.concatenate(
        [
            project_bias,
            attend_bias[None],
            down_bias[None],
            first_gain[None],
            first_shift[None],
            second_gain[None],
            second_shift[None],
            up_bias.reshape(FF // D, depth),
        ],
        axis=0,
    )
    shards = {
        "project": jnp.concatenate(
            [
                project_weight.reshape(depth, 3 * HALF),
                jnp.pad(jnp.transpose(vectors), ((0, 0), (0, LANES - vectors.shape[0]))),
            ],
            axis=1,
        ),
        "upper": jnp.concatenate([up_weight, jnp.transpose(attend_weight)], axis=1),
        "down": jnp.transpose(down_weight),
    }
    custom = fitting(shards, own)
    tables = mask_tables(segments, pads)
    cosine, sine = angles()
    if custom:
        *saved, wide, x, wholes = gather_attend(
            shards, tokens, cosine, sine, *[table[0] for table in tables]
        )
        query, key, value, attended, level, x = [array[None] for array in saved + [x]]
    else:
        wholes, x = gather_plain(shards), to_sequences(tokens)
    project = wholes["project"].reshape(D, 2 * PACKED)
    upper = wholes["upper"].reshape(D, 2 * UPPER)
    down_t = wholes["down"].reshape(D, FF)
    if not custom:
        wide = jnp.transpose(project[:, 3 * HALF : 3 * HALF + 16]).astype(jnp.float32)
        query, key, value, attended, level = attend(x, project, wide, cosine, sine, *tables)
    up_shift = jnp.swapaxes(wide[9:13].reshape(FF // D, pieces, depth), 0, 1).reshape(FF)
    params = (upper, down_t, wide, up_shift)
    if custom:
        parts = [feed_forward(attended[0], x[0], cotangent, *params, shared=True)]
    else:
        incoming = to_sequences(cotangent)
        parts = [feed_forward(attended[i], x[i], incoming[i], *params) for i in range(own)]
    attended_grad = jnp.stack([part[0] for part in parts])
    branch_grad = jnp.stack([part[1] for part in parts])
    sums = sum(part[2] for part in parts)
    up_bias_grad = sum(part[3] for part in parts)
    output = parts[0][4] if custom else to_blocks(jnp.stack([part[4] for part in parts]))
    upper_grad, down_grad = (
        parts[0][k] if own == 1 else sum(part[k].astype(jnp.float32) for part in parts).astype(jnp.bfloat16)
        for k in (5, 6)
    )
    up_bias_grad = jnp.swapaxes(up_bias_grad.reshape(pieces, FF // D, depth), 0, 1).reshape(FF // D, D)
    given = jnp.concatenate([jnp.zeros((3, D), jnp.float32), sums, up_bias_grad, jnp.zeros((3, D), jnp.float32)])
    grads = {
        "upper": upper_grad.reshape(pieces, depth, 2 * UPPER),
        "down": down_grad.reshape(pieces, depth, FF),
    }
    inputs = (query, key, value, attended, attended_grad, level)
    if custom:
        (tokens_grad, project_grad), shards = back_scatter(
            *[array[0] for array in inputs], cosine, sine, *[table[0] for table in tables], x[0],
            branch_grad[0], project, given, grads,
        )
        shards["project"], tokens_grad = scatter_last(
            project_grad.reshape(pieces, depth, 2 * PACKED), tokens_grad.reshape(tokens.shape)
        )
    else:
        given = jnp.concatenate([given[None], jnp.zeros((own - 1,) + given.shape, jnp.float32)])
        tokens_grad, project_grad = attend_back(
            *inputs, cosine, sine, *tables, x, branch_grad, project, given
        )
        project_grad = jnp.sum(project_grad.astype(jnp.float32), axis=0).astype(jnp.bfloat16)
        grads["project"] = project_grad.reshape(pieces, depth, 2 * PACKED)
        shards, tokens_grad = scatter_plain(grads), to_blocks(tokens_grad)
    sums = jnp.transpose(shards["project"][:, 3 * HALF : 3 * HALF + 13])
    return (
        output,
        tokens_grad,
        shards["project"][:, : 3 * HALF].reshape(depth, 3, HALF),
        jnp.transpose(shards["upper"][:, RISE:]),
        shards["upper"][:, :RISE],
        jnp.transpose(shards["down"]),
        sums[:3],
        sums[3],
        sums[9:].reshape(-1),
        sums[4],
        sums[5],
        sums[6],
        sums[7],
        sums[8],
    )


def solution(mesh):
    in_specs = (
        P("shard", ("ctx", "tp"), None),
        P(("shard", "ctx"), None, "tp"),
        P("tp", ("shard", "ctx")),
        P(("shard", "ctx"), "tp"),
        P("tp", ("shard", "ctx")),
        P(None, ("shard", "ctx")),
        P(("shard", "ctx")),
        P(("shard", "ctx")),
        P(("shard", "ctx")),
        P(("shard", "ctx")),
        P(("shard", "ctx")),
        P(("shard", "ctx")),
        P(("shard", "ctx")),
        P("shard", None),
        P("shard", None),
        P("shard", ("ctx", "tp"), None),
    )
    out_specs = (
        P("shard", ("ctx", "tp"), None),
        P("shard", ("ctx", "tp"), None),
        P(("shard", "ctx"), None, "tp"),
        P("tp", ("shard", "ctx")),
        P(("shard", "ctx"), "tp"),
        P("tp", ("shard", "ctx")),
        P(None, ("shard", "ctx")),
        P(("shard", "ctx")),
        P(("shard", "ctx")),
        P(("shard", "ctx")),
        P(("shard", "ctx")),
        P(("shard", "ctx")),
        P(("shard", "ctx")),
        P(("shard", "ctx")),
    )
    return jax.shard_map(local, mesh=mesh, in_specs=in_specs, out_specs=out_specs, check_vma=False)
```

```python
import functools
import math

import jax
import jax.numpy as jnp
from jax import lax
from jax.experimental import pallas as pl
from jax.experimental.pallas import tpu as pltpu
from jax.sharding import PartitionSpec as P

D = 768
HEADS = 12
HEAD_DIM = 64
FF = 3072
S = 1024
LANES = 128
PAIRS = HEADS // 2
Q_ROWS = 128

HALF = D // 2
PACKED = 3 * HALF + LANES
RISE = FF // 2
UPPER = RISE + HALF

norm_eps = 1e-12
mask_fill = -1000000000.0

NT = (((1,), (1,)), ((), ()))
TN = (((0,), (0,)), ((), ()))
NN = (((1,), (0,)), ((), ()))


def dot(left, right, dims):
    return lax.dot_general(left, right, dims, preferred_element_type=jnp.float32)


def swap_pairs(values):
    lane = lax.broadcasted_iota(jnp.int32, values.shape, 1)
    width = values.shape[1]
    return jnp.where(
        lane % 2 == 0, -pltpu.roll(values, width - 1, 1), pltpu.roll(values, 1, 1)
    )


def turn(target, source):
    @pl.loop(0, source.shape[1] // LANES)
    def _(step):
        part = pl.ds(pl.multiple_of(step * LANES, LANES), LANES)
        target[part, :] = jnp.transpose(source[:, part])


def stack_heads(rows):
    lane = lax.broadcasted_iota(jnp.int32, rows.shape, 1)
    zero = jnp.zeros_like(rows)
    return jnp.concatenate(
        [jnp.where(lane < HEAD_DIM, rows, zero), jnp.where(lane < HEAD_DIM, zero, rows)], axis=0
    )


def pick_heads(both):
    return jnp.concatenate([both[:HEAD_DIM, :Q_ROWS], both[HEAD_DIM:, Q_ROWS:]], axis=0)


def spread_heads(row):
    return jnp.concatenate(
        [
            jnp.broadcast_to(row[:, :Q_ROWS], (HEAD_DIM, Q_ROWS)),
            jnp.broadcast_to(row[:, Q_ROWS:], (HEAD_DIM, Q_ROWS)),
        ],
        axis=0,
    )


def mask_bias(key_code, query_low, query_high):
    keys = jnp.broadcast_to(key_code, (key_code.shape[0], Q_ROWS))
    allowed = (keys >= query_low) & (keys <= query_high)
    return jnp.where(allowed, 0.0, mask_fill)


def stack_turned(turned):
    feature = lax.broadcasted_iota(jnp.int32, turned.shape, 0)
    zero = jnp.zeros_like(turned)
    return jnp.concatenate(
        [jnp.where(feature < HEAD_DIM, turned, zero), jnp.where(feature < HEAD_DIM, zero, turned)],
        axis=1,
    )


def twice(bias):
    return jnp.concatenate([bias, bias], axis=1)


def for_blocks(body, tick=None):
    @pl.loop(0, S // Q_ROWS)
    def _(block):
        if tick is not None:
            tick(block)
        body(block)


def packed(part, half):
    first = half * PACKED + part * HALF
    return slice(first, first + HALF)


def packed_weight(w_ref, part, half):
    return w_ref[..., packed(part, half)].reshape(D, HALF)


def project_rows(x_ref, w_ref, b_ref, cos_ref, sin_ref, q_ref, k_ref, v_ref):
    row_tile = 512

    @pl.loop(0, S // row_tile)
    def _(tile):
        rows = pl.ds(pl.multiple_of(tile * row_tile, row_tile), row_tile)
        x = x_ref[rows, :]
        cosine = cos_ref[rows, :]
        sine = sin_ref[rows, :]
        for part, out in enumerate((q_ref, k_ref, v_ref)):
            for pair in range(PAIRS):
                lanes = slice(pair * LANES, (pair + 1) * LANES)
                half, place = divmod(pair, PAIRS // 2)
                if place == 0:
                    joint = dot(x, packed_weight(w_ref, part, half), NN)
                piece = joint[:, place * LANES : (place + 1) * LANES] + b_ref[pl.ds(part, 1), lanes]
                if part < 2:
                    piece = piece * cosine + swap_pairs(piece) * sine
                if part == 0:
                    piece = piece.astype(jnp.bfloat16) * jnp.asarray(HEAD_DIM**-0.5, jnp.bfloat16)
                out[rows, lanes] = piece.astype(jnp.bfloat16)


def attend_kernel(
    x_ref, w_ref, b_ref, cos_ref, sin_ref, code_ref, low_ref, high_ref,
    q_ref, k_ref, v_ref, o_ref, lse_ref, *scratch,
):
    project_rows(x_ref, w_ref, b_ref, cos_ref, sin_ref, q_ref, k_ref, v_ref)
    attend_blocks(q_ref, k_ref, v_ref, o_ref, lse_ref, code_ref, low_ref, high_ref, *scratch)


def attend_scratch():
    return [
        pltpu.VMEM((D, S), jnp.bfloat16),
        pltpu.VMEM((D, S), jnp.bfloat16),
        pltpu.VMEM((S, Q_ROWS), jnp.float32),
        pltpu.VMEM((2, S, 2 * Q_ROWS), jnp.float32),
        pltpu.VMEM((2, S, 2 * Q_ROWS), jnp.bfloat16),
    ]


def attend_blocks(
    q_ref, k_ref, v_ref, o_ref, lse_ref, code_ref, low_ref, high_ref, q_turned, v_turned, bias, scores,
    probs, tick=None,
):
    turn(q_turned, q_ref)
    turn(v_turned, v_ref)

    def attend_block(block):
        rows = pl.ds(pl.multiple_of(block * Q_ROWS, Q_ROWS), Q_ROWS)
        bias[...] = mask_bias(code_ref[...], low_ref[:, rows], high_ref[:, rows])
        tops = {}

        def score(pair):
            lanes = slice(pair * LANES, (pair + 1) * LANES)
            raw = dot(k_ref[:, lanes], stack_turned(q_turned[lanes, rows]), NN)
            raw = raw + twice(bias[...])
            scores[pair % 2] = raw
            tops[pair] = jnp.max(raw, axis=0, keepdims=True)

        def mix(pair):
            lanes = slice(pair * LANES, (pair + 1) * LANES)
            expo = jnp.exp(scores[pair % 2] - tops[pair])
            probs[pair % 2] = expo.astype(jnp.bfloat16)
            total = jnp.sum(expo, axis=0, keepdims=True)
            mixed = dot(v_turned[lanes, :], probs[pair % 2], NN)
            out = pick_heads(mixed) / spread_heads(total)
            o_ref[rows, lanes] = jnp.transpose(out).astype(jnp.bfloat16)
            lse = tops[pair] + jnp.log(total)
            lse_ref[pl.ds(2 * pair, 1), rows] = lse[:, :Q_ROWS]
            lse_ref[pl.ds(2 * pair + 1, 1), rows] = lse[:, Q_ROWS:]

        score(0)
        for pair in range(PAIRS):
            if pair + 1 < PAIRS:
                score(pair + 1)
            mix(pair)

    for_blocks(attend_block, tick)


def attend_back_kernel(
    q_ref, k_ref, v_ref, o_ref, g_ref, lse_ref, cos_ref, sin_ref, code_ref, low_ref, high_ref,
    x_hbm, branch_hbm, w_hbm, given_ref, *rest,
):
    own = pl.program_id(0)
    attend_back_body(
        q_ref, k_ref, v_ref, o_ref, g_ref, lse_ref, cos_ref, sin_ref, code_ref, low_ref, high_ref,
        x_hbm.at[own], branch_hbm.at[own], w_hbm, given_ref, *rest,
    )


def attend_back_scratch():
    return [
        pltpu.VMEM((S, 3 * D), jnp.bfloat16),
        pltpu.VMEM((S, D), jnp.float32),
        pltpu.VMEM((S, D), jnp.float32),
        pltpu.VMEM((D, S), jnp.bfloat16),
        pltpu.VMEM((D, S), jnp.bfloat16),
        pltpu.VMEM((D, S), jnp.bfloat16),
        pltpu.VMEM((S, Q_ROWS), jnp.float32),
        pltpu.VMEM((2, S, 2 * Q_ROWS), jnp.bfloat16),
        pltpu.VMEM((2, S, 2 * Q_ROWS), jnp.bfloat16),
        pltpu.VMEM((S, D), jnp.bfloat16),
        pltpu.VMEM((S, D), jnp.bfloat16),
        pltpu.VMEM((D, 2 * PACKED), jnp.bfloat16),
        pltpu.VMEM((8, 3 * D), jnp.float32),
        pltpu.VMEM((LANES, D), jnp.float32),
        pltpu.SemaphoreType.DMA((3,)),
    ]


def attend_back_body(
    q_ref, k_ref, v_ref, o_ref, g_ref, lse_ref, cos_ref, sin_ref, code_ref, low_ref, high_ref,
    x_hbm, branch_hbm, w_hbm, given_ref, token_ref, weight_ref,
    joint_ref, keys_acc, values_acc, q_turned, k_turned, g_turned, bias, probs, score_grads,
    x_ref, branch_ref, w_ref, sums, vectors, sem, tick=None, after=None,
):
    loads = [
        pltpu.make_async_copy(source, target, sem.at[i])
        for i, (source, target) in enumerate(
            ((x_hbm, x_ref), (branch_hbm, branch_ref), (w_hbm, w_ref))
        )
    ]
    for load in loads:
        load.start()
    sums[...] = jnp.zeros_like(sums)
    keys_acc[...] = jnp.zeros_like(keys_acc)
    values_acc[...] = jnp.zeros_like(values_acc)
    turn(q_turned, q_ref)
    turn(k_turned, k_ref)
    turn(g_turned, g_ref)

    def keep(rows, lanes, grad):
        low = grad.astype(jnp.bfloat16)
        joint_ref[rows, lanes] = low
        sums[:, lanes] += jnp.sum(low.astype(jnp.float32).reshape(Q_ROWS // 8, 8, LANES), axis=0)

    def back_block(block):
        rows = pl.ds(pl.multiple_of(block * Q_ROWS, Q_ROWS), Q_ROWS)
        bias[...] = mask_bias(code_ref[...], low_ref[:, rows], high_ref[:, rows])
        cosine = cos_ref[rows, :]
        sine = sin_ref[rows, :]

        def slopes(pair):
            lanes = slice(pair * LANES, (pair + 1) * LANES)
            both = g_turned[lanes, rows].astype(jnp.float32) * jnp.transpose(
                o_ref[rows, lanes].astype(jnp.float32)
            )
            delta = jnp.concatenate(
                [
                    jnp.sum(both[:HEAD_DIM], axis=0, keepdims=True),
                    jnp.sum(both[HEAD_DIM:], axis=0, keepdims=True),
                ],
                axis=1,
            )
            level = jnp.concatenate(
                [lse_ref[pl.ds(2 * pair, 1), rows], lse_ref[pl.ds(2 * pair + 1, 1), rows]], axis=1
            )
            raw = dot(k_ref[:, lanes], stack_turned(q_turned[lanes, rows]), NN)
            prob = jnp.exp(raw + twice(bias[...]) - level)
            prob_grad = dot(v_ref[:, lanes], stack_turned(g_turned[lanes, rows]), NN)
            probs[pair % 2] = prob.astype(jnp.bfloat16)
            score_grads[pair % 2] = (prob * (prob_grad - delta)).astype(jnp.bfloat16)

        def gather(pair):
            lanes = slice(pair * LANES, (pair + 1) * LANES)
            values_acc[:, lanes] += dot(probs[pair % 2], stack_heads(g_ref[rows, lanes]), NN)
            keys_acc[:, lanes] += dot(
                score_grads[pair % 2], stack_heads(q_ref[rows, lanes]), NN
            )
            query = pick_heads(dot(k_turned[lanes, :], score_grads[pair % 2], NN))
            query = jnp.transpose(query) * (HEAD_DIM**-0.5)
            keep(rows, lanes, query * cosine - swap_pairs(query) * sine)

        slopes(0)
        for pair in range(PAIRS):
            if pair + 1 < PAIRS:
                slopes(pair + 1)
            gather(pair)

    for_blocks(back_block, tick)
    if after is not None:
        after()

    @pl.loop(0, S // Q_ROWS)
    def _(block):
        rows = pl.ds(pl.multiple_of(block * Q_ROWS, Q_ROWS), Q_ROWS)
        cosine = cos_ref[rows, :]
        sine = sin_ref[rows, :]
        for pair in range(PAIRS):
            lanes = slice(pair * LANES, (pair + 1) * LANES)
            key = keys_acc[rows, lanes]
            keep(
                rows,
                slice(D + pair * LANES, D + (pair + 1) * LANES),
                key * cosine - swap_pairs(key) * sine,
            )
            keep(
                rows,
                slice(2 * D + pair * LANES, 2 * D + (pair + 1) * LANES),
                values_acc[rows, lanes],
            )

    for load in loads:
        load.wait()
    turn(q_turned, x_ref)
    vectors[...] = jnp.zeros_like(vectors)
    vectors[: given_ref.shape[0], :] = given_ref[...]
    for part in range(3):
        columns = slice(part * D, (part + 1) * D)
        vectors[pl.ds(part, 1), :] = jnp.sum(sums[:, columns], axis=0, keepdims=True)

    def thirds(index):
        first = index % 2 * PACKED + index // 2 * HALF
        return (
            pl.ds(pl.multiple_of(index * HALF, LANES), HALF),
            pl.ds(pl.multiple_of(first, LANES), HALF),
        )

    keys_acc[...] = branch_ref[...].astype(jnp.float32)

    @pl.loop(0, 6)
    def _(index):
        plain, spread = thirds(index)
        grad = joint_ref[:, plain]
        weight_ref[:, spread] = dot(q_turned[...], grad, NN).astype(jnp.bfloat16)
        keys_acc[...] += dot(grad, w_ref[:, spread], NT)

    token_ref[...] = keys_acc[...].astype(jnp.bfloat16)
    turned = jnp.transpose(vectors[...]).astype(jnp.bfloat16)
    for half in range(2):
        weight_ref[:, half * PACKED + 3 * HALF : (half + 1) * PACKED] = turned


def whole(*shape):
    return pl.BlockSpec(shape, lambda i, *_: (0,) * len(shape))


def per(*shape):
    return pl.BlockSpec((None,) + shape, lambda i, *_: (i,) + (0,) * len(shape))


def attend(x, weight, bias, cosine, sine, code, low, high):
    own = x.shape[0]
    act = jax.ShapeDtypeStruct((own, S, D), jnp.bfloat16)
    return pl.pallas_call(
        attend_kernel,
        grid=(own,),
        in_specs=[
            per(S, D), whole(D, 2 * PACKED), whole(16, D), whole(S, LANES), whole(S, LANES),
            per(S, 1), per(1, S), per(1, S),
        ],
        out_specs=[per(S, D), per(S, D), per(S, D), per(S, D), per(HEADS, S)],
        scratch_shapes=attend_scratch(),
        out_shape=[act, act, act, act, jax.ShapeDtypeStruct((own, HEADS, S), jnp.float32)],
        compiler_params=pltpu.CompilerParams(vmem_limit_bytes=60 << 20),
        name="attend",
        cost_estimate=pl.CostEstimate(flops=6 * 10**9, bytes_accessed=12 << 20, transcendentals=6 << 20),
    )(x, weight, bias, cosine, sine, code, low, high)


def attend_back(q, k, v, o, g, lse, cosine, sine, code, low, high, x, branch_grad, weight, given):
    own = q.shape[0]
    hbm = pl.BlockSpec(memory_space=pl.ANY)
    return pl.pallas_call(
        attend_back_kernel,
        grid=(own,),
        in_specs=[
            per(S, D), per(S, D), per(S, D), per(S, D), per(S, D), per(HEADS, S),
            whole(S, LANES), whole(S, LANES), per(S, 1), per(1, S), per(1, S), hbm, hbm, hbm,
            per(16, D),
        ],
        out_specs=[per(S, D), per(D, 2 * PACKED)],
        scratch_shapes=attend_back_scratch(),
        out_shape=[
            jax.ShapeDtypeStruct((own, S, D), jnp.bfloat16),
            jax.ShapeDtypeStruct((own, D, 2 * PACKED), jnp.bfloat16),
        ],
        compiler_params=pltpu.CompilerParams(vmem_limit_bytes=60 << 20),
        name="attend_back",
        cost_estimate=pl.CostEstimate(flops=19 * 10**9, bytes_accessed=24 << 20, transcendentals=6 << 20),
    )(q, k, v, o, g, lse, cosine, sine, code, low, high, x, branch_grad, weight, given)


def mask_tables(segments, padding):
    code = 2 * segments + padding
    low = code
    high = 2 * segments + 1
    return code[:, :, None], low[:, None, :], high[:, None, :]


def angles():
    position = jnp.arange(S, dtype=jnp.int32).astype(jnp.float32)
    column = jnp.arange(LANES, dtype=jnp.int32) % HEAD_DIM // 2
    rate = jnp.exp(column.astype(jnp.float32) * (-2.0 * math.log(10000.0) / HEAD_DIM))
    phase = position[:, None] * rate[None, :]
    return jnp.cos(phase), jnp.sin(phase)


MESH = pl.DeviceIdType.MESH
ROWS = ("shard", "ctx")
EVERY = ("shard", "ctx", "tp")
SEQ = ("ctx", "tp")

BULK = ("upper", "down")
ITEMS = ("project",) + BULK
ROUTES = {"project": "zyx", "upper": "xyz", "down": "zxy"}
BEFORE = (('upper', None, 0), ('project', 1, None), ('project', 2, None), ('down', 1, None), ('project', 3, None), ('upper', None, 1), ('project', 4, None), ('down', 2, None), ('project', 5, None))
DURING = ((1, 'upper', None, 2), (3, 'down', 3, None), (6, 'down', 4, None))
AFTER = (('down', 5, None), ('upper', None, 3))
SUM_ROUTES = {"project": "xyz", "upper": "zyx", "down": "zxy"}


def places(depth):
    steps = [0]
    for k in range(1, depth):
        steps += [k, -k]
    return [(k, dy, dx) for k in steps for dy in (0, 1) for dx in (0, 1)]


def hops(place):
    return abs(place[0]) + place[1] + place[2]


def links(route, place, depth):
    apart = {"z": place[0] != 0, "y": place[1], "x": place[2]}
    level = max([i for i, axis in enumerate(route) if apart[axis]], default=-1)
    sign = (place[0] > 0) - (place[0] < 0)
    onward = []
    if level >= 0 and route[level] == "z" and abs(place[0]) + 1 < depth:
        onward.append(("z", -sign))
    for axis in route[level + 1 :]:
        onward += [("z", 1), ("z", -1)] if axis == "z" else [(axis, 1)]
    back = None if level < 0 else (route[level], sign if route[level] == "z" else 1)
    return back, onward


def seen_from(place, link):
    k, dy, dx = place
    axis, way = link
    return {"z": (k - way, dy, dx), "y": (k, 1 - dy, dx), "x": (k, dy, 1 - dx)}[axis]


class Here:
    def __init__(self):
        self.depth = lax.axis_size("shard")
        self.z = lax.axis_index("shard")
        self.c = lax.axis_index("ctx")
        self.t = lax.axis_index("tp")
        self.y = self.c // 2
        self.x = self.c % 2
        self.sides = lax.axis_size("tp")
        self.members = lax.axis_size("ctx") * self.sides
        self.rank = self.c * self.sides + self.t

    def rank_of(self, offset):
        return (self.rank + offset) % self.members

    def member(self, offset):
        rank = self.rank_of(offset)
        return (self.z, rank // self.sides, rank % self.sides)

    def device(self, link):
        axis, way = link
        if axis == "z":
            return (self.z + way, self.c, self.t)
        if axis == "y":
            return (self.z, 2 * (1 - self.y) + self.x, self.t)
        if axis == "x":
            return (self.z, 2 * self.y + (1 - self.x), self.t)
        return (self.z, self.c, 1 - self.t)

    def piece(self, place):
        k, dy, dx = place
        y = 1 - self.y if dy else self.y
        x = 1 - self.x if dx else self.x
        return (self.z + k) * 4 + 2 * y + x

    def inside(self, way):
        if way == 0:
            return None
        return self.z + way < self.depth if way > 0 else self.z + way >= 0

    def meet(self):
        barrier = pltpu.get_barrier_semaphore()
        for offset in range(1, self.members):
            pl.semaphore_signal(
                barrier, inc=1, device_id=self.member(offset), device_id_type=MESH
            )
        for way in (1, -1):

            @pl.when(self.inside(way))
            def _():
                pl.semaphore_signal(
                    barrier, inc=1, device_id=self.device(("z", way)), device_id_type=MESH
                )

        above = (self.z < self.depth - 1).astype(jnp.int32)
        below = (self.z > 0).astype(jnp.int32)
        pl.semaphore_wait(barrier, self.members - 1 + above + below)


class Exchange:
    def __init__(self, here, source, target, send_sem, recv_sem, own_sem):
        self.here, self.source, self.target = here, source, target
        self.send_sem, self.recv_sem, self.own_sem = send_sem, recv_sem, own_sem

    def block(self, ref, index):
        return ref.at[index] if len(ref.shape) == 3 else ref.at[rows_of(index)]

    def copy(self, offset):
        here = self.here
        return pltpu.make_async_remote_copy(
            src_ref=self.block(self.source, here.rank_of(offset)),
            dst_ref=self.block(self.target, here.rank),
            send_sem=self.send_sem.at[offset],
            recv_sem=self.recv_sem.at[offset],
            device_id=here.member(offset),
            device_id_type=MESH,
        )

    def arrival(self, offset):
        here = self.here
        landed = self.block(self.target, here.rank_of(here.members - offset))
        return pltpu.make_async_remote_copy(
            src_ref=landed,
            dst_ref=landed,
            send_sem=self.send_sem.at[offset],
            recv_sem=self.recv_sem.at[offset],
            device_id=here.member(offset),
            device_id_type=MESH,
        )

    def own(self):
        rank = self.here.rank
        return pltpu.make_async_copy(
            self.block(self.source, rank), self.block(self.target, rank), self.own_sem
        )

    def start(self):
        for offset in range(1, self.here.members):
            self.copy(offset).start()
        self.own().start()

    def receive(self):
        for offset in range(1, self.here.members):
            self.arrival(offset).wait_recv()
        self.own().wait()

    def drain(self):
        for offset in range(1, self.here.members):
            self.copy(offset).wait_send()


def rows_of(index):
    return pl.ds(pl.multiple_of(index * Q_ROWS, Q_ROWS), Q_ROWS)


def exchange_scratch(members):
    return [
        pltpu.SemaphoreType.DMA((members,)),
        pltpu.SemaphoreType.DMA((members,)),
        pltpu.SemaphoreType.DMA,
    ]


def guarded(condition, action):
    if condition is None:
        action()
    else:
        pl.when(condition)(action)


def columns(half, width):
    return pl.ds(pl.multiple_of(half * width, LANES), width)


def block_of(name, refs, piece, half, widths):
    return refs[name].at[piece, :, columns(half, widths[name])]


def gather_attend_kernel(
    widths, chip_count, project_hbm, upper_hbm, down_hbm, tokens_hbm,
    cos_ref, sin_ref, code_ref, low_ref, high_ref,
    q_ref, k_ref, v_ref, o_ref, lse_ref, wide_ref, project_out, x_out, upper_out, down_out,
    x_ref, w_ref, q_turned, v_turned, bias, scores, probs,
    send_sem, recv_sem, side_send, side_recv, own_sem, keep_sem, *exchange_sems,
):
    shards = dict(zip(ITEMS, (project_hbm, upper_hbm, down_hbm)))
    wholes = dict(zip(ITEMS, (w_ref, upper_out, down_out)))
    here = Here()
    tokens = Exchange(here, tokens_hbm, x_ref, *exchange_sems)
    spots = places(chip_count)
    order = sorted(spots, key=hops)
    home = (0, 0, 0)
    slot = {}
    for name in ITEMS:
        for place in spots:
            for link in links(ROUTES[name], place, chip_count)[1]:
                slot[name, place, link] = len(slot)

    def block(name, place, half):
        return block_of(name, wholes, here.piece(place), half, widths)

    def source(name, place, half):
        return shards[name] if place == home else block(name, place, half)

    def send(name, place, link):
        return pltpu.make_async_remote_copy(
            src_ref=source(name, place, here.t),
            dst_ref=block(name, place, here.t),
            send_sem=send_sem.at[slot[name, place, link]],
            recv_sem=recv_sem.at[ITEMS.index(name), spots.index(seen_from(place, link))],
            device_id=here.device(link),
            device_id_type=MESH,
        )

    def side(name, place, half):
        return pltpu.make_async_remote_copy(
            src_ref=source(name, place, half) if half is here.t else block(name, place, half),
            dst_ref=block(name, place, half),
            send_sem=side_send.at[ITEMS.index(name), spots.index(place)],
            recv_sem=side_recv.at[ITEMS.index(name), spots.index(place)],
            device_id=here.device(("tp", 1)),
            device_id_type=MESH,
        )

    def arrival(name, place):
        return pltpu.make_async_remote_copy(
            src_ref=block(name, place, here.t),
            dst_ref=block(name, place, here.t),
            send_sem=send_sem.at[0],
            recv_sem=recv_sem.at[ITEMS.index(name), spots.index(place)],
            device_id=here.device(("tp", 1)),
            device_id_type=MESH,
        )

    def own(name):
        return pltpu.make_async_copy(
            shards[name], block(name, home, here.t), own_sem.at[ITEMS.index(name)]
        )

    def relay(names, place):
        def pass_on():
            for name in names:
                if place != home:
                    arrival(name, place).wait_recv()
                for link in links(ROUTES[name], place, chip_count)[1]:
                    guarded(
                        here.inside(link[1]) if link[0] == "z" else None,
                        lambda name=name, link=link: send(name, place, link).start(),
                    )
                side(name, place, here.t).start()

        guarded(here.inside(place[0]), pass_on)

    def beside(names):
        for place in order:

            def wait(place=place):
                for name in names:
                    side(name, place, 1 - here.t).wait_recv()

            guarded(here.inside(place[0]), wait)

    def wave(name, far, near):
        for place in order[1:]:
            if (hops(place) == far if far is not None else abs(place[0]) == near):
                relay((name,), place)

    early = ITEMS[:1]
    here.meet()
    relay(ITEMS, home)
    tokens.start()
    for name in ITEMS:
        own(name).start()
    for stage in BEFORE:
        wave(*stage)
    own("project").wait()
    tokens.receive()
    beside(early)
    vectors = w_ref[:, :, 3 * HALF : PACKED].reshape(D, LANES).astype(jnp.float32)
    wide_ref[...] = jnp.transpose(vectors)[: wide_ref.shape[0]]
    keep = [
        pltpu.make_async_copy(w_ref, project_out, keep_sem.at[0]),
        pltpu.make_async_copy(x_ref, x_out, keep_sem.at[1]),
    ]
    for copy in keep:
        copy.start()
    project_rows(x_ref, w_ref, wide_ref, cos_ref, sin_ref, q_ref, k_ref, v_ref)

    def tick(step):
        for when, *stage in DURING:
            pl.when(step == when)(functools.partial(wave, *stage))

    attend_blocks(
        q_ref, k_ref, v_ref, o_ref, lse_ref, code_ref, low_ref, high_ref, q_turned, v_turned, bias,
        scores, probs, tick,
    )
    for stage in AFTER:
        wave(*stage)
    beside(BULK)
    for name in BULK:
        own(name).wait()
    tokens.drain()
    for copy in keep:
        copy.wait()
    for place in order:

        def finish(place=place):
            for name in ITEMS:
                side(name, place, here.t).wait_send()
                for link in links(ROUTES[name], place, chip_count)[1]:
                    guarded(
                        here.inside(link[1]) if link[0] == "z" else None,
                        lambda name=name, link=link: send(name, place, link).wait_send(),
                    )

        guarded(here.inside(place[0]), finish)


def link_count(depth):
    return sum(len(links(ROUTES[name], place, depth)[1]) for name in ITEMS for place in places(depth))


def gather_attend(shards, tokens, cosine, sine, code, low, high):
    chips, pieces = lax.axis_size("shard"), lax.axis_size("shard") * lax.axis_size("ctx")
    members = tokens.shape[0]
    widths = {name: shards[name].shape[-1] for name in ITEMS}
    depth = shards["upper"].shape[0]
    spots = len(places(chips))
    vmem, hbm = pl.BlockSpec(memory_space=pltpu.VMEM), pl.BlockSpec(memory_space=pl.ANY)

    def act(*shape):
        return jax.ShapeDtypeStruct(shape, jnp.bfloat16)

    def gathered(name):
        return act(pieces, depth, 2 * widths[name])

    per_place = pltpu.SemaphoreType.DMA((len(ITEMS), spots))
    outs = pl.pallas_call(
        functools.partial(gather_attend_kernel, widths, chips),
        out_shape=[
            act(S, D), act(S, D), act(S, D), act(S, D), jax.ShapeDtypeStruct((HEADS, S), jnp.float32),
            jax.ShapeDtypeStruct((16, D), jnp.float32), gathered("project"), act(S, D),
            gathered("upper"), gathered("down"),
        ],
        in_specs=[hbm] * 4 + [vmem] * 5,
        out_specs=[vmem] * 6 + [hbm] * 4,
        scratch_shapes=[
            pltpu.VMEM((S, D), jnp.bfloat16),
            pltpu.VMEM((pieces, depth, 2 * widths["project"]), jnp.bfloat16),
        ]
        + attend_scratch()
        + [
            pltpu.SemaphoreType.DMA((link_count(chips),)),
            per_place,
            per_place,
            per_place,
            pltpu.SemaphoreType.DMA((len(ITEMS),)),
            pltpu.SemaphoreType.DMA((2,)),
        ]
        + exchange_scratch(members),
        compiler_params=pltpu.CompilerParams(
            collective_id=0, has_side_effects=True, vmem_limit_bytes=60 << 20
        ),
        name="gather_attend",
    )(*[shards[name] for name in ITEMS], tokens, cosine, sine, code, low, high)
    query, key, value, attended, level, wide, project, x, upper, down = outs
    return query, key, value, attended, level, wide, x, dict(project=project, upper=upper, down=down)


def add_into(target, addend):
    height = 16

    @pl.loop(0, target.shape[0] // height)
    def _(step):
        rows = pl.ds(pl.multiple_of(step * height, height), height)
        total = target[rows, :].astype(jnp.float32) + addend[rows, :].astype(jnp.float32)
        target[rows, :] = total.astype(target.dtype)


class Sums:
    def __init__(self, here, names, routes, chip_count, widths, grads, mine, theirs, inbox, sems):
        self.here, self.names, self.routes, self.chip_count = here, names, routes, chip_count
        self.widths, self.grads, self.mine, self.theirs, self.inbox = widths, grads, mine, theirs, inbox
        self.load_sem, self.side_send, self.side_recv, self.send_sem, self.recv_sem = sems
        self.spots = places(chip_count)
        self.order = sorted(self.spots, key=hops, reverse=True)
        self.slot, self.box = {}, {}
        for name in names:
            local = 0
            for place in self.spots:
                for link in links(routes[name], place, chip_count)[1]:
                    self.slot[name, place, link] = len(self.slot)
                    self.box[name, place, link] = local
                    local += 1

    def at(self, name, place):
        return self.names.index(name), self.spots.index(place)

    def total(self, name, place):
        return self.mine[name].at[self.here.piece(place)]

    def other(self, name, place):
        return self.theirs[name].at[self.here.piece(place)]

    def load(self, name, place):
        source = block_of(name, self.grads, self.here.piece(place), self.here.t, self.widths)
        return pltpu.make_async_copy(
            source, self.total(name, place), self.load_sem.at[self.at(name, place)]
        )

    def side(self, name, place):
        here = self.here
        return pltpu.make_async_remote_copy(
            src_ref=block_of(name, self.grads, here.piece(place), 1 - here.t, self.widths),
            dst_ref=self.other(name, place),
            send_sem=self.side_send.at[self.at(name, place)],
            recv_sem=self.side_recv.at[self.at(name, place)],
            device_id=here.device(("tp", 1)),
            device_id_type=MESH,
        )

    def send(self, name, place, link):
        there = seen_from(place, link)
        back = (link[0], -link[1]) if link[0] == "z" else link
        return pltpu.make_async_remote_copy(
            src_ref=self.total(name, place),
            dst_ref=self.inbox[name].at[self.box[name, there, back]],
            send_sem=self.send_sem.at[self.at(name, place)],
            recv_sem=self.recv_sem.at[self.slot[name, there, back]],
            device_id=self.here.device(link),
            device_id_type=MESH,
        )

    def arrival(self, name, place, link):
        landed = self.inbox[name].at[self.box[name, place, link]]
        return pltpu.make_async_remote_copy(
            src_ref=landed,
            dst_ref=landed,
            send_sem=self.send_sem.at[0, 0],
            recv_sem=self.recv_sem.at[self.slot[name, place, link]],
            device_id=self.here.device(link),
            device_id_type=MESH,
        )

    def start(self):
        for place in self.order:

            def begin(place=place):
                for name in self.names:
                    self.side(name, place).start()
                    self.load(name, place).start()

            guarded(self.here.inside(place[0]), begin)

    def settle(self, distance):
        for place in self.order:
            if hops(place) != distance:
                continue

            def work(place=place):
                for name in self.names:
                    back, onward = links(self.routes[name], place, self.chip_count)
                    total = self.total(name, place)
                    self.load(name, place).wait()
                    self.side(name, place).wait_recv()
                    add_into(total, self.other(name, place))
                    for link in onward:

                        def take(link=link):
                            self.arrival(name, place, link).wait_recv()
                            add_into(total, self.inbox[name].at[self.box[name, place, link]])

                        guarded(self.here.inside(link[1]) if link[0] == "z" else None, take)
                    if back is not None:
                        self.send(name, place, back).start()

            guarded(self.here.inside(place[0]), work)

    def result(self, name):
        return self.total(name, (0, 0, 0))[...].astype(jnp.float32)

    def drain(self):
        for place in self.order:

            def finish(place=place):
                for name in self.names:
                    back, _ = links(self.routes[name], place, self.chip_count)
                    self.side(name, place).wait_send()
                    if back is not None:
                        self.send(name, place, back).wait_send()

            guarded(self.here.inside(place[0]), finish)


def sums_scratch(names, routes, chips, pieces, blocks, kinds):
    spots = places(chips)
    boxes = [sum(len(links(routes[name], place, chips)[1]) for place in spots) for name in names]
    per_place = pltpu.SemaphoreType.DMA((len(names), len(spots)))
    return (
        [pltpu.VMEM((pieces,) + block, kind) for block, kind in zip(blocks, kinds)] * 2
        + [pltpu.VMEM((box,) + block, kind) for box, block, kind in zip(boxes, blocks, kinds)]
        + [per_place] * 4
        + [pltpu.SemaphoreType.DMA((sum(boxes),))]
    )


def sums_of(here, names, routes, chip_count, widths, grads, refs):
    count = len(names)
    groups = [dict(zip(names, refs[i * count : (i + 1) * count])) for i in range(3)]
    return Sums(here, names, routes, chip_count, widths, grads, *groups, refs[3 * count :])


def back_scatter_kernel(
    widths, chip_count, *refs,
):
    body, bulk, outs = refs[:15], refs[15:17], refs[17:21]
    scratch = len(attend_back_scratch())
    local, rest = refs[21 : 21 + scratch], refs[21 + scratch :]
    here = Here()
    grads = dict(zip(BULK, bulk))
    sums = sums_of(here, BULK, SUM_ROUTES, chip_count, widths, grads, rest)
    here.meet()
    sums.start()
    farthest = max(hops(place) for place in sums.spots)
    steps = (1, 2, 3, 5, 7)

    def tick(step):
        for i, when in enumerate(steps):
            pl.when(step == when)(functools.partial(sums.settle, farthest - i))

    def after():
        for distance in range(farthest - len(steps), 0, -1):
            sums.settle(distance)

    attend_back_body(*body, *outs[:2], *local, tick=tick, after=after)
    sums.settle(0)
    for name, out in zip(BULK, outs[2:]):
        out[...] = sums.result(name)
    sums.drain()


def back_scatter(q, k, v, o, g, lse, cosine, sine, code, low, high, x, branch_grad, weight, given, grads):
    chips, pieces = lax.axis_size("shard"), lax.axis_size("shard") * lax.axis_size("ctx")
    vmem, hbm = pl.BlockSpec(memory_space=pltpu.VMEM), pl.BlockSpec(memory_space=pl.ANY)
    blocks = [(grads[name].shape[1], grads[name].shape[2] // 2) for name in BULK]
    widths = {name: block[-1] for name, block in zip(BULK, blocks)}
    outs = pl.pallas_call(
        functools.partial(back_scatter_kernel, widths, chips),
        out_shape=[
            jax.ShapeDtypeStruct((S, D), jnp.bfloat16),
            jax.ShapeDtypeStruct((D, 2 * PACKED), jnp.bfloat16),
        ]
        + [jax.ShapeDtypeStruct(block, jnp.float32) for block in blocks],
        in_specs=[vmem] * 11 + [hbm] * 3 + [vmem] + [hbm] * 2,
        out_specs=[vmem] * 4,
        scratch_shapes=attend_back_scratch()
        + sums_scratch(BULK, SUM_ROUTES, chips, pieces, blocks, [jnp.bfloat16] * len(BULK)),
        compiler_params=pltpu.CompilerParams(
            collective_id=3, has_side_effects=True, vmem_limit_bytes=67043328
        ),
        name="back_scatter",
    )(
        q, k, v, o, g, lse, cosine, sine, code, low, high, x, branch_grad, weight, given,
        *[grads[name] for name in BULK],
    )
    return outs[:2], dict(zip(BULK, outs[2:]))


LAST = ("project",)


def scatter_kernel(widths, chip_count, project_hbm, tokens_hbm, project_ref, tokens_out, *rest):
    here = Here()
    sums = sums_of(here, LAST, SUM_ROUTES, chip_count, widths, {"project": project_hbm}, rest[:-3])
    tokens = Exchange(here, tokens_hbm, tokens_out, *rest[-3:])
    here.meet()
    sums.start()
    farthest = max(hops(place) for place in sums.spots)
    for distance in range(farthest, -1, -1):
        sums.settle(distance)
        if distance == farthest - 1:
            tokens.start()
    project_ref[...] = sums.result("project")
    tokens.receive()
    tokens.drain()
    sums.drain()


def scatter_last(project, tokens_grad):
    chips, pieces = lax.axis_size("shard"), lax.axis_size("shard") * lax.axis_size("ctx")
    vmem, hbm = pl.BlockSpec(memory_space=pltpu.VMEM), pl.BlockSpec(memory_space=pl.ANY)
    block = (project.shape[1], project.shape[2] // 2)
    return pl.pallas_call(
        functools.partial(scatter_kernel, {"project": block[-1]}, chips),
        out_shape=[
            jax.ShapeDtypeStruct(block, jnp.float32),
            jax.ShapeDtypeStruct(tokens_grad.shape, tokens_grad.dtype),
        ],
        in_specs=[hbm] * 2,
        out_specs=[vmem, hbm],
        scratch_shapes=sums_scratch(LAST, SUM_ROUTES, chips, pieces, [block], [jnp.bfloat16])
        + exchange_scratch(tokens_grad.shape[0]),
        compiler_params=pltpu.CompilerParams(
            collective_id=1, has_side_effects=True, vmem_limit_bytes=60 << 20
        ),
        name="scatter_last",
    )(project, tokens_grad)


CHUNK = 512
STEP = 16
UNROLL = 4
ATTEND_BIAS, DOWN_BIAS, FIRST_GAIN, FIRST_SHIFT, SECOND_GAIN, SECOND_SHIFT = range(3, 9)
SUMS = 6


def row_mean(values):
    return jnp.sum(values, axis=-1, keepdims=True) * (1.0 / D)


def fold(values):
    return jnp.sum(values.reshape(values.shape[0] // 8, 8, values.shape[1]), axis=0)


def chunk_at(index):
    return pl.ds(pl.multiple_of(index * CHUNK, CHUNK), CHUNK)


def ffn_kernel(
    shared, a_ref, wide_ref, shift_ref, x_hbm, c_hbm, upper_hbm, down_hbm,
    joined_ref, branch_ref, sums_ref, up_sums_ref, out_hbm, upper_grad_hbm, down_grad_hbm,
    x_ref, c_ref, attend_ref, up_ref, down_ref, out_ref, hidden_ref, slope_ref, low_ref, ffn_ref, turned_ref,
    left, right, near, far, first, unit, acc, factor, sums, up_sums, stage, in_sem, out_sem, stage_sem,
    *exchange_sems,
):
    halves = [(half * UPPER, half * RISE, half * HALF) for half in range(2)]
    copies = [
        (upper_hbm.at[:, start + RISE : start + UPPER], attend_ref.at[:, low : low + HALF])
        for start, _, low in halves
    ]
    copies.append((x_hbm, x_ref))
    copies += [
        (upper_hbm.at[:, start : start + RISE], up_ref.at[:, rise : rise + RISE])
        for start, rise, _ in halves
    ]
    copies.append((down_hbm, down_ref))
    if not shared:
        copies.append((c_hbm, c_ref))
    loads = [
        pltpu.make_async_copy(source, target, in_sem.at[i]) for i, (source, target) in enumerate(copies)
    ]
    for load in loads:
        load.start()
    if shared:
        here = Here()
        barrier = pltpu.get_barrier_semaphore()
        for offset in range(1, here.members):
            pl.semaphore_signal(barrier, inc=1, device_id=here.member(offset), device_id_type=MESH)
        arriving = Exchange(here, c_hbm, c_ref, *exchange_sems[:3])
        leaving = Exchange(here, out_ref, out_hbm, *exchange_sems[3:])
    sums[...] = jnp.zeros_like(sums)
    up_sums[...] = jnp.zeros_like(up_sums)
    pairs = FF // CHUNK // 2

    def vector(index):
        return wide_ref[pl.ds(index, 1), :]

    def add_sum(index, values):
        sums[index - ATTEND_BIAS] += fold(values)

    def rows_loop(body):
        @pl.loop(0, S // STEP, unroll=UNROLL)
        def _(step):
            body(pl.ds(pl.multiple_of(step * STEP, STEP), STEP))

    loads[0].wait()
    loads[1].wait()
    acc[...] = dot(a_ref[...], attend_ref[...], NT)
    if shared:
        pl.semaphore_wait(barrier, here.members - 1)
        arriving.start()
    loads[2].wait()

    @rows_loop
    def _(rows):
        joined = x_ref[rows, :].astype(jnp.float32) + acc[rows, :] + vector(ATTEND_BIAS)
        centred = joined - row_mean(joined)
        scale = lax.rsqrt(row_mean(centred * centred) + norm_eps)
        normed = centred * scale
        unit[rows, :] = normed
        factor[rows, :] = scale
        result = normed * vector(FIRST_GAIN) + vector(FIRST_SHIFT)
        first[rows, :] = result
        low_ref[rows, :] = result.astype(jnp.bfloat16)

    for load in loads[3:6]:
        load.wait()

    def expand(target, index):
        target[...] = dot(low_ref[...], up_ref[:, chunk_at(index)], NN)

    def activate(source, target, index):
        pre = source[...] + shift_ref[:, chunk_at(index)]
        cumulative = 0.5 + 0.5 * lax.erf(pre * (1.0 / math.sqrt(2.0)))
        density = jnp.exp(-0.5 * pre * pre) * (1.0 / math.sqrt(2.0 * math.pi))
        hidden = (pre * cumulative).astype(jnp.bfloat16)
        target[...] = hidden
        hidden_ref[:, chunk_at(index)] = hidden
        slope_ref[:, chunk_at(index)] = (cumulative + pre * density).astype(jnp.bfloat16)

    def contract(source, index):
        acc[...] += dot(source[...], down_ref[:, chunk_at(index)], NT)

    def forward(pair):
        expand(right, 2 * pair + 1)
        activate(left, near, 2 * pair)
        expand(left, jnp.minimum(2 * pair + 2, 2 * pairs - 1))
        contract(near, 2 * pair)
        activate(right, far, 2 * pair + 1)
        contract(far, 2 * pair + 1)

    expand(left, 0)
    acc[...] = jnp.zeros_like(acc)

    pl.loop(0, pairs)(forward)
    if shared:
        arriving.receive()
    else:
        loads[6].wait()

    @rows_loop
    def _(rows):
        joined = first[rows, :] + acc[rows, :] + vector(DOWN_BIAS)
        centred = joined - row_mean(joined)
        scale = lax.rsqrt(row_mean(centred * centred) + norm_eps)
        normed = centred * scale
        out_ref[rows, :] = (normed * vector(SECOND_GAIN) + vector(SECOND_SHIFT)).astype(jnp.bfloat16)
        grad = c_ref[rows, :].astype(jnp.float32)
        add_sum(SECOND_GAIN, grad * normed)
        add_sum(SECOND_SHIFT, grad)
        inner = grad * vector(SECOND_GAIN)
        back = scale * (inner - row_mean(inner) - normed * row_mean(inner * normed))
        first[rows, :] = back
        low = back.astype(jnp.bfloat16)
        ffn_ref[rows, :] = low
        add_sum(DOWN_BIAS, low.astype(jnp.float32))

    if not shared:
        store = pltpu.make_async_copy(out_ref, out_hbm, out_sem)
        store.start()

    def stored(slot, target, index, spread):
        first = index * CHUNK + index // pairs * spread
        return pltpu.make_async_copy(
            stage.at[slot],
            target.at[:, pl.ds(pl.multiple_of(first, LANES), CHUNK)],
            stage_sem.at[slot],
        )

    def weight_grad(source, target, spread):
        @pl.loop(0, 2 * pairs)
        def _(index):
            slot = index % 2

            @pl.when(index > 1)
            def _():
                stored(slot, target, index, spread).wait()

            stage[slot] = dot(turned_ref[...], source[:, chunk_at(index)], NN).astype(jnp.bfloat16)
            stored(slot, target, index, spread).start()

        for slot in range(2):
            stored(slot, target, slot, spread).wait()

    turn(turned_ref, ffn_ref)
    if shared:
        leaving.start()
    weight_grad(hidden_ref, down_grad_hbm, 0)

    def widen(target, index):
        target[...] = dot(ffn_ref[...], down_ref[:, chunk_at(index)], NN)

    def reweigh(source, target, index):
        grad = (source[...] * slope_ref[:, chunk_at(index)].astype(jnp.float32)).astype(jnp.bfloat16)
        target[...] = grad
        hidden_ref[:, chunk_at(index)] = grad
        up_sums[:, chunk_at(index)] += fold(grad.astype(jnp.float32))

    def collect(source, index):
        acc[...] += dot(source[...], up_ref[:, chunk_at(index)], NT)

    def backward(pair):
        widen(right, 2 * pair + 1)
        reweigh(left, near, 2 * pair)
        widen(left, jnp.minimum(2 * pair + 2, 2 * pairs - 1))
        collect(near, 2 * pair)
        reweigh(right, far, 2 * pair + 1)
        collect(far, 2 * pair + 1)

    widen(left, 0)
    acc[...] = jnp.zeros_like(acc)

    pl.loop(0, pairs)(backward)

    @rows_loop
    def _(rows):
        grad = first[rows, :] + acc[rows, :]
        normed = unit[rows, :]
        add_sum(FIRST_GAIN, grad * normed)
        add_sum(FIRST_SHIFT, grad)
        inner = grad * vector(FIRST_GAIN)
        back = factor[rows, :] * (inner - row_mean(inner) - normed * row_mean(inner * normed))
        low = back.astype(jnp.bfloat16)
        branch_ref[rows, :] = low
        add_sum(ATTEND_BIAS, low.astype(jnp.float32))

    joined_ref[...] = dot(branch_ref[...], attend_ref[...], NN).astype(jnp.bfloat16)
    turn(turned_ref, low_ref)
    weight_grad(hidden_ref, upper_grad_hbm, HALF)
    turn(turned_ref, branch_ref)

    def attend_stored(slot):
        first = slot * UPPER + RISE
        return pltpu.make_async_copy(
            stage.at[slot, :, :HALF], upper_grad_hbm.at[:, first : first + HALF], stage_sem.at[slot]
        )

    for slot in range(2):
        stage[slot, :, :HALF] = dot(
            turned_ref[...], a_ref[:, slot * HALF : (slot + 1) * HALF], NN
        ).astype(jnp.bfloat16)
        attend_stored(slot).start()
    for index in range(SUMS):
        sums_ref[pl.ds(index, 1), :] = jnp.sum(sums[index], axis=0, keepdims=True)
    up_sums_ref[...] = jnp.sum(up_sums[...], axis=0, keepdims=True)
    for slot in range(2):
        attend_stored(slot).wait()
    if shared:
        leaving.receive()
        arriving.drain()
        leaving.drain()
    else:
        store.wait()


def feed_forward(attended, x, cotangent, upper, down_t, wide, up_shift, shared=False):
    vmem, hbm = pl.BlockSpec(memory_space=pltpu.VMEM), pl.BlockSpec(memory_space=pl.ANY)

    def low(*shape):
        return jax.ShapeDtypeStruct(shape, jnp.bfloat16)

    def full(*shape):
        return jax.ShapeDtypeStruct(shape, jnp.float32)

    def scratch(width, kind=jnp.bfloat16):
        return pltpu.VMEM((S, width), kind)

    return pl.pallas_call(
        functools.partial(ffn_kernel, shared),
        in_specs=[vmem] * 3 + [hbm] * 4,
        out_specs=[vmem] * 4 + [hbm] * 3,
        out_shape=[
            low(S, D), low(S, D), full(SUMS, D), full(1, FF), low(*cotangent.shape),
            low(D, 2 * UPPER), low(D, FF),
        ],
        scratch_shapes=[
            scratch(D), scratch(D), pltpu.VMEM((D, D), jnp.bfloat16), pltpu.VMEM((D, FF), jnp.bfloat16),
            pltpu.VMEM((D, FF), jnp.bfloat16),
            scratch(D), scratch(FF), scratch(FF), scratch(D), scratch(D), pltpu.VMEM((D, S), jnp.bfloat16),
            scratch(CHUNK, jnp.float32), scratch(CHUNK, jnp.float32), scratch(CHUNK), scratch(CHUNK),
            scratch(D, jnp.float32), scratch(D, jnp.float32), scratch(D, jnp.float32),
            scratch(1, jnp.float32),
            pltpu.VMEM((SUMS, 8, D), jnp.float32), pltpu.VMEM((8, FF), jnp.float32),
            pltpu.VMEM((2, D, CHUNK), jnp.bfloat16),
            pltpu.SemaphoreType.DMA((7,)), pltpu.SemaphoreType.DMA, pltpu.SemaphoreType.DMA((2,)),
        ]
        + 2 * (exchange_scratch(cotangent.shape[0]) if shared else []),
        compiler_params=pltpu.CompilerParams(
            vmem_limit_bytes=63 << 20,
            collective_id=2 if shared else None,
            has_side_effects=shared,
        ),
        name="feed_forward",
        cost_estimate=pl.CostEstimate(
            flops=6 * S * D * (D + 2 * FF), bytes_accessed=30 << 20, transcendentals=2 * S * FF
        ),
    )(attended, wide, up_shift.reshape(1, FF), x, cotangent, upper, down_t)


def fitting(shards, own):
    return own == 1 and lax.axis_size("ctx") == 4 and lax.axis_size("tp") == 2 and shards["upper"].shape[0] % 16 == 0


def gather_plain(shards):
    return {
        name: lax.all_gather(
            lax.all_gather(shards[name], ROWS, axis=0), "tp", axis=2, tiled=True
        )
        for name in ITEMS
    }


def scatter_plain(grads):
    shards = {}
    for name in ITEMS:
        part = lax.psum_scatter(grads[name], "tp", scatter_dimension=2, tiled=True)
        part = lax.psum_scatter(part, ROWS, scatter_dimension=0, tiled=False)
        shards[name] = part.astype(jnp.float32)
    return shards


def local(
    tokens, project_weight, attend_weight, up_weight, down_weight, project_bias, attend_bias,
    up_bias, down_bias, first_gain, first_shift, second_gain, second_shift, segment_ids, padding,
    cotangent,
):
    seq_count = tokens.shape[0]
    members = lax.axis_size("ctx") * lax.axis_size("tp")
    own = seq_count // members
    rank = lax.axis_index("ctx") * lax.axis_size("tp") + lax.axis_index("tp")
    pieces = lax.axis_size("shard") * lax.axis_size("ctx")
    depth = D // pieces

    def to_sequences(array):
        parts = array.reshape((members, own) + array.shape[1:])
        parts = lax.all_to_all(parts, SEQ, 0, 0, tiled=True)
        return jnp.swapaxes(parts, 0, 1).reshape(own, S, D)

    def to_blocks(array):
        parts = jnp.swapaxes(array.reshape(own, members, S // members, D), 0, 1)
        return lax.all_to_all(parts, SEQ, 0, 0, tiled=True).reshape(tokens.shape)

    segments = lax.dynamic_slice_in_dim(segment_ids, rank * own, own, 0)
    pads = lax.dynamic_slice_in_dim(padding, rank * own, own, 0)

    vectors = jnp.concatenate(
        [
            project_bias,
            attend_bias[None],
            down_bias[None],
            first_gain[None],
            first_shift[None],
            second_gain[None],
            second_shift[None],
            up_bias.reshape(FF // D, depth),
        ],
        axis=0,
    )
    shards = {
        "project": jnp.concatenate(
            [
                project_weight.reshape(depth, 3 * HALF),
                jnp.pad(jnp.transpose(vectors), ((0, 0), (0, LANES - vectors.shape[0]))),
            ],
            axis=1,
        ),
        "upper": jnp.concatenate([up_weight, jnp.transpose(attend_weight)], axis=1),
        "down": jnp.transpose(down_weight),
    }
    custom = fitting(shards, own)
    tables = mask_tables(segments, pads)
    cosine, sine = angles()
    if custom:
        *saved, wide, x, wholes = gather_attend(
            shards, tokens, cosine, sine, *[table[0] for table in tables]
        )
        query, key, value, attended, level, x = [array[None] for array in saved + [x]]
    else:
        wholes, x = gather_plain(shards), to_sequences(tokens)
    project = wholes["project"].reshape(D, 2 * PACKED)
    upper = wholes["upper"].reshape(D, 2 * UPPER)
    down_t = wholes["down"].reshape(D, FF)
    if not custom:
        wide = jnp.transpose(project[:, 3 * HALF : 3 * HALF + 16]).astype(jnp.float32)
        query, key, value, attended, level = attend(x, project, wide, cosine, sine, *tables)
    up_shift = jnp.swapaxes(wide[9:13].reshape(FF // D, pieces, depth), 0, 1).reshape(FF)
    params = (upper, down_t, wide, up_shift)
    if custom:
        parts = [feed_forward(attended[0], x[0], cotangent, *params, shared=True)]
    else:
        incoming = to_sequences(cotangent)
        parts = [feed_forward(attended[i], x[i], incoming[i], *params) for i in range(own)]
    attended_grad = jnp.stack([part[0] for part in parts])
    branch_grad = jnp.stack([part[1] for part in parts])
    sums = sum(part[2] for part in parts)
    up_bias_grad = sum(part[3] for part in parts)
    output = parts[0][4] if custom else to_blocks(jnp.stack([part[4] for part in parts]))
    upper_grad, down_grad = (
        parts[0][k] if own == 1 else sum(part[k].astype(jnp.float32) for part in parts).astype(jnp.bfloat16)
        for k in (5, 6)
    )
    up_bias_grad = jnp.swapaxes(up_bias_grad.reshape(pieces, FF // D, depth), 0, 1).reshape(FF // D, D)
    given = jnp.concatenate([jnp.zeros((3, D), jnp.float32), sums, up_bias_grad, jnp.zeros((3, D), jnp.float32)])
    grads = {
        "upper": upper_grad.reshape(pieces, depth, 2 * UPPER),
        "down": down_grad.reshape(pieces, depth, FF),
    }
    inputs = (query, key, value, attended, attended_grad, level)
    if custom:
        (tokens_grad, project_grad), shards = back_scatter(
            *[array[0] for array in inputs], cosine, sine, *[table[0] for table in tables], x[0],
            branch_grad[0], project, given, grads,
        )
        shards["project"], tokens_grad = scatter_last(
            project_grad.reshape(pieces, depth, 2 * PACKED), tokens_grad.reshape(tokens.shape)
        )
    else:
        given = jnp.concatenate([given[None], jnp.zeros((own - 1,) + given.shape, jnp.float32)])
        tokens_grad, project_grad = attend_back(
            *inputs, cosine, sine, *tables, x, branch_grad, project, given
        )
        project_grad = jnp.sum(project_grad.astype(jnp.float32), axis=0).astype(jnp.bfloat16)
        grads["project"] = project_grad.reshape(pieces, depth, 2 * PACKED)
        shards, tokens_grad = scatter_plain(grads), to_blocks(tokens_grad)
    sums = jnp.transpose(shards["project"][:, 3 * HALF : 3 * HALF + 13])
    return (
        output,
        tokens_grad,
        shards["project"][:, : 3 * HALF].reshape(depth, 3, HALF),
        jnp.transpose(shards["upper"][:, RISE:]),
        shards["upper"][:, :RISE],
        jnp.transpose(shards["down"]),
        sums[:3],
        sums[3],
        sums[9:].reshape(-1),
        sums[4],
        sums[5],
        sums[6],
        sums[7],
        sums[8],
    )


def solution(mesh):
    in_specs = (
        P("shard", ("ctx", "tp"), None),
        P(("shard", "ctx"), None, "tp"),
        P("tp", ("shard", "ctx")),
        P(("shard", "ctx"), "tp"),
        P("tp", ("shard", "ctx")),
        P(None, ("shard", "ctx")),
        P(("shard", "ctx")),
        P(("shard", "ctx")),
        P(("shard", "ctx")),
        P(("shard", "ctx")),
        P(("shard", "ctx")),
        P(("shard", "ctx")),
        P(("shard", "ctx")),
        P("shard", None),
        P("shard", None),
        P("shard", ("ctx", "tp"), None),
    )
    out_specs = (
        P("shard", ("ctx", "tp"), None),
        P("shard", ("ctx", "tp"), None),
        P(("shard", "ctx"), None, "tp"),
        P("tp", ("shard", "ctx")),
        P(("shard", "ctx"), "tp"),
        P("tp", ("shard", "ctx")),
        P(None, ("shard", "ctx")),
        P(("shard", "ctx")),
        P(("shard", "ctx")),
        P(("shard", "ctx")),
        P(("shard", "ctx")),
        P(("shard", "ctx")),
        P(("shard", "ctx")),
        P(("shard", "ctx")),
    )
    return jax.shard_map(local, mesh=mesh, in_specs=in_specs, out_specs=out_specs, check_vma=False)
```
